32 devices in a mesh: dp: 8 (over y, x, core), tensor: 4 (over z).
Axes of the slice: x: 2, y: 2, z: 4, core: 2. Of those that a mesh axis runs over, the one named last changes fastest.
Arguments:
- x_in: bfloat16 [8, 2048, 1536], P('dp'), may hold values from -6 to 6
- segments: int32 [8, 2048], P('dp'), may hold values from 0 to 4, as said below
- out_grad: bfloat16 [8, 2048, 1536], P('dp'), may hold values from -6 to 6
- norm_gain: float32 [1536], replicated, may hold values from 0.5 to 1.5
- w_z: bfloat16 [1536, 3072], P(None, 'tensor'), may hold values from -0.15625 to 0.15625
- w_x: bfloat16 [1536, 3072], P(None, 'tensor'), may hold values from -0.15625 to 0.15625
- w_bc: bfloat16 [1536, 256], replicated, may hold values from -0.15625 to 0.15625
- w_dt: bfloat16 [1536, 48], P(None, 'tensor'), may hold values from -0.15625 to 0.15625
- conv_x: float32 [4, 3072], P(None, 'tensor'), may hold values from -3 to 3
- conv_bc: float32 [4, 256], replicated, may hold values from -3 to 3
- bias_x: float32 [3072], P('tensor'), may hold values from -3 to 3
- bias_bc: float32 [256], replicated, may hold values from -3 to 3
- dt_bias: float32 [48], P('tensor'), may hold values from -4.5 to -2
- a_log: float32 [48], P('tensor'), may hold values from 0 to 2.77
- d_skip: float32 [48], P('tensor'), may hold values from 0.5 to 1.5
- out_gain: float32 [3072], P('tensor'), may hold values from 0.5 to 1.5
- w_out: bfloat16 [3072, 1536], P('tensor'), may hold values from -0.109375 to 0.109375
Outputs:
- y_out: bfloat16 [8, 2048, 1536], P('dp')
- x_grad: bfloat16 [8, 2048, 1536], P('dp')
- norm_gain_grad: float32 [1536], replicated
- w_z_grad: float32 [1536, 3072], P(None, 'tensor')
- w_x_grad: float32 [1536, 3072], P(None, 'tensor')
- w_bc_grad: float32 [1536, 256], replicated
- w_dt_grad: float32 [1536, 48], P(None, 'tensor')
- conv_x_grad: float32 [4, 3072], P(None, 'tensor')
- conv_bc_grad: float32 [4, 256], replicated
- bias_x_grad: float32 [3072], P('tensor')
- bias_bc_grad: float32 [256], replicated
- dt_bias_grad: float32 [48], P('tensor')
- a_log_grad: float32 [48], P('tensor')
- d_skip_grad: float32 [48], P('tensor')
- out_gain_grad: float32 [3072], P('tensor')
- w_out_grad: float32 [3072, 1536], P('tensor')
The draws below stay inside these ranges and needn't reach their ends.
Inputs may be any that keep to these rules, and one draw needn't show every extreme that they name: `segments`: segment numbers never fall along a sequence and each of the 5 documents of a sequence holds 204 to 1024 neighbouring positions; one document of every sequence holds exactly 1024.
All inputs are finite; a program needn't handle non-finite values.
Results may differ from the reference program's by a relative error of at most 0.0083.
Values may be sent and summed in bfloat16 or wider, within the bound.
A program may use at most 192 MiB of HBM per device.

```python
from functools import partial
import jax
import jax.numpy as jnp
from jax import lax

D = 1536
H = 48
DI = 3072
N = 128
K = 4
GROUP = 256
LEN = 2048
SEQS = 8
DOCS = 5


def one_sequence(key):
    floor_len = LEN // 10
    most_len = LEN // 2
    extra = LEN - most_len - (DOCS - 1) * floor_len
    cut_key, order_key = jax.random.split(key)
    cuts = jnp.sort(jax.random.randint(cut_key, (DOCS - 2,), 0, extra + 1))
    edges = jnp.concatenate([jnp.zeros((1,), jnp.int32), cuts.astype(jnp.int32), jnp.full((1,), extra, jnp.int32)])
    shares = edges[1:] - edges[:-1] + floor_len
    lengths = jnp.concatenate([jnp.full((1,), most_len, jnp.int32), shares])
    order = jax.random.permutation(order_key, DOCS)
    lengths = lengths[order]
    bounds = jnp.cumsum(lengths)[:-1]
    position = jnp.arange(LEN, dtype=jnp.int32)
    return jnp.sum((position[:, None] >= bounds[None, :]).astype(jnp.int32), 1).astype(jnp.int32)


def draw_segments(key, part):
    keys = jax.random.split(jax.random.fold_in(key, 17), SEQS)
    return jax.vmap(one_sequence)(keys)


def level_of(rng, dims, shards, smallest, high):
    level = 1.0
    for dim, shards_of in shards:
        draws = jax.random.uniform(jax.random.fold_in(jax.random.fold_in(rng, 6), dim), (shards_of,), jnp.float32, smallest / len(shards), high / len(shards))
        level = level * jnp.repeat(jnp.exp(draws), dims[dim] // shards_of).reshape((-1,) + (1,) * (len(dims) - 1 - dim))
    return level


def bell_draw(stream_key, extent, scale, limit, pieces=(), kind=jnp.bfloat16):
    entries = jax.random.normal(stream_key, extent, jnp.float32) * scale
    if len(pieces) > 0:
        entries = level_of(stream_key, extent, pieces, -0.22, 0.18) * entries
    return jnp.clip(entries, min=-limit, max=limit).astype(kind)


def setup_inputs(seed: int = 0) -> dict:
    streams_of = jax.random.split(jax.random.key(seed), 18)
    x_in = bell_draw(streams_of[0], (SEQS, LEN, D), 1.0, 6.0, ((0, 8),))
    segments = draw_segments(jax.random.fold_in(streams_of[17], 71), 0)
    out_grad = bell_draw(streams_of[2], (SEQS, LEN, D), 1.0, 6.0, ((0, 8),))
    norm_gain = jnp.clip(1.0 + 0.1 * jax.random.normal(streams_of[3], (D,), jnp.float32), 0.5, 1.5)
    w_z = bell_draw(streams_of[4], (D, DI), D ** -0.5, 0.15625, ((1, 4),))
    w_x = bell_draw(streams_of[5], (D, DI), D ** -0.5, 0.15625, ((1, 4),))
    w_bc = bell_draw(streams_of[6], (D, 2 * N), D ** -0.5, 0.15625)
    w_dt = bell_draw(streams_of[7], (D, H), D ** -0.5, 0.15625, ((1, 4),))
    conv_x = bell_draw(streams_of[8], (K, DI), K ** -0.5, 3.0, ((1, 4),), jnp.float32)
    conv_bc = bell_draw(streams_of[9], (K, 2 * N), K ** -0.5, 3.0, (), jnp.float32)
    bias_x = bell_draw(streams_of[10], (DI,), 0.5, 3.0, ((0, 4),), jnp.float32)
    bias_bc = bell_draw(streams_of[11], (2 * N,), 0.5, 3.0, (), jnp.float32)
    dt_bias = jnp.clip(-4.5 + 2.5 * jax.random.uniform(streams_of[12], (H,), jnp.float32) ** level_of(streams_of[12], (H,), ((0, 4),), -0.2, 0.2), -4.5, -2.0)
    a_log = jnp.clip(2.77 * jax.random.uniform(streams_of[13], (H,), jnp.float32) ** level_of(streams_of[13], (H,), ((0, 4),), -0.2, 0.2), 0.0, 2.77)
    d_skip = jnp.clip(0.5 + 1.0 * jax.random.uniform(streams_of[14], (H,), jnp.float32) ** level_of(streams_of[14], (H,), ((0, 4),), -0.2, 0.2), 0.5, 1.5)
    out_gain = jnp.clip(1.0 + 0.1 * jax.random.normal(streams_of[15], (DI,), jnp.float32), 0.5, 1.5)
    w_out = bell_draw(streams_of[16], (DI, D), DI ** -0.5, 0.109375, ((0, 4),))
    return dict(x_in=x_in, segments=segments, out_grad=out_grad, norm_gain=norm_gain, w_z=w_z, w_x=w_x, w_bc=w_bc, w_dt=w_dt, conv_x=conv_x, conv_bc=conv_bc, bias_x=bias_x, bias_bc=bias_bc, dt_bias=dt_bias, a_log=a_log, d_skip=d_skip, out_gain=out_gain, w_out=w_out)


epsilon = 1e-05

@jax.custom_vjp
def low(v):
    return lax.optimization_barrier(v.astype(jnp.bfloat16)).astype(jnp.float32)

@jax.custom_vjp
def low_back(v):
    return v

def low_keep(v):
    return (low(v), None)

def low_pass(kept, grad):
    return (grad,)

def back_keep(v):
    return (v, None)

def back_low(kept, grad):
    return (low(grad),)
low.defvjp(low_keep, low_pass)
low_back.defvjp(back_keep, back_low)

def matmul_hi(left, right):
    return jnp.dot(left, right, precision=lax.Precision.HIGHEST, preferred_element_type=jnp.float32)

def causal_conv(values, kernel, seg_ids):
    tap_count = kernel.shape[0]
    result = values * kernel[tap_count - 1]
    for offset in range(1, tap_count):
        earlier = jnp.concatenate([jnp.zeros((offset, values.shape[1]), values.dtype), values[:-offset]], 0)
        prior_seg = jnp.concatenate([jnp.full((offset,), -1, jnp.int32), seg_ids[:-offset]], 0)
        same_seg = (prior_seg == seg_ids).astype(values.dtype)
        result = result + earlier * same_seg[:, None] * kernel[tap_count - 1 - offset]
    return result

def group_step(carry, inputs):
    carried, prev_seg = carry
    head_x, step_dt, log_decay, b_rows, c_rows, seg_rows = inputs
    cum_decay = jnp.cumsum(log_decay, axis=0)
    block_len = seg_rows.shape[0]
    position = jnp.arange(block_len)
    visible = (position[:, None] >= position[None, :]) & (seg_rows[:, None] == seg_rows[None, :])
    gap_decay = cum_decay[:, None, :] - cum_decay[None, :, :]
    decay_mat = jnp.exp(jnp.where(visible[:, :, None], gap_decay, 0.0)) * visible[:, :, None].astype(cum_decay.dtype)
    scores = jnp.dot(c_rows, b_rows.T, precision=lax.Precision.HIGHEST)
    mixing = scores[:, :, None] * decay_mat * step_dt[None, :, :]
    inside = jnp.einsum('tsh,shp->thp', mixing, head_x, precision=lax.Precision.HIGHEST)
    keep_prev = (seg_rows == prev_seg).astype(cum_decay.dtype)
    entering = jnp.einsum('tn,hnp->thp', c_rows, carried, precision=lax.Precision.HIGHEST)
    entering = entering * (jnp.exp(cum_decay) * keep_prev[:, None])[:, :, None]
    last_seg = seg_rows[-1]
    to_end = jnp.exp(cum_decay[-1][None, :] - cum_decay) * (seg_rows == last_seg).astype(cum_decay.dtype)[:, None] * step_dt
    carry_scale = jnp.exp(cum_decay[-1]) * (last_seg == prev_seg).astype(cum_decay.dtype)
    updated = carried * carry_scale[:, None, None] + jnp.einsum('sn,sh,shp->hnp', b_rows, to_end, head_x, precision=lax.Precision.HIGHEST)
    return ((updated, last_seg), inside + entering)

def state_scan(head_x, step_dt, log_decay, b_mat, c_mat, seg_ids):
    length, head_count, head_size = head_x.shape
    blocks = length // GROUP

    def to_blocks(array):
        return array.reshape((blocks, GROUP) + array.shape[1:])
    start = (jnp.zeros((head_count, b_mat.shape[1], head_size), head_x.dtype), jnp.int32(-1))
    final_state, outputs = lax.scan(jax.checkpoint(group_step), start, (to_blocks(head_x), to_blocks(step_dt), to_blocks(log_decay), to_blocks(b_mat), to_blocks(c_mat), to_blocks(seg_ids)))
    return outputs.reshape(length, head_count, head_size)

def bc_conv(values, kernel, shift_bc, seg_ids):
    return jax.nn.silu(causal_conv(values, kernel, seg_ids) + shift_bc)

def head_mix(gate_in, inner_in, dt_in, state_in, kernel_x, shift_x, dt_shift, decay_log, skip_gain, seg_ids):
    length = inner_in.shape[0]
    head_count = dt_in.shape[1]
    mixed_x = jax.nn.silu(causal_conv(inner_in, kernel_x, seg_ids) + shift_x)
    head_x = mixed_x.reshape(length, head_count, -1)
    step_dt = jax.nn.softplus(dt_in + dt_shift)
    log_decay = -jnp.exp(decay_log) * step_dt
    state_dim = state_in.shape[1] // 2
    scanned = state_scan(head_x, step_dt, log_decay, state_in[:, :state_dim], state_in[:, state_dim:], seg_ids)
    scanned = scanned + skip_gain[None, :, None] * head_x
    return scanned.reshape(length, -1) * jax.nn.silu(gate_in)

def full_layer(tokens, norm_gain, w_z, w_x, w_bc, w_dt, conv_x, conv_bc, bias_x, bias_bc, dt_bias, a_log, d_skip, out_gain, w_out, seg_ids):
    inv_rms = lax.rsqrt(lax.optimization_barrier(jnp.mean(tokens * tokens, -1, keepdims=True)) + epsilon)
    normal_in = low(tokens * inv_rms * norm_gain)
    proj_z = low_back(matmul_hi(normal_in, w_z))
    proj_x = low_back(matmul_hi(normal_in, w_x))
    proj_bc = low_back(matmul_hi(normal_in, w_bc))
    proj_dt = low_back(matmul_hi(normal_in, w_dt))
    state_in = bc_conv(proj_bc, conv_bc, bias_bc, seg_ids)
    gated = head_mix(proj_z, proj_x, proj_dt, state_in, conv_x, bias_x, dt_bias, a_log, d_skip, seg_ids)
    inv_gate = lax.rsqrt(lax.optimization_barrier(jnp.mean(gated * gated, -1, keepdims=True)) + epsilon)
    normed = low(gated * inv_gate * out_gain)
    return tokens + matmul_hi(normed, w_out)

def reference(x_in, segments, out_grad, norm_gain, w_z, w_x, w_bc, w_dt, conv_x, conv_bc, bias_x, bias_bc, dt_bias, a_log, d_skip, out_gain, w_out):
    params = tuple((item.astype(jnp.float32) for item in (norm_gain, w_z, w_x, w_bc, w_dt, conv_x, conv_bc, bias_x, bias_bc, dt_bias, a_log, d_skip, out_gain, w_out)))
    zero_grads = tuple((jnp.zeros_like(item) for item in params))

    def per_sequence(totals, inputs):
        tokens, seg_ids, cotangent = inputs
        layer_fn = partial(full_layer, seg_ids=seg_ids)
        output, pull_back = jax.vjp(layer_fn, tokens.astype(jnp.float32), *params)
        pulled = pull_back(cotangent.astype(jnp.float32))
        summed = tuple((total + extra for total, extra in zip(totals, pulled[1:])))
        return (summed, (output.astype(jnp.bfloat16), pulled[0].astype(jnp.bfloat16)))
    totals, (outputs, input_grads) = lax.scan(per_sequence, zero_grads, (x_in, segments, out_grad))
    return (outputs, input_grads, totals[0], totals[1], totals[2], totals[3], totals[4], totals[5], totals[6], totals[7], totals[8], totals[9], totals[10], totals[11], totals[12], totals[13])
```

```python
import functools

import jax
import jax.numpy as jnp
from jax import lax
from jax.experimental import pallas as pl
from jax.experimental.pallas import tpu as pltpu
from jax.sharding import PartitionSpec as P

EPS = 1e-05
CHUNK = 128
BLOCK = 256
LANES = 128
F32 = jnp.float32
BF16 = jnp.bfloat16
HIGHEST = lax.Precision.HIGHEST


def dot(a, b, precision=None):
    return lax.dot_general(a, b, (((1,), (0,)), ((), ())), precision=precision, preferred_element_type=F32)


def dot_t(a, b):
    return lax.dot_general(a, b, (((1,), (1,)), ((), ())), preferred_element_type=F32)


def tdot(a, b):
    return lax.dot_general(a, b, (((0,), (0,)), ((), ())), preferred_element_type=F32)


def sigmoid(v):
    return 1.0 / (1.0 + jnp.exp(-v))


def softplus(v):
    e = jnp.exp(-jnp.abs(v))
    series = e * (1.0 - e * (0.5 - e * (1.0 / 3.0 - e * 0.25)))
    return jnp.maximum(v, 0.0) + jnp.where(e < 0.03, series, jnp.log(1.0 + e))


def spread(columns, heads):
    rows = columns.shape[0]
    low = lax.broadcasted_iota(jnp.int32, (rows, LANES), 1) < LANES // 2
    pieces = []
    for pair in range(heads // 2):
        first = columns[:, 2 * pair : 2 * pair + 1]
        second = columns[:, 2 * pair + 1 : 2 * pair + 2]
        pieces.append(jnp.where(low, first, second))
    return jnp.concatenate(pieces, axis=1)


def iotas(rows, cols):
    return (
        lax.broadcasted_iota(jnp.int32, (rows, cols), 0),
        lax.broadcasted_iota(jnp.int32, (rows, cols), 1),
    )


def decays(la, seg_col, seg_row):
    r, c = iotas(CHUNK, CHUNK)
    lower = (r >= c).astype(F32)
    cum = dot(lower, la, HIGHEST)
    visible = (r >= c) & (seg_col == seg_row)
    return cum, cum.T, visible


def decay_matrix(cum, cum_t, visible, head):
    gap = cum[:, head : head + 1] - cum_t[head : head + 1, :]
    return jnp.exp(jnp.where(visible, gap, -1e30))


def split_pair(values):
    low = lax.broadcasted_iota(jnp.int32, values.shape, 1) < LANES // 2
    zero = jnp.zeros_like(values)
    return jnp.where(low, values, zero), jnp.where(low, zero, values)


def conv_taps(hist, weight, meta, rows):
    out = hist[8 : 8 + rows, :] * weight[3:4, :]
    for k in range(1, 4):
        out = out + hist[8 - k : 8 - k + rows, :] * meta[:, k - 1 : k] * weight[3 - k : 4 - k, :]
    return out


MESH = pl.DeviceIdType.MESH


def greet(count):
    me = lax.axis_index("tensor")
    barrier = pltpu.get_barrier_semaphore()
    left, right = me > 0, me < count - 1

    @pl.when(left)
    def _():
        pl.semaphore_signal(barrier, inc=1, device_id={"tensor": me - 1}, device_id_type=MESH)

    @pl.when(right)
    def _():
        pl.semaphore_signal(barrier, inc=1, device_id={"tensor": me + 1}, device_id_type=MESH)

    pl.semaphore_wait(barrier, left.astype(jnp.int32) + right.astype(jnp.int32))


class Line:
    def __init__(self, count, pairs, half, steps, refs, own):
        self.count, self.pairs, self.half, self.steps, self.own = count, pairs, half, steps, own
        (self.res, self.land, self.mine, self.send, self.red_out, self.red_in, self.bc_out, self.bc_in, self.local) = refs

    def slot(self, k):
        return jnp.where(k < self.half, k, 3 * self.half - 1 - k)

    def flow(self, f):
        me = lax.axis_index("tensor")
        if f == 0:
            return me, me - 1, me + 1
        return self.count - 1 - me, me + 1, me - 1

    def red(self, f, ls, toward):
        return pltpu.make_async_remote_copy(
            src_ref=self.send.at[f], dst_ref=self.land.at[ls + 1, f], send_sem=self.red_out.at[f, ls],
            recv_sem=self.red_in.at[f, ls], device_id={"tensor": toward}, device_id_type=MESH,
        )

    def cast(self, f, ls, away, k, src=None):
        there = self.res.at[self.slot(k), f]
        return pltpu.make_async_remote_copy(
            src_ref=there if src is None else src, dst_ref=there, send_sem=self.bc_out.at[f, ls],
            recv_sem=self.bc_in.at[f, ls], device_id={"tensor": away}, device_id_type=MESH,
        )

    def finish(self, f, s, ls):
        z, toward, away = self.flow(f)
        n = self.count
        i = s - (n - 1) + z
        k = s - (n - 1) - z
        i_ok = (i >= 0) & (i < self.pairs)
        k_ok = (k >= 0) & (k < self.pairs)

        @pl.when(i_ok & (z > 0))
        def _():
            self.red(f, ls, toward).wait_send()

        @pl.when(k_ok & (z < n - 1))
        def _():
            self.cast(f, ls, away, k).wait_send()

        @pl.when((i + 1 >= 0) & (i + 1 < self.pairs) & (z < n - 1))
        def _():
            self.red(f, ls, toward).wait_recv()

        @pl.when((k + 1 >= 0) & (k + 1 < self.pairs) & (z > 0))
        def _():
            self.cast(f, ls, away, k + 1).wait_recv()

    def step(self, s, ls):
        n = self.count
        for f in range(2):

            @pl.when(ls > 0)
            def _():
                self.finish(f, s - 1, ls - 1)

            z, toward, away = self.flow(f)
            i = s - (n - 1) + z
            k = s - (n - 1) - z

            @pl.when((i >= 0) & (i < self.pairs))
            def _():
                self.own(self.mine.at[f], f, i, self.local.at[f])

                @pl.when(z == n - 1)
                def _():
                    self.send[f] = self.mine[f]

                @pl.when(z < n - 1)
                def _():
                    total = self.mine[f].astype(F32) + self.land[ls, f].astype(F32)
                    self.send[f] = total.astype(BF16)

                @pl.when(z > 0)
                def _():
                    self.red(f, ls, toward).start()

                @pl.when(z == 0)
                def _():
                    self.cast(f, ls, away, i, self.send.at[f]).start()
                    keep = pltpu.make_async_copy(self.send.at[f], self.res.at[self.slot(i), f], self.local.at[f])
                    keep.start()
                    keep.wait()

            @pl.when((k >= 0) & (k < self.pairs) & (z > 0) & (z < n - 1))
            def _():
                self.cast(f, ls, away, k).start()

    def open(self, carry):
        for f in range(2):
            if carry is not None:
                self.land[0, f] = carry[f]

    def close(self, s, ls, carry):
        for f in range(2):
            self.finish(f, s, ls)
            z, _, _ = self.flow(f)
            i = s + 1 - (self.count - 1) + z
            got = (i >= 0) & (i < self.pairs) & (z < self.count - 1)
            if carry is None:
                continue

            @pl.when(got)
            def _():
                carry[f] = self.land[ls + 1, f]

            @pl.when(jnp.logical_not(got))
            def _():
                carry[f] = jnp.zeros(carry.shape[1:], carry.dtype)


def line_scratch(steps, rows, width):
    return [
        pltpu.VMEM((steps + 1, 2, rows, width), BF16),
        pltpu.VMEM((2, rows, width), BF16),
        pltpu.VMEM((2, rows, width), BF16),
        pltpu.SemaphoreType.DMA((2, steps)),
        pltpu.SemaphoreType.DMA((2, steps)),
        pltpu.SemaphoreType.DMA((2, steps)),
        pltpu.SemaphoreType.DMA((2, steps)),
        pltpu.SemaphoreType.DMA((2,)),
    ]


def bring(src, dst, sem):
    copy = pltpu.make_async_copy(src, dst, sem)
    copy.start()
    copy.wait()


def line_kernel(count, pairs, half, first, steps, y_ref, x_ref, carry_ref, res_in, res_ref, *scratch):
    del res_in

    def own(dst, f, i, sem):
        @pl.when(i < half)
        def _():
            bring(y_ref.at[i, f], dst, sem)

        @pl.when(i >= half)
        def _():
            bring(x_ref.at[2 * half - 1 - i, f], dst, sem)

    line = Line(count, pairs, half, steps, (res_ref, *scratch), own)
    at = pl.program_id(0)

    @pl.when(at == 0)
    def _():
        greet(count)
        line.open(carry_ref)

    line.step(first + at, at)

    @pl.when(at == steps - 1)
    def _():
        line.close(first + at, at, None)


def forward_kernel(
    heads, count, pairs, half, steps, when,
    x_ref, g_ref, seg_ref, meta_ref, wz_ref, wx_ref, wbc_ref, wdt_ref, wo_ref, ng_ref,
    cx_ref, bx_ref, cbc_ref, bbc_ref, dtb_ref, al_ref, dsk_ref, og_ref,
    z_ref, p_ref, xc_ref, ys_ref, pbc_ref, bc_ref, dtr_ref, dn_ref, xn_ref, st_ref, yp_ref, stat_ref,
    carry_out, res_ref, hist, hist_bc, state, part, *scratch,
):
    rows = x_ref.shape[0]
    width = x_ref.shape[1]
    block = pl.program_id(0)

    def own(dst, f, i, sem):
        bring(part.at[i, f], dst, sem)

    line = Line(count, pairs, half, steps, (res_ref, *scratch), own)

    @pl.when(block == 0)
    def _():
        greet(count)
        hist[0:8, :] = jnp.zeros((8, hist.shape[1]), F32)
        hist_bc[0:8, :] = jnp.zeros((8, hist_bc.shape[1]), F32)
        state[...] = jnp.zeros_like(state)

    x = x_ref[...].astype(F32)
    r1 = lax.rsqrt(jnp.sum(x * x, axis=1, keepdims=True) * (1.0 / width) + EPS)
    xn = (x * r1 * ng_ref[...]).astype(BF16)
    xn_ref[...] = xn
    z_ref[...] = dot(xn, wz_ref[...])
    xc = dot(xn, wx_ref[...])
    bc = dot(xn, wbc_ref[...])
    dtr = dot(xn, wdt_ref[...])
    xc_ref[...] = xc.astype(BF16)
    bc_ref[...] = bc
    dtr_ref[...] = dtr
    hist[8 : 8 + rows, :] = xc
    hist_bc[8 : 8 + rows, :] = bc
    meta = meta_ref[...]
    p_ref[...] = conv_taps(hist, cx_ref, meta, rows) + bx_ref[...]
    pbc_ref[...] = conv_taps(hist_bc, cbc_ref, meta, rows) + bbc_ref[...]
    hist[0:8, :] = hist[rows : rows + 8, :]
    hist_bc[0:8, :] = hist_bc[rows : rows + 8, :]
    g = g_ref[...]
    dn_ref[...] = dot_t(g, wo_ref[...])
    dt_all = softplus(dtr + dtb_ref[...])
    la_all = -jnp.exp(al_ref[...]) * dt_all
    lane8 = lax.broadcasted_iota(jnp.int32, (CHUNK, 8), 1)
    for piece in range(rows // CHUNK):
        at = pl.ds(piece * CHUNK, CHUNK)
        span = slice(piece * CHUNK, (piece + 1) * CHUNK)
        seg_col = meta[span, 6:7]
        keep = meta[span, 7:8]
        tail = meta[span, 8:9]
        dt = dt_all[span, :]
        cum, cum_t, visible = decays(la_all[span, :], seg_col, seg_ref[:, span])
        p = p_ref[at, :]
        u = p * sigmoid(p)
        pbc = pbc_ref[at, :]
        bcu = (pbc * sigmoid(pbc)).astype(BF16)
        n = bcu.shape[1] // 2
        b, c = bcu[:, :n], bcu[:, n:]
        scores = dot_t(c, b)
        v = spread(dt, heads) * u
        v_low = v.astype(BF16)
        pieces = []
        for pair in range(heads // 2):
            mats = [
                (scores * decay_matrix(cum, cum_t, visible, 2 * pair + k)).astype(BF16)
                for k in range(2)
            ]
            halves = split_pair(v_low[:, pair * LANES : (pair + 1) * LANES])
            pieces.append(dot(jnp.concatenate(mats, axis=1), jnp.concatenate(halves, axis=0)))
        inside = jnp.concatenate(pieces, axis=1)
        old = state[...]
        old_low = old.astype(BF16)
        st_ref[piece] = old_low
        entering = dot(c, old_low) * spread(jnp.exp(cum) * keep, heads)
        last = cum[CHUNK - 1 : CHUNK, :]
        to_end = spread(jnp.exp(last - cum) * tail, heads)
        carry = spread(jnp.exp(last) * keep[CHUNK - 1 : CHUNK, :], heads)
        state[...] = old * carry + tdot(b, (to_end * v).astype(BF16))
        ys = inside + entering + dsk_ref[...] * u
        ys_ref[at, :] = ys
        z = z_ref[at, :]
        gated = ys * (z * sigmoid(z))
        scaled = gated * og_ref[...]
        y_part = dot(scaled.astype(BF16), wo_ref[...]).astype(BF16)
        yp_ref[0, piece] = y_part
        part[block, piece] = y_part
        sums = jnp.sum(gated * gated, axis=1, keepdims=True)
        inner = jnp.sum(dn_ref[at, :] * scaled, axis=1, keepdims=True)
        stat_ref[at, :] = jnp.where(lane8 == 0, sums, jnp.where(lane8 == 1, inner, 0.0))
    run_steps(line, block, when, 0)

    @pl.when(block == len(when) - 1)
    def _():
        line.close(steps - 1, steps - 1, carry_out)


def run_steps(line, block, when, first):
    for b, ls in enumerate(when):
        if ls >= 0:

            @pl.when(block == b)
            def _():
                line.step(first + ls, ls)


def backward_kernel(
    heads, count, pairs, half, first, steps, when,
    z_ref, p_ref, xc_ref, ys_ref, pbc_ref, bc_ref, dtr_ref, dn_ref, st_ref, seg_ref, meta_ref, scal_ref,
    wz_ref, wx_ref, wbc_ref, wdt_ref, cx_ref, cbc_ref, dtb_ref, al_ref, dsk_ref, og_ref, y_ref, carry_ref, res_in,
    dz_ref, dx_ref, ddt_ref, dbc_ref, xp_ref, nm_ref, a768_ref, a256_ref, a128_ref,
    carry_out, res_ref, ahead, ahead_bc, d_state, part, *scratch,
):
    del res_in
    rows = z_ref.shape[0]
    inner = z_ref.shape[1]
    block = pl.program_id(0)

    def own(dst, f, i, sem):
        @pl.when(i < half)
        def _():
            bring(y_ref.at[i, f], dst, sem)

        @pl.when(i >= half)
        def _():
            bring(part.at[i - half, f], dst, sem)

    line = Line(count, pairs, half, steps, (res_ref, *scratch), own)

    @pl.when(block == 0)
    def _():
        greet(count)
        line.open(carry_ref)
        ahead[rows : rows + 8, :] = jnp.zeros((8, ahead.shape[1]), F32)
        ahead_bc[rows : rows + 8, :] = jnp.zeros((8, ahead_bc.shape[1]), F32)
        d_state[...] = jnp.zeros_like(d_state)
        a768_ref[...] = jnp.zeros_like(a768_ref)
        a256_ref[...] = jnp.zeros_like(a256_ref)
        a128_ref[...] = jnp.zeros_like(a128_ref)

    meta = meta_ref[...]
    r, c_ = iotas(CHUNK, CHUNK)
    upper = (r <= c_).astype(F32)
    below = (r > c_).astype(F32)
    seg_r, seg_l = iotas(inner, LANES)
    to_head = (seg_r // (inner // heads) == seg_l).astype(BF16)
    two_r, two_l = iotas(2 * CHUNK, LANES)
    decay_rate = -jnp.exp(al_ref[...])
    for piece in reversed(range(rows // CHUNK)):
        at = pl.ds(piece * CHUNK, CHUNK)
        span = slice(piece * CHUNK, (piece + 1) * CHUNK)
        seg_col = meta[span, 6:7]
        keep = meta[span, 7:8]
        tail = meta[span, 8:9]
        r2 = scal_ref[at, 0:1]
        k2 = scal_ref[at, 1:2]
        pre = dtr_ref[at, :] + dtb_ref[...]
        dt = softplus(pre)
        la = decay_rate * dt
        cum, cum_t, visible = decays(la, seg_col, seg_ref[:, span])
        z = z_ref[at, :]
        ys = ys_ref[at, :]
        sz = sigmoid(z)
        silu = z * sz
        gated = ys * silu
        dn = dn_ref[at, :]
        og = og_ref[...]
        d_gated = r2 * og * dn - gated * k2
        nm_ref[at, :] = (gated * r2 * og).astype(BF16)
        a768_ref[6:7, :] += jnp.sum(dn * gated * r2, axis=0, keepdims=True)
        dz_ref[at, :] = (d_gated * ys * (sz * (1.0 + z * (1.0 - sz)))).astype(BF16)
        dy = d_gated * silu
        dy_low = dy.astype(BF16)
        p = p_ref[at, :]
        sp = sigmoid(p)
        u = p * sp
        a768_ref[5:6, :] += jnp.sum(dy * u, axis=0, keepdims=True)
        pbc = pbc_ref[at, :]
        spbc = sigmoid(pbc)
        bcu = (pbc * spbc).astype(BF16)
        n = bcu.shape[1] // 2
        b, c = bcu[:, :n], bcu[:, n:]
        scores = dot_t(c, b)
        dt_x = spread(dt, heads)
        v = dt_x * u
        v_low = v.astype(BF16)
        d_scores = jnp.zeros((CHUNK, CHUNK), F32)
        d_cum = jnp.zeros((CHUNK, LANES), F32)
        pieces = []
        for pair in range(heads // 2):
            lanes = slice(pair * LANES, (pair + 1) * LANES)
            dy_halves = jnp.concatenate(split_pair(dy_low[:, lanes]), axis=0)
            grads = dot_t(dy_halves, v_low[:, lanes])
            mats, weighed = [], []
            for k in range(2):
                decay = decay_matrix(cum, cum_t, visible, 2 * pair + k)
                grad = grads[k * CHUNK : (k + 1) * CHUNK, :]
                mat = scores * decay
                d_scores = d_scores + grad * decay
                weighed.append((grad * mat).astype(BF16))
                mats.append(mat.astype(BF16))
            pieces.append(tdot(jnp.concatenate(mats, axis=0), dy_halves))
            pick = (two_l == 2 * pair + two_r // CHUNK).astype(BF16)
            d_cum = d_cum + dot(jnp.concatenate(weighed, axis=1), pick)
            d_cum = d_cum - tdot(jnp.concatenate(weighed, axis=0), pick)
        old_low = st_ref[piece]
        last = cum[CHUNK - 1 : CHUNK, :]
        enter_x = spread(jnp.exp(cum) * keep, heads)
        end_x = spread(jnp.exp(last - cum) * tail, heads)
        carry = spread(jnp.exp(last) * keep[CHUNK - 1 : CHUNK, :], heads)
        ds = d_state[...]
        ds_low = ds.astype(BF16)
        dv_state = end_x * dot(b, ds_low)
        dv = jnp.concatenate(pieces, axis=1) + dv_state
        dy_enter = enter_x * dy
        dy_enter_low = dy_enter.astype(BF16)
        d_b = dot_t((end_x * v).astype(BF16), ds_low)
        d_c = dot_t(dy_enter_low, old_low)
        e = dot((dy_enter * dot(c, old_low)).astype(BF16), to_head)
        f = dot((dv_state * v).astype(BF16), to_head)
        flow = jnp.sum(ds * old_low.astype(F32) * carry, axis=0, keepdims=True)
        flow = dot(flow, to_head.astype(F32), HIGHEST)
        d_state[...] = carry * ds + tdot(c, dy_enter_low)
        d_scores_low = d_scores.astype(BF16)
        d_c = d_c + dot(d_scores_low, b)
        d_b = d_b + tdot(d_scores_low, c)
        d_la = dot(upper, d_cum + e, HIGHEST) + dot(below, f, HIGHEST) + flow
        d_dt = d_la * decay_rate + dot((dv * u).astype(BF16), to_head)
        d_pre = d_dt * sigmoid(pre)
        ddt_ref[at, :] = d_pre.astype(BF16)
        a128_ref[0:1, :] += jnp.sum(d_pre, axis=0, keepdims=True)
        a128_ref[1:2, :] += jnp.sum(d_la * la, axis=0, keepdims=True)
        du = dt_x * dv + dsk_ref[...] * dy
        ahead[at, :] = du * (sp * (1.0 + p * (1.0 - sp)))
        d_bcu = jnp.concatenate([d_b, d_c], axis=1)
        ahead_bc[at, :] = d_bcu * (spbc * (1.0 + pbc * (1.0 - spbc)))

    for hist, weight, raw, out, acc in (
        (ahead, cx_ref, xc_ref, dx_ref, a768_ref),
        (ahead_bc, cbc_ref, bc_ref, dbc_ref, a256_ref),
    ):
        value = raw[...].astype(F32)
        dp = hist[0:rows, :]
        acc[4:5, :] += jnp.sum(dp, axis=0, keepdims=True)
        acc[3:4, :] += jnp.sum(dp * value, axis=0, keepdims=True)
        total = dp * weight[3:4, :]
        for k in range(1, 4):
            later = hist[k : k + rows, :] * meta[:, 2 + k : 3 + k]
            total = total + later * weight[3 - k : 4 - k, :]
            acc[3 - k : 4 - k, :] += jnp.sum(later * value, axis=0, keepdims=True)
        out[...] = total.astype(BF16)
        hist[rows : rows + 8, :] = hist[0:8, :]
    partial = dot_t(dz_ref[...], wz_ref[...]) + dot_t(dx_ref[...], wx_ref[...])
    partial = partial + dot_t(ddt_ref[...], wdt_ref[...]) + dot_t(dbc_ref[...], wbc_ref[...])
    for piece in range(rows // CHUNK):
        low = partial[piece * CHUNK : (piece + 1) * CHUNK, :].astype(BF16)
        xp_ref[0, piece] = low
        part[block, piece] = low
    run_steps(line, block, when, first)

    @pl.when(block == len(when) - 1)
    def _():
        line.close(first + steps - 1, steps - 1, carry_out)


def rows_spec(block, cols, last=None):
    if last is None:
        return pl.BlockSpec((block, cols), lambda i: (i, 0))
    return pl.BlockSpec((block, cols), lambda i: (last - i, 0))


def whole_spec(array):
    return pl.BlockSpec(array.shape, lambda i: (0, 0), pipeline_mode=pl.Buffered(1))


def lane_pad(array):
    return jnp.pad(array, ((0, 0), (0, LANES - array.shape[1])))


def token_masks(seg):
    length = seg.shape[0]
    t = jnp.arange(length)
    columns = []
    for k in range(1, 4):
        columns.append((jnp.roll(seg, k) == seg) & (t >= k))
    for k in range(1, 4):
        columns.append((jnp.roll(seg, -k) == seg) & (t < length - k))
    chunked = seg.reshape(-1, CHUNK)
    ends = chunked[:, -1:]
    before = jnp.concatenate([jnp.full((1, 1), -1, seg.dtype), ends[:-1]], axis=0)
    columns.append(seg)
    columns.append((chunked == before).reshape(-1))
    columns.append((chunked == ends).reshape(-1))
    columns = [column.astype(F32) for column in columns]
    columns += [jnp.zeros((length,), F32)] * (16 - len(columns))
    return jnp.stack(columns, axis=1)


def on_device(
    x_in, segments, out_grad, norm_gain, w_z, w_x, w_bc, w_dt, conv_x, conv_bc, bias_x, bias_bc,
    dt_bias, a_log, d_skip, out_gain, w_out,
):
    tensor_count = lax.axis_size("tensor")
    x, g, seg = x_in[0], out_grad[0], segments[0]
    length, width = x.shape
    inner = w_x.shape[1]
    heads = w_dt.shape[1]
    bc_width = w_bc.shape[1]
    blocks = length // BLOCK
    chunks = length // CHUNK
    per_block = BLOCK // CHUNK
    meta = token_masks(seg)
    seg_row = seg.astype(F32)[None, :]
    wdt = lane_pad(w_dt)
    dtb = lane_pad(dt_bias[None, :])
    al = lane_pad(a_log[None, :])
    dsk = jnp.repeat(d_skip, inner // heads)[None, :]
    og = out_gain[None, :]
    shape = jax.ShapeDtypeStruct
    pairs = 2 * blocks
    all_steps = pairs + 2 * tensor_count - 3
    spread_fwd = [b if b < 4 else (4 + (b - 5) // 2 if b % 2 else -1) for b in range(blocks)]
    spread_bwd = [b // 2 if b % 2 == 0 else -1 for b in range(blocks)]
    n_fwd = max(spread_fwd) + 1
    n_bwd = max(spread_bwd) + 1
    anywhere = pl.BlockSpec(memory_space=pl.ANY)
    pair_shape = (blocks, 2, CHUNK, width)
    carry_spec = pl.BlockSpec((2, CHUNK, width), lambda i: (0, 0, 0))
    carry_shape = jax.ShapeDtypeStruct((2, CHUNK, width), BF16)
    res_shape = jax.ShapeDtypeStruct((pairs, 2, CHUNK, width), BF16)

    def params(ident):
        return pltpu.CompilerParams(
            vmem_limit_bytes=60 * 2**20, dimension_semantics=("arbitrary",), collective_id=ident, has_side_effects=True
        )

    weights = (w_z, w_x, w_bc, wdt, w_out, norm_gain[None, :], conv_x, bias_x[None, :], conv_bc, bias_bc[None, :], dtb, al, dsk, og)
    z, p, xc, ys, pbc, bc, dtr, dn, xn, st, yp, stat, carry, res = pl.pallas_call(
        functools.partial(forward_kernel, heads, tensor_count, pairs, blocks, n_fwd, spread_fwd),
        grid=(blocks,),
        in_specs=[
            rows_spec(BLOCK, width),
            rows_spec(BLOCK, width),
            pl.BlockSpec((1, BLOCK), lambda i: (0, i)),
            rows_spec(BLOCK, meta.shape[1]),
            *[whole_spec(w) for w in weights],
        ],
        out_specs=[
            rows_spec(BLOCK, inner),
            rows_spec(BLOCK, inner),
            rows_spec(BLOCK, inner),
            rows_spec(BLOCK, inner),
            rows_spec(BLOCK, bc_width),
            rows_spec(BLOCK, bc_width),
            rows_spec(BLOCK, LANES),
            rows_spec(BLOCK, inner),
            rows_spec(BLOCK, width),
            pl.BlockSpec((per_block, bc_width // 2, inner), lambda i: (i, 0, 0)),
            pl.BlockSpec((1, 2, CHUNK, width), lambda i: (i, 0, 0, 0)),
            rows_spec(BLOCK, 8),
            carry_spec,
            anywhere,
        ],
        out_shape=[
            shape((length, inner), F32),
            shape((length, inner), F32),
            shape((length, inner), BF16),
            shape((length, inner), F32),
            shape((length, bc_width), F32),
            shape((length, bc_width), F32),
            shape((length, LANES), F32),
            shape((length, inner), F32),
            shape((length, width), BF16),
            shape((chunks, bc_width // 2, inner), BF16),
            shape(pair_shape, BF16),
            shape((length, 8), F32),
            carry_shape,
            res_shape,
        ],
        scratch_shapes=[
            pltpu.VMEM((BLOCK + 8, inner), F32),
            pltpu.VMEM((BLOCK + 8, bc_width), F32),
            pltpu.VMEM((bc_width // 2, inner), F32),
            pltpu.VMEM(pair_shape, BF16),
            *line_scratch(n_fwd, CHUNK, width),
        ],
        compiler_params=params(0),
        name="forward_scan",
    )(x, g, seg_row, meta, *weights)

    sums = lax.psum(stat[:, :2].T, "tensor")
    total = inner * tensor_count
    r2 = lax.rsqrt(sums[0] / total + EPS)
    k2 = r2 * r2 * r2 * (sums[1] / total)
    scal = jnp.stack([r2, k2] + [jnp.zeros_like(r2)] * 6, axis=1)

    last = blocks - 1
    weights = (w_z, w_x, w_bc, wdt, conv_x, conv_bc, dtb, al, dsk, og)
    dz, dx, ddt, dbc, xp, normed, a768, a256, a128, carry, res = pl.pallas_call(
        functools.partial(backward_kernel, heads, tensor_count, pairs, blocks, n_fwd, n_bwd, spread_bwd),
        grid=(blocks,),
        in_specs=[
            rows_spec(BLOCK, inner, last),
            rows_spec(BLOCK, inner, last),
            rows_spec(BLOCK, inner, last),
            rows_spec(BLOCK, inner, last),
            rows_spec(BLOCK, bc_width, last),
            rows_spec(BLOCK, bc_width, last),
            rows_spec(BLOCK, LANES, last),
            rows_spec(BLOCK, inner, last),
            pl.BlockSpec((per_block, bc_width // 2, inner), lambda i: (last - i, 0, 0)),
            pl.BlockSpec((1, BLOCK), lambda i: (0, last - i)),
            rows_spec(BLOCK, meta.shape[1], last),
            rows_spec(BLOCK, 8, last),
            *[whole_spec(w) for w in weights],
            anywhere,
            carry_spec,
            anywhere,
        ],
        out_specs=[
            rows_spec(BLOCK, inner, last),
            rows_spec(BLOCK, inner, last),
            rows_spec(BLOCK, LANES, last),
            rows_spec(BLOCK, bc_width, last),
            pl.BlockSpec((1, 2, CHUNK, width), lambda i: (last - i, 0, 0, 0)),
            rows_spec(BLOCK, inner, last),
            pl.BlockSpec((8, inner), lambda i: (0, 0)),
            pl.BlockSpec((8, bc_width), lambda i: (0, 0)),
            pl.BlockSpec((8, LANES), lambda i: (0, 0)),
            carry_spec,
            anywhere,
        ],
        out_shape=[
            shape((length, inner), BF16),
            shape((length, inner), BF16),
            shape((length, LANES), BF16),
            shape((length, bc_width), BF16),
            shape(pair_shape, BF16),
            shape((length, inner), BF16),
            shape((8, inner), F32),
            shape((8, bc_width), F32),
            shape((8, LANES), F32),
            carry_shape,
            res_shape,
        ],
        scratch_shapes=[
            pltpu.VMEM((BLOCK + 8, inner), F32),
            pltpu.VMEM((BLOCK + 8, bc_width), F32),
            pltpu.VMEM((bc_width // 2, inner), F32),
            pltpu.VMEM(pair_shape, BF16),
            *line_scratch(n_bwd, CHUNK, width),
        ],
        input_output_aliases={12 + len(weights) + 2: 10},
        compiler_params=params(1),
        name="backward_scan",
    )(z, p, xc, ys, pbc, bc, dtr, dn, st, seg_row, meta, scal, *weights, yp, carry, res)

    grad_wout = tdot(normed, g)
    grad_wz = tdot(xn, dz)
    grad_wx = tdot(xn, dx)
    grad_wdt = tdot(xn, ddt)[:, :heads]
    grad_wbc = tdot(xn, dbc)
    low = (grad_wz.astype(BF16), grad_wx.astype(BF16), grad_wout.astype(BF16))
    low, xp = lax.optimization_barrier((low, xp))
    rest = all_steps - n_fwd - n_bwd
    res = pl.pallas_call(
        functools.partial(line_kernel, tensor_count, pairs, blocks, n_fwd + n_bwd, rest),
        grid=(rest,),
        in_specs=[anywhere, anywhere, carry_spec, anywhere],
        out_specs=anywhere,
        out_shape=res_shape,
        scratch_shapes=line_scratch(rest, CHUNK, width),
        input_output_aliases={3: 0},
        compiler_params=params(2),
        cost_estimate=pl.CostEstimate(flops=10**11, bytes_accessed=3 * 10**8, transcendentals=0),
        name="line_sums",
    )(yp, xp, carry, res)
    y_sum = res[:blocks].reshape(length, width)
    x_sum = res[blocks:].reshape(length, width)
    result = (x.astype(F32) + r2[:, None] * y_sum.astype(F32)).astype(BF16)
    grad_wz, grad_wx, grad_wout = (v.astype(F32) for v in lax.psum(low, "dp"))
    grad_wbc = lax.psum(grad_wbc, ("dp", "tensor"))

    tokens = x.astype(F32)
    r1 = lax.rsqrt(jnp.mean(tokens * tokens, -1, keepdims=True) + EPS)
    dxn = x_sum.astype(F32)
    dot_x = jnp.sum(dxn * norm_gain * tokens, -1, keepdims=True)
    grad_x = (g.astype(F32) + r1 * norm_gain * dxn - tokens * (r1 * r1 * r1 * dot_x / width)).astype(BF16)
    grad_gain = jnp.sum(dxn * tokens * r1, 0)

    grad_dskip = jnp.sum(a768[5].reshape(heads, -1), axis=1)
    own = lax.psum((grad_gain, a768, a128, grad_wdt), "dp")
    shared = lax.psum(a256, ("dp", "tensor"))
    grad_gain, a768_all, a128_all, grad_wdt = own
    grad_dskip = jnp.sum(a768_all[5].reshape(heads, -1), axis=1)
    return (
        result[None],
        grad_x[None],
        grad_gain,
        grad_wz,
        grad_wx,
        grad_wbc,
        grad_wdt,
        a768_all[:4],
        shared[:4],
        a768_all[4],
        shared[4],
        a128_all[0, :heads],
        a128_all[1, :heads],
        grad_dskip,
        a768_all[6],
        grad_wout,
    )


def solution(mesh):
    tensor_last = P(None, "tensor")
    in_specs = (
        P("dp", None, None), P("dp", None), P("dp", None, None), P(), tensor_last, tensor_last, P(), tensor_last,
        tensor_last, P(), P("tensor"), P(), P("tensor"), P("tensor"), P("tensor"), P("tensor"), P("tensor", None),
    )
    out_specs = (
        P("dp", None, None), P("dp", None, None), P(), tensor_last, tensor_last, P(), tensor_last, tensor_last, P(),
        P("tensor"), P(), P("tensor"), P("tensor"), P("tensor"), P("tensor"), P("tensor", None),
    )
    return jax.shard_map(on_device, mesh=mesh, in_specs=in_specs, out_specs=out_specs, check_vma=False)
```

```python
import functools

import jax
import jax.numpy as jnp
from jax import lax
from jax.experimental import pallas as pl
from jax.experimental.pallas import tpu as pltpu
from jax.sharding import PartitionSpec as P

EPS = 1e-05
CHUNK = 128
BLOCK = 256
PIECES = BLOCK // CHUNK
LANES = 128
F32 = jnp.float32
BF16 = jnp.bfloat16
HIGHEST = lax.Precision.HIGHEST
MESH = pl.DeviceIdType.MESH


def dot(a, b, precision=None):
    return lax.dot_general(a, b, (((1,), (0,)), ((), ())), precision=precision, preferred_element_type=F32)


def dot_t(a, b):
    return lax.dot_general(a, b, (((1,), (1,)), ((), ())), preferred_element_type=F32)


def tdot(a, b):
    return lax.dot_general(a, b, (((0,), (0,)), ((), ())), preferred_element_type=F32)


def sigmoid(v):
    return 1.0 / (1.0 + jnp.exp(-v))


def softplus(v):
    e = jnp.exp(-jnp.abs(v))
    series = e * (1.0 - e * (0.5 - e * (1.0 / 3.0 - e * 0.25)))
    return jnp.maximum(v, 0.0) + jnp.where(e < 0.03, series, jnp.log(1.0 + e))


def iotas(rows, cols):
    return (
        lax.broadcasted_iota(jnp.int32, (rows, cols), 0),
        lax.broadcasted_iota(jnp.int32, (rows, cols), 1),
    )


def spread(columns, heads):
    rows = columns.shape[0]
    low = lax.broadcasted_iota(jnp.int32, (rows, LANES), 1) < LANES // 2
    pieces = []
    for pair in range(heads // 2):
        first = columns[:, 2 * pair : 2 * pair + 1]
        second = columns[:, 2 * pair + 1 : 2 * pair + 2]
        pieces.append(jnp.where(low, first, second))
    return jnp.concatenate(pieces, axis=1)


def decays(la, seg_col, seg_row):
    r, c = iotas(CHUNK, CHUNK)
    cum = dot((r >= c).astype(F32), la, HIGHEST)
    visible = (r >= c) & (seg_col == seg_row)
    return cum, cum.T, visible


def decay_matrix(cum, cum_t, visible, head):
    gap = cum[:, head : head + 1] - cum_t[head : head + 1, :]
    return jnp.exp(jnp.where(visible, gap, -1e30))


def split_pair(values):
    low = lax.broadcasted_iota(jnp.int32, values.shape, 1) < LANES // 2
    zero = jnp.zeros_like(values)
    return jnp.where(low, values, zero), jnp.where(low, zero, values)


def conv_taps(hist, weight, same, rows):
    out = hist[8 : 8 + rows, :] * weight[3:4, :]
    for k in range(1, 4):
        out = out + hist[8 - k : 8 - k + rows, :] * same[k - 1] * weight[3 - k : 4 - k, :]
    return out


def columns_of(segr_ref):
    rows = segr_ref.shape[1]
    pieces = []
    for at in range(0, rows, LANES):
        row = segr_ref[:, at : at + LANES].astype(F32)
        pieces.append(jnp.broadcast_to(row, (LANES, LANES)).T[:, 0:1])
    return jnp.concatenate(pieces, axis=0)


def fill_heads(hv, wdt_s, dtb_ref, al_ref, dsk_ref, wdt_ref):
    heads = wdt_ref.shape[0]
    hv[...] = jnp.zeros_like(hv)
    for j, ref in enumerate((dtb_ref, al_ref, dsk_ref)):
        hv[j : j + 1, 0:heads] = ref[...]
    wdt_s[...] = jnp.zeros_like(wdt_s)
    wdt_s[0:heads, :] = wdt_ref[...]


def row_of(ref):
    return ref[...].reshape(1, ref.shape[0])


def inverse_rms(tokens):
    return lax.rsqrt(jnp.sum(tokens * tokens, axis=1, keepdims=True) * (1.0 / tokens.shape[1]) + EPS)


def bring(src, dst, sem):
    copy = pltpu.make_async_copy(src, dst, sem)
    copy.start()
    copy.wait()


def greet(peers, dp_peers=()):
    barrier = pltpu.get_barrier_semaphore()
    total = jnp.int32(len(dp_peers))
    for peer in dp_peers:
        pl.semaphore_signal(barrier, inc=1, device_id={"dp": peer}, device_id_type=MESH)
    for peer, there in peers:

        @pl.when(there)
        def _():
            pl.semaphore_signal(barrier, inc=1, device_id={"tensor": peer}, device_id_type=MESH)

        total = total + there.astype(jnp.int32)
    pl.semaphore_wait(barrier, total)


def neighbours(count):
    me = lax.axis_index("tensor")
    return [(me - 1, me > 0), (me + 1, me < count - 1)]


class Line:
    def __init__(self, count, pairs, first, steps, refs, source, finals=None):
        self.count, self.pairs, self.first, self.steps = count, pairs, first, steps
        self.source, self.finals = source, finals
        (self.res_y, self.res_x, self.land, self.send) = refs[:4]
        (self.red_out, self.red_in, self.bc_out, self.bc_in, self.local) = refs[4:]

    def to_result(self, k, q, act):
        half = self.pairs // 2

        @pl.when(k < half)
        def _():
            act(self.res_y.at[k, q])

        @pl.when(k >= half)
        def _():
            act(self.res_x.at[2 * half - 1 - k, q])

    def flow(self, q):
        me = lax.axis_index("tensor")
        if q % 2 == 0:
            return me, me - 1, me + 1
        return self.count - 1 - me, me + 1, me - 1

    def is_pair(self, i):
        return (i >= 0) & (i < self.pairs)

    def red(self, q, ls, toward, src):
        return pltpu.make_async_remote_copy(
            src_ref=src, dst_ref=self.land.at[ls + 1, q], send_sem=self.red_out.at[q, ls],
            recv_sem=self.red_in.at[q, ls], device_id={"tensor": toward}, device_id_type=MESH,
        )

    def cast(self, q, ls, away, src, there):
        return pltpu.make_async_remote_copy(
            src_ref=src, dst_ref=there, send_sem=self.bc_out.at[q, ls],
            recv_sem=self.bc_in.at[q, ls], device_id={"tensor": away}, device_id_type=MESH,
        )

    def keep(self, q, there):
        return pltpu.make_async_copy(self.send.at[q], there, self.local.at[q])

    def finish_red(self, q, s, ls):
        z, toward, away = self.flow(q)
        n = self.count
        i = s - (n - 1) + z

        @pl.when(self.is_pair(i) & (z > 0))
        def _():
            self.red(q, ls, toward, self.send.at[q]).wait_send()

        @pl.when(self.is_pair(i) & (z == 0))
        def _():
            self.cast(q, ls, away, self.send.at[q], self.res_y.at[0, q]).wait_send()
            self.keep(q, self.res_y.at[0, q]).wait()

        @pl.when(self.is_pair(i + 1) & (z < n - 1))
        def _():
            self.red(q, ls, toward, self.send.at[q]).wait_recv()

    def finish_cast(self, q, s, ls):
        z, _, away = self.flow(q)
        n = self.count
        k = s - (n - 1) - z

        @pl.when(self.is_pair(k) & (z > 0) & (z < n - 1))
        def _():
            self.cast(q, ls, away, self.res_y.at[0, q], self.res_y.at[0, q]).wait_send()

        @pl.when(self.is_pair(k + 1) & (z > 0))
        def _():
            self.cast(q, ls, away, self.res_y.at[0, q], self.res_y.at[0, q]).wait_recv()

    def step(self, ls, h):
        n = self.count
        s = self.first + ls
        for q in (2 * h, 2 * h + 1):
            z, toward, away = self.flow(q)
            i = s - (n - 1) + z

            @pl.when(ls > 0)
            def _():
                self.finish_red(q, s - 1, ls - 1)

            @pl.when(self.is_pair(i))
            def _():
                mine = self.source(q, i)

                @pl.when(z == n - 1)
                def _():
                    self.red(q, ls, toward, mine).start()

                @pl.when((z > 0) & (z < n - 1))
                def _():
                    self.send[q] = (mine[...].astype(F32) + self.land[ls, q].astype(F32)).astype(BF16)
                    self.red(q, ls, toward, self.send.at[q]).start()

                @pl.when(z == 0)
                def _():
                    total = mine[...].astype(F32) + self.land[ls, q].astype(F32)
                    if self.finals is None:
                        self.send[q] = total.astype(BF16)
                    else:
                        self.finals.last(q, i, total, self.send)

                    def give(there):
                        self.cast(q, ls, away, self.send.at[q], there).start()
                        self.keep(q, there).start()

                    self.to_result(i, q, give)
                    if self.finals is not None:

                        @pl.when(ls + 1 < self.steps)
                        def _():
                            self.finals.fetch(q, i + 1)

        for q in (2 * h, 2 * h + 1):

            @pl.when(ls > 0)
            def _():
                self.finish_cast(q, s - 1, ls - 1)

            z, toward, away = self.flow(q)
            k = s - (n - 1) - z

            @pl.when(self.is_pair(k) & (z > 0) & (z < n - 1))
            def _():
                self.to_result(k, q, lambda there: self.cast(q, ls, away, there, there).start())

    def held(self, q, s):
        z, _, _ = self.flow(q)
        return self.is_pair(s - (self.count - 1) + z) & (z < self.count - 1)

    def open(self, carry):
        for q in range(4):

            @pl.when(self.held(q, self.first))
            def _():
                bring(carry.at[q], self.land.at[0, q], self.local.at[q])

            z, _, _ = self.flow(q)

            @pl.when(z == 0)
            def _():
                self.finals.fetch(q, jnp.int32(self.first - (self.count - 1)))

    def close(self, carry):
        ls = self.steps - 1
        s = self.first + ls
        for q in range(4):
            self.finish_red(q, s, ls)
            self.finish_cast(q, s, ls)
            if carry is None:
                continue

            @pl.when(self.held(q, s + 1))
            def _():
                bring(self.land.at[ls + 1, q], carry.at[q], self.local.at[q])


def line_scratch(steps, width):
    return [
        pltpu.VMEM((steps + 1, 4, BLOCK // 4, width), BF16),
        pltpu.VMEM((4, BLOCK // 4, width), BF16),
        pltpu.SemaphoreType.DMA((4, steps)),
        pltpu.SemaphoreType.DMA((4, steps)),
        pltpu.SemaphoreType.DMA((4, steps)),
        pltpu.SemaphoreType.DMA((4, steps)),
        pltpu.SemaphoreType.DMA((4,)),
    ]


class Finals:
    def __init__(self, pairs, x_any, g_any, gain, rows, sems):
        self.pairs, self.half, self.x_any, self.g_any, self.gain, self.rows, self.sems = (
            pairs, pairs // 2, x_any, g_any, gain, rows, sems,
        )

    def copies(self, q, i):
        b = 2 * self.half - 1 - i
        return [
            pltpu.make_async_copy(src.at[b, q], self.rows.at[q, j], self.sems.at[q, j])
            for j, src in enumerate((self.x_any, self.g_any))
        ]

    def fetch(self, q, i):
        @pl.when((i >= self.half) & (i < self.pairs))
        def _():
            for copy in self.copies(q, i):
                copy.start()

    def last(self, q, i, total, out):
        @pl.when(i < self.half)
        def _():
            out[q] = total.astype(BF16)

        @pl.when(i >= self.half)
        def _():
            for copy in self.copies(q, i):
                copy.wait()
            x = self.rows[q, 0].astype(F32)
            r1 = inverse_rms(x)
            scaled = total * self.gain
            across = jnp.sum(scaled * x, axis=1, keepdims=True) * (1.0 / x.shape[1])
            out[q] = (self.rows[q, 1].astype(F32) + r1 * scaled - x * (r1 * r1 * r1 * across)).astype(BF16)


def finals_scratch(width):
    return [pltpu.VMEM((4, 2, BLOCK // 4, width), BF16), pltpu.SemaphoreType.DMA((4, 2))]


def dp_bits():
    me = lax.axis_index("dp")
    bits = []
    for b in range(lax.axis_size("dp").bit_length() - 1):
        bit = lax.rem(me // 2**b, 2)
        bits.append((bit, me + (1 - 2 * bit) * 2**b))
    return bits


class Cube:
    def __init__(self, order, refs, across=None):
        self.order, self.across = order, across
        (self.src, self.out, self.total, self.send, self.land, self.out_sem, self.in_sem, self.local) = refs
        self.rows = self.src.shape[0]
        self.bits = dp_bits()
        self.events = 2 * len(order) + (1 if across is None else 2)

    def start_of(self, depth):
        at = 0
        for j in range(depth):
            at = at + self.bits[self.order[j]][0] * (self.rows >> (j + 1))
        return at

    def span(self, at, size):
        return pl.ds(pl.multiple_of(at, 8 if self.src.dtype == F32 else 16), size)

    def inside(self, depth):
        return self.start_of(depth) - self.start_of(1)

    def halving(self, j):
        size = self.rows >> (j + 1)
        bit, partner = self.bits[self.order[j]]
        theirs = self.start_of(j) + (1 - bit) * size
        src = self.src.at[self.span(theirs, size), :] if j == 0 else self.send.at[pl.ds(0, size), :]
        return pltpu.make_async_remote_copy(
            src_ref=src, dst_ref=self.land.at[pl.ds(self.rows - 2 * size, size), :], send_sem=self.out_sem.at[j],
            recv_sem=self.in_sem.at[j], device_id={"dp": partner}, device_id_type=MESH,
        )

    def doubling(self, j):
        count = len(self.order)
        size = self.rows >> (count - j)
        _, partner = self.bits[self.order[count - 1 - j]]
        mine = self.out.at[self.span(self.start_of(count - j), size), :]
        return pltpu.make_async_remote_copy(
            src_ref=mine, dst_ref=mine, send_sem=self.out_sem.at[count + j], recv_sem=self.in_sem.at[count + j],
            device_id={"dp": partner}, device_id_type=MESH,
        )

    def crossing(self, d):
        land, out_sem, in_sem, peers = self.across
        return pltpu.make_async_remote_copy(
            src_ref=self.send.at[pl.ds(0, land.shape[1]), :], dst_ref=land.at[d - 1], send_sem=out_sem.at[d - 1],
            recv_sem=in_sem.at[d - 1], device_id={"tensor": peers[d - 1]}, device_id_type=MESH,
        )

    def turn(self):
        count = len(self.order)
        size = self.rows >> count
        bring(self.send.at[pl.ds(0, size), :], self.out.at[self.span(self.start_of(count), size), :], self.local)
        self.doubling(0).start()

    def event(self, e):
        count = len(self.order)
        if e == 0:
            self.halving(0).start()
            mine = self.src.at[self.span(self.start_of(1), self.rows // 2), :]
            bring(mine, self.send.at[pl.ds(0, self.rows // 2), :], self.local)
            return
        if e <= count:
            self.halving(e - 1).wait()
            size = self.rows >> e
            at = self.inside(e)
            for r in range(0, size, 192):
                tile = min(192, size - r)
                landed = self.land[self.rows - 2 * size + r : self.rows - 2 * size + r + tile, :].astype(F32)
                here = self.span(at + r, tile)
                if e == 1:
                    self.total[here, :] = self.send[r : r + tile, :].astype(F32) + landed
                else:
                    self.total[here, :] = self.total[here, :] + landed
            if e < count:
                bit, _ = self.bits[self.order[e]]
                at = at + (1 - bit) * (size // 2)
                size = size // 2
            self.send[0:size, :] = self.total[self.span(at, size), :].astype(self.send.dtype)
            if e < count:
                self.halving(e).start()
            elif self.across is None:
                self.turn()
            else:
                for d in range(1, len(self.across[3]) + 1):
                    self.crossing(d).start()
            return
        if self.across is not None:
            if e == count + 1:
                size = self.rows >> count
                total = self.total[self.span(self.inside(count), size), :]
                for d in range(1, len(self.across[3]) + 1):
                    self.crossing(d).wait()
                    total = total + self.across[0][d - 1].astype(F32)
                self.send[0:size, :] = total.astype(self.send.dtype)
                self.turn()
                return
            e = e - 1
        self.doubling(e - count - 1).wait()
        if e < 2 * count:
            self.doubling(e - count).start()


def cube_scratch(rows, cols, bits, dtype):
    return [
        pltpu.VMEM((rows // 2, cols), F32),
        pltpu.VMEM((rows // 2, cols), dtype),
        pltpu.VMEM((rows - (rows >> bits), cols), dtype),
        pltpu.SemaphoreType.DMA((2 * bits,)),
        pltpu.SemaphoreType.DMA((2 * bits,)),
        pltpu.SemaphoreType.DMA,
    ]


def cross_scratch(count, rows, cols, dtype):
    return [
        pltpu.VMEM((count - 1, rows, cols), dtype),
        pltpu.SemaphoreType.DMA((count - 1,)),
        pltpu.SemaphoreType.DMA((count - 1,)),
    ]


def tensor_peers(count):
    me = lax.axis_index("tensor")
    return [lax.rem(me + d, count) for d in range(1, count)]


def line_kernel(
    count, pairs, first, steps, xp_ref, x_any, g_any, ng_ref, carry_ref, gz_ref, gx_ref, gb_ref, pk_ref, res_y_in, res_x_in,
    res_y, res_x, oz_ref, ox_ref, ob_ref, op_ref, part, part_sem, rows, sems, *scratch,
):
    del res_y_in, res_x_in
    half = pairs // 2
    order = list(range(len(dp_bits())))
    other = order[:1] + order[:0:-1]
    peers = tensor_peers(count)
    cubes = [
        Cube(order, (gz_ref, oz_ref, *scratch[0:6])),
        Cube(other, (gx_ref, ox_ref, *scratch[6:12])),
        Cube(other, (gb_ref, ob_ref, *scratch[12:18]), (*scratch[24:27], peers)),
        Cube(order, (pk_ref, op_ref, *scratch[18:24]), (*scratch[27:30], peers)),
    ]
    finals = Finals(pairs, x_any, g_any, row_of(ng_ref), rows, sems)
    line = Line(
        count, pairs, first, steps, (res_y, res_x, *scratch[30:]), lambda q, i: part.at[2 * half - 1 - i, q], finals
    )
    at = pl.program_id(0)

    @pl.when(at == 0)
    def _():
        terms = pltpu.make_async_copy(xp_ref.at[pl.ds(0, part.shape[0])], part, part_sem)
        terms.start()
        greet([(peer, peer >= 0) for peer in peers], [partner for _, partner in dp_bits()])
        line.open(carry_ref)
        terms.wait()

    turn = len(order)
    last = 2 * steps - 1
    plain = [0, 1] + [2 * e - 1 for e in range(2, turn)] + [2 * turn - 2, 2 * turn - 1]
    plain += [2 * (turn + j) - 1 for j in range(1, turn - 1)] + [4 * turn - 4]
    crossed = plain[: turn + 1] + [2 * turn - 1, 2 * turn + 1] + plain[turn + 3 :] + [4 * turn - 3]
    times = [plain, plain, crossed, crossed]
    for h in range(2):
        line.step(at, h)
        for cube, when in zip(cubes, times):
            for e, t in enumerate(when):
                t = min(t, last)
                if t % 2 == h:

                    @pl.when(at == t // 2)
                    def _():
                        cube.event(e)

    @pl.when(at == steps - 1)
    def _():
        line.close(None)


def finish_kernel(
    heads, count, x_ref, y_ref, dx_ref, scal_ref, gz_ref, gx_ref, go_ref, go2_ref, gb_ref, pack_ref,
    yo_ref, xo_ref, oz_ref, ox_ref, oo_ref, wbc_ref, wdt_ref, ng_ref, cx_ref, bx_ref, og_ref, ds_ref, cbc_ref, bbc_ref,
    dtb_ref, al_ref,
):
    inner = cx_ref.shape[1]
    width, bcw = x_ref.shape[1], wbc_ref.shape[1]
    me = lax.axis_index("tensor")
    for piece in range(PIECES):
        span = slice(piece * CHUNK, (piece + 1) * CHUNK)
        r2 = jnp.concatenate([scal_ref[piece], jnp.zeros((CHUNK - 8, CHUNK), F32)], axis=0).T[:, 0:1]
        yo_ref[span, :] = (x_ref[span, :].astype(F32) + r2 * y_ref[span, :].astype(F32)).astype(BF16)
    xo_ref[...] = dx_ref[...]
    oz_ref[...] = gz_ref[...].astype(F32)
    ox_ref[...] = gx_ref[...].astype(F32)
    oo_ref[:, 0 : width // 2] = go_ref[...].astype(F32)
    oo_ref[:, width // 2 :] = go2_ref[...].astype(F32)
    wbc_ref[...] = gb_ref[...].astype(F32)

    @pl.when(pl.program_id(0) == 0)
    def _():
        at = 0
        base = pl.multiple_of(at + me * dt_rows(width), 8)
        for j in range(width // LANES):
            wdt_ref[:, j * LANES : (j + 1) * LANES] = pack_ref[pl.ds(base + 16 * j, 16), :][0:heads, :]
        at += count * dt_rows(width)
        def put(ref, row):
            ref[...] = row.reshape(ref.shape)

        put(ng_ref, jnp.concatenate([pack_ref[at + 8 * j : at + 8 * j + 1, :] for j in range(width // LANES)], axis=1))
        at += width // LANES * 8
        rows = jnp.concatenate([pack_ref[at + 8 * j : at + 8 * j + 8, :] for j in range(bcw // LANES)], axis=1)
        cbc_ref[...] = rows[0:4, :]
        put(bbc_ref, rows[4:5, :])
        at += bcw // LANES * 8
        base = pl.multiple_of(at + me * slot_rows(inner), 8)
        rows = jnp.concatenate([pack_ref[pl.ds(base + 8 * j, 8), :] for j in range(inner // LANES)], axis=1)
        cx_ref[...] = rows[0:4, :]
        put(bx_ref, rows[4:5, :])
        put(og_ref, rows[6:7, :])
        lane = lax.broadcasted_iota(jnp.int32, (1, heads), 1)
        skip = jnp.zeros((1, heads), F32)
        for h in range(heads):
            head = jnp.sum(rows[5:6, h * 64 : h * 64 + 64], axis=1, keepdims=True)
            skip = jnp.where(lane == h, head, skip)
        ds_ref[...] = skip
        rows = pack_ref[pl.ds(base + inner // LANES * 8, 8), :]
        dtb_ref[...] = rows[0:1, 0:heads]
        al_ref[...] = rows[1:2, 0:heads]


def forward_kernel(
    heads, count, pairs, steps, blocks,
    x_ref, g_ref, segr_ref, wz_ref, wx_ref, wbc_ref, wdt_ref, wo_ref, ng_ref, bx_ref, og_ref, bbc_ref, cx_ref, cbc_ref,
    dtb_ref, al_ref, dsk_ref,
    z_ref, p_ref, xc_ref, ys_ref, pbc_ref, bc_ref, dtr_ref, dn_ref, st_ref, yp_ref, scal_ref, wout_ref,
    carry_out, res_y, res_x,
    hv_ref, wdt_s, hist, hist_bc, segs, state, scaled_s, g_s, acc_out, stat_mine, stat_land, stat_out, stat_in, part, *scratch,
):
    rows, width = x_ref.shape
    inner = z_ref.shape[1]
    block = pl.program_id(0)
    me = lax.axis_index("tensor")
    ng, bx, og, bbc = row_of(ng_ref), row_of(bx_ref), row_of(og_ref), row_of(bbc_ref)

    line = Line(count, pairs, 0, steps, (res_y, res_x, *scratch), lambda q, i: part.at[i, q])

    @pl.when(block == 0)
    def _():
        greet([(lax.rem(me + d, count), me >= 0) for d in range(1, count)])
        fill_heads(hv_ref, wdt_s, dtb_ref, al_ref, dsk_ref, wdt_ref)
        hist[0:8, :] = jnp.zeros((8, hist.shape[1]), F32)
        hist_bc[0:8, :] = jnp.zeros((8, hist_bc.shape[1]), F32)
        segs[0:8, :] = jnp.full((8, 1), -1.0, F32)
        state[...] = jnp.zeros_like(state)
        acc_out[...] = jnp.zeros_like(acc_out)

    x = x_ref[...].astype(F32)
    xn = (x * inverse_rms(x) * ng).astype(BF16)
    z_ref[...] = dot(xn, wz_ref[...])
    xc = dot(xn, wx_ref[...])
    bc = dot(xn, wbc_ref[...])
    dtr = dot_t(xn, wdt_s[...])
    xc_ref[...] = xc.astype(BF16)
    bc_ref[...] = bc
    dtr_ref[...] = dtr
    seg_all = columns_of(segr_ref)
    segs[8 : 8 + rows, :] = seg_all
    hist[8 : 8 + rows, :] = xc
    hist_bc[8 : 8 + rows, :] = bc
    same = [(segs[8 - k : 8 - k + rows, :] == seg_all).astype(F32) for k in range(1, 4)]
    p_ref[...] = conv_taps(hist, cx_ref, same, rows) + bx
    pbc_ref[...] = conv_taps(hist_bc, cbc_ref, same, rows) + bbc
    g = g_ref[...]
    g_s[lax.rem(block, 2)] = g
    dn_ref[...] = dot_t(g, wo_ref[...])
    dt_all = softplus(dtr + hv_ref[0:1, :])
    la_all = -jnp.exp(hv_ref[1:2, :]) * dt_all
    dsk = spread(hv_ref[2:3, :], heads)
    row_i, lane_i = iotas(CHUNK, LANES)
    for piece in range(PIECES):
        at = pl.ds(piece * CHUNK, CHUNK)
        span = slice(piece * CHUNK, (piece + 1) * CHUNK)
        seg_col = seg_all[span, :]
        keep = (seg_col == segs[7 + piece * CHUNK : 8 + piece * CHUNK, :]).astype(F32)
        tail = (seg_col == seg_col[CHUNK - 1 : CHUNK, :]).astype(F32)
        dt = dt_all[span, :]
        cum, cum_t, visible = decays(la_all[span, :], seg_col, segr_ref[:, span].astype(F32))
        p = p_ref[at, :]
        u = p * sigmoid(p)
        pbc = pbc_ref[at, :]
        bcu = (pbc * sigmoid(pbc)).astype(BF16)
        n = bcu.shape[1] // 2
        b, c = bcu[:, :n], bcu[:, n:]
        scores = dot_t(c, b)
        v = spread(dt, heads) * u
        v_low = v.astype(BF16)
        pieces = []
        for pair in range(heads // 2):
            mats = [
                (scores * decay_matrix(cum, cum_t, visible, 2 * pair + k)).astype(BF16)
                for k in range(2)
            ]
            halves = split_pair(v_low[:, pair * LANES : (pair + 1) * LANES])
            pieces.append(dot(jnp.concatenate(mats, axis=1), jnp.concatenate(halves, axis=0)))
        inside = jnp.concatenate(pieces, axis=1)
        old = state[...]
        old_low = old.astype(BF16)
        st_ref[piece] = old_low
        entering = dot(c, old_low) * spread(jnp.exp(cum) * keep, heads)
        last = cum[CHUNK - 1 : CHUNK, :]
        to_end = spread(jnp.exp(last - cum) * tail, heads)
        carry = spread(jnp.exp(last) * keep[CHUNK - 1 : CHUNK, :], heads)
        state[...] = old * carry + tdot(b, (to_end * v).astype(BF16))
        ys = inside + entering + dsk * u
        ys_ref[at, :] = ys
        z = z_ref[at, :]
        gated = ys * (z * sigmoid(z))
        scaled = gated * og
        scaled_s[lax.rem(block, 2), at, :] = scaled
        y_part = dot(scaled.astype(BF16), wo_ref[...]).astype(BF16)
        for q in range(2):
            yp_ref[0, 2 * piece + q] = y_part[q * 64 : q * 64 + 64, :]

        @pl.when(block < part.shape[0])
        def _():
            for q in range(2):
                part[jnp.minimum(block, part.shape[0] - 1), 2 * piece + q] = y_part[q * 64 : q * 64 + 64, :]

        if piece == 0:

            @pl.when((block >= 4) & (lax.rem(block, 2) == 0))
            def _():
                line.step(block // 2 + 1, 1)

            @pl.when((block < 4) | (lax.rem(block, 2) == 1))
            def _():
                line.step(jnp.where(block < 4, block, (block + 3) // 2), 0)

        else:

            @pl.when(block < 3)
            def _():
                line.step(block, 1)

        sums = jnp.sum(gated * gated, axis=1, keepdims=True)
        across = jnp.sum(dn_ref[at, :] * scaled, axis=1, keepdims=True)
        both = jnp.where(lane_i == 0, sums, jnp.where(lane_i == 1, across, 0.0))
        stat_mine[block, piece] = both.T[0:8, :]
    hist[0:8, :] = hist[rows : rows + 8, :]
    hist_bc[0:8, :] = hist_bc[rows : rows + 8, :]
    segs[0:8, :] = segs[rows : rows + 8, :]

    def stat_copy(d, b):
        return pltpu.make_async_remote_copy(
            src_ref=stat_mine.at[b], dst_ref=stat_land.at[d - 1, b], send_sem=stat_out.at[d - 1, b],
            recv_sem=stat_in.at[d - 1, b], device_id={"tensor": lax.rem(me + d, count)}, device_id_type=MESH,
        )

    def settle(b):
        total = stat_mine[b]
        for d in range(1, count):
            stat_copy(d, b).wait()
            total = total + stat_land[d - 1, b]
        place = lax.rem(b, 2)
        low = []
        for piece in range(PIECES):
            r2 = lax.rsqrt(total[piece, 0:1, :] * (1.0 / (inner * count)) + EPS)
            k2 = r2 * r2 * r2 * (total[piece, 1:2, :] * (1.0 / (inner * count)))
            both = jnp.where(row_i == 0, r2, jnp.where(row_i == 1, k2, 0.0))
            scal_ref[b * PIECES + piece] = both[0:8, :]
            low.append((scaled_s[place, piece * CHUNK : (piece + 1) * CHUNK, :] * both.T[:, 0:1]).astype(BF16))
        normed = jnp.concatenate(low, axis=0)
        up = g_s[place]
        for c in range(0, inner, 256):
            acc_out[c : c + 256, :] += tdot(normed[:, c : c + 256], up)

    for d in range(1, count):
        stat_copy(d, block).start()

    @pl.when(block > 0)
    def _():
        settle(block - 1)

    @pl.when(block == blocks - 1)
    def _():
        settle(block)
        for c in range(0, inner, 256):
            low = acc_out[c : c + 256, :].astype(BF16)
            wout_ref[c : c + 256, :] = low[:, 0 : width // 2]
            wout_ref[inner + c : inner + c + 256, :] = low[:, width // 2 :]
        line.step(jnp.int32(steps - 1), 1)
        line.close(carry_out)


def backward_kernel(
    heads, count, pairs, first, steps,
    z_ref, p_ref, xc_ref, ys_ref, pbc_ref, bc_ref, dtr_ref, dn_ref, st_ref, segp_ref, segr_ref, scal_ref, x_ref,
    wz_ref, wx_ref, wbc_ref, wdt_ref, ng_ref, og_ref, cx_ref, cbc_ref, dtb_ref, al_ref, dsk_ref, y_ref, x_any, g_any, carry_ref, go_ref, res_y_in, res_x_in,
    xp_ref, gz_ref, gx_ref, gb_ref, pack_ref, carry_out, go_sum, res_y, res_x,
    hv_ref, wdt_s, ahead, ahead_bc, segs, d_state, dz_s, dx_s, ddt_s, dbc_s, acc_z, acc_x, acc_bc, acc_dt,
    a1536, a768, a256, a128, rest, low_bc, stage, stage_sem, part, part_sem, rows_s, rows_sem, *scratch,
):
    del res_y_in, res_x_in
    rows, inner = z_ref.shape
    width = x_ref.shape[1]
    block = pl.program_id(0)
    blocks = steps
    half = pairs // 2
    me = lax.axis_index("tensor")
    ng, og = row_of(ng_ref), row_of(og_ref)

    finals = Finals(pairs, x_any, g_any, ng, rows_s, rows_sem)
    line = Line(
        count, pairs, first, steps, (res_y, res_x, *scratch[6:]), lambda q, i: part.at[lax.rem(i, half), q], finals
    )
    cube = Cube(list(range(len(dp_bits()))), (go_ref, go_sum, *scratch[0:6]))
    old = first - (count - 1)

    @pl.when(block == 0)
    def _():
        terms = pltpu.make_async_copy(y_ref.at[pl.ds(old, half - old)], part.at[pl.ds(old, half - old)], part_sem)
        terms.start()
        greet(neighbours(count), [partner for _, partner in dp_bits()])
        line.open(carry_ref)
        terms.wait()
        fill_heads(hv_ref, wdt_s, dtb_ref, al_ref, dsk_ref, wdt_ref)
        ahead[rows : rows + 8, :] = jnp.zeros((8, ahead.shape[1]), F32)
        ahead_bc[rows : rows + 8, :] = jnp.zeros((8, ahead_bc.shape[1]), F32)
        segs[rows : rows + 8, :] = jnp.full((8, 1), -1.0, F32)
        for ref in (d_state, acc_z, acc_x, acc_bc, acc_dt, a1536, a768, a256, a128, rest):
            ref[...] = jnp.zeros_like(ref)

    line.step(block, 0)
    seg_all = columns_of(segr_ref)
    segs[0:rows, :] = seg_all
    before = jnp.where(block == blocks - 1, -1.0, segp_ref[:, rows - 1 : rows].astype(F32))
    r, c_ = iotas(CHUNK, CHUNK)
    upper = (r <= c_).astype(F32)
    below = (r > c_).astype(F32)
    seg_r, seg_l = iotas(inner, LANES)
    to_head = (seg_r // (inner // heads) == seg_l).astype(BF16)
    two_r, two_l = iotas(2 * CHUNK, LANES)
    decay_rate = -jnp.exp(hv_ref[1:2, :])
    dsk = spread(hv_ref[2:3, :], heads)
    for piece in reversed(range(PIECES)):
        at = pl.ds(piece * CHUNK, CHUNK)
        span = slice(piece * CHUNK, (piece + 1) * CHUNK)
        seg_col = seg_all[span, :]
        prev = seg_all[piece * CHUNK - 1 : piece * CHUNK, :] if piece else before
        keep = (seg_col == prev).astype(F32)
        tail = (seg_col == seg_col[CHUNK - 1 : CHUNK, :]).astype(F32)
        scal = jnp.concatenate([scal_ref[piece], jnp.zeros((CHUNK - 8, CHUNK), F32)], axis=0).T
        r2 = scal[:, 0:1]
        k2 = scal[:, 1:2]
        pre = dtr_ref[at, :] + hv_ref[0:1, :]
        dt = softplus(pre)
        la = decay_rate * dt
        cum, cum_t, visible = decays(la, seg_col, segr_ref[:, span].astype(F32))
        z = z_ref[at, :]
        ys = ys_ref[at, :]
        sz = sigmoid(z)
        silu = z * sz
        gated = ys * silu
        dn = dn_ref[at, :]
        d_gated = r2 * og * dn - gated * k2
        a768[6:7, :] += jnp.sum(dn * gated * r2, axis=0, keepdims=True)
        dz_s[at, :] = (d_gated * ys * (sz * (1.0 + z * (1.0 - sz)))).astype(BF16)
        dy = d_gated * silu
        dy_low = dy.astype(BF16)
        p = p_ref[at, :]
        sp = sigmoid(p)
        u = p * sp
        a768[5:6, :] += jnp.sum(dy * u, axis=0, keepdims=True)
        pbc = pbc_ref[at, :]
        spbc = sigmoid(pbc)
        bcu = (pbc * spbc).astype(BF16)
        n = bcu.shape[1] // 2
        b, c = bcu[:, :n], bcu[:, n:]
        scores = dot_t(c, b)
        dt_x = spread(dt, heads)
        v = dt_x * u
        v_low = v.astype(BF16)
        d_scores = jnp.zeros((CHUNK, CHUNK), F32)
        d_cum = jnp.zeros((CHUNK, LANES), F32)
        pieces = []
        for pair in range(heads // 2):
            lanes = slice(pair * LANES, (pair + 1) * LANES)
            dy_halves = jnp.concatenate(split_pair(dy_low[:, lanes]), axis=0)
            grads = dot_t(dy_halves, v_low[:, lanes])
            mats, weighed = [], []
            for k in range(2):
                decay = decay_matrix(cum, cum_t, visible, 2 * pair + k)
                grad = grads[k * CHUNK : (k + 1) * CHUNK, :]
                mat = scores * decay
                d_scores = d_scores + grad * decay
                weighed.append((grad * mat).astype(BF16))
                mats.append(mat.astype(BF16))
            pieces.append(tdot(jnp.concatenate(mats, axis=0), dy_halves))
            pick = (two_l == 2 * pair + two_r // CHUNK).astype(BF16)
            d_cum = d_cum + dot(jnp.concatenate(weighed, axis=1), pick)
            d_cum = d_cum - tdot(jnp.concatenate(weighed, axis=0), pick)
        old_low = st_ref[piece]
        last = cum[CHUNK - 1 : CHUNK, :]
        enter_x = spread(jnp.exp(cum) * keep, heads)
        end_x = spread(jnp.exp(last - cum) * tail, heads)
        carry = spread(jnp.exp(last) * keep[CHUNK - 1 : CHUNK, :], heads)
        ds = d_state[...]
        ds_low = ds.astype(BF16)
        dv_state = end_x * dot(b, ds_low)
        dv = jnp.concatenate(pieces, axis=1) + dv_state
        dy_enter = enter_x * dy
        dy_enter_low = dy_enter.astype(BF16)
        d_b = dot_t((end_x * v).astype(BF16), ds_low)
        d_c = dot_t(dy_enter_low, old_low)
        e = dot((dy_enter * dot(c, old_low)).astype(BF16), to_head)
        f = dot((dv_state * v).astype(BF16), to_head)
        flow = jnp.sum(ds * old_low.astype(F32) * carry, axis=0, keepdims=True)
        flow = dot(flow, to_head.astype(F32), HIGHEST)
        d_state[...] = carry * ds + tdot(c, dy_enter_low)
        d_scores_low = d_scores.astype(BF16)
        d_c = d_c + dot(d_scores_low, b)
        d_b = d_b + tdot(d_scores_low, c)
        d_la = dot(upper, d_cum + e, HIGHEST) + dot(below, f, HIGHEST) + flow
        d_dt = d_la * decay_rate + dot((dv * u).astype(BF16), to_head)
        d_pre = d_dt * sigmoid(pre)
        ddt_s[at, :] = d_pre.astype(BF16)
        a128[0:1, :] += jnp.sum(d_pre, axis=0, keepdims=True)
        a128[1:2, :] += jnp.sum(d_la * la, axis=0, keepdims=True)
        du = dt_x * dv + dsk * dy
        ahead[at, :] = du * (sp * (1.0 + p * (1.0 - sp)))
        d_bcu = jnp.concatenate([d_b, d_c], axis=1)
        ahead_bc[at, :] = d_bcu * (spbc * (1.0 + pbc * (1.0 - spbc)))

    line.step(block, 1)
    for e in range(cube.events):

        @pl.when(block == min(e, blocks - 1))
        def _():
            cube.event(e)

    same = [(segs[k : k + rows, :] == seg_all).astype(F32) for k in range(1, 4)]
    for hist, weight, raw, out, acc in (
        (ahead, cx_ref, xc_ref, dx_s, a768),
        (ahead_bc, cbc_ref, bc_ref, dbc_s, a256),
    ):
        value = raw[...].astype(F32)
        dp = hist[0:rows, :]
        acc[4:5, :] += jnp.sum(dp, axis=0, keepdims=True)
        acc[3:4, :] += jnp.sum(dp * value, axis=0, keepdims=True)
        total = dp * weight[3:4, :]
        for k in range(1, 4):
            later = hist[k : k + rows, :] * same[k - 1]
            total = total + later * weight[3 - k : 4 - k, :]
            acc[3 - k : 4 - k, :] += jnp.sum(later * value, axis=0, keepdims=True)
        out[...] = total.astype(BF16)
        hist[rows : rows + 8, :] = hist[0:8, :]
    segs[rows : rows + 8, :] = segs[0:8, :]
    partial = dot_t(dz_s[...], wz_ref[...]) + dot_t(dx_s[...], wx_ref[...])
    partial = partial + dot(ddt_s[...], wdt_s[...]) + dot_t(dbc_s[...], wbc_ref[...])
    for piece in range(PIECES):
        low = partial[piece * CHUNK : (piece + 1) * CHUNK, :].astype(BF16)
        for q in range(2):
            xp_ref[0, 2 * piece + q] = low[q * 64 : q * 64 + 64, :]

        @pl.when(first + block < pairs)
        def _():
            for q in range(2):
                part[block, 2 * piece + q] = low[q * 64 : q * 64 + 64, :]

    x = x_ref[...].astype(F32)
    xr = x * inverse_rms(x)
    a1536[0:1, :] += jnp.sum(partial * xr, axis=0, keepdims=True)
    xn = (xr * ng).astype(BF16)
    for w in range(0, width, 512):
        left = xn[:, w : w + 512]
        acc_z[w : w + 512, :] += tdot(left, dz_s[...])
        acc_x[w : w + 512, :] += tdot(left, dx_s[...])
        for j in range(acc_bc.shape[0]):
            acc_bc[j, w : w + 512, :] += tdot(left, dbc_s[:, j * LANES : (j + 1) * LANES])
        acc_dt[w : w + 512, :] += tdot(left, ddt_s[...])
    @pl.when(block == blocks - 1)
    def _():
        bits = [(acc_z, gz_ref, w) for w in range(0, width, 256)] + [(acc_x, gx_ref, w) for w in range(0, width, 256)]
        copies = []
        for j, (acc, out, w) in enumerate(bits):
            if j >= 2:
                copies[j - 2].wait()
            stage[j % 2] = acc[w : w + 256, :].astype(BF16)
            copies.append(pltpu.make_async_copy(stage.at[j % 2], out.at[pl.ds(w, 256), :], stage_sem.at[j % 2]))
            copies[j].start()
        copies[-2].wait()
        copies[-1].wait()
        for j in range(acc_bc.shape[0]):
            low_bc[:, j * LANES : (j + 1) * LANES] = acc_bc[j].astype(BF16)
        turned = pl.multiple_of(me * dt_rows(width), 8)
        for j in range(width // LANES):
            rest[pl.ds(turned + 16 * j, 16), :] = acc_dt[j * LANES : (j + 1) * LANES, :].T[0:16, :]
        base = count * dt_rows(width)
        for acc in (a1536, a256):
            for j in range(acc.shape[1] // LANES):
                rest[base : base + 8, :] = acc[:, j * LANES : (j + 1) * LANES]
                base += 8
        mine = pl.multiple_of(base + me * slot_rows(inner), 8)
        for j in range(inner // LANES):
            rest[pl.ds(mine + 8 * j, 8), :] = a768[:, j * LANES : (j + 1) * LANES]
        rest[pl.ds(mine + inner // LANES * 8, 8), :] = a128[...]
        first_copy = pltpu.make_async_copy(rest, pack_ref, stage_sem.at[2])
        second_copy = pltpu.make_async_copy(low_bc, gb_ref, stage_sem.at[3])
        first_copy.start()
        second_copy.start()
        first_copy.wait()
        second_copy.wait()
        line.close(carry_out)


def dt_rows(width):
    return width // LANES * 16


def slot_rows(inner):
    return (inner // LANES + 1) * 8


def rows_spec(block, cols, last=None):
    if last is None:
        return pl.BlockSpec((block, cols), lambda i: (i, 0))
    return pl.BlockSpec((block, cols), lambda i: (last - i, 0))


def whole_spec(array):
    return pl.BlockSpec(array.shape, lambda i: (0,) * array.ndim, pipeline_mode=pl.Buffered(1))


def fixed_spec(*dims):
    return pl.BlockSpec(dims, lambda i: (0,) * len(dims))


def on_device(
    x_in, segments, out_grad, norm_gain, w_z, w_x, w_bc, w_dt, conv_x, conv_bc, bias_x, bias_bc,
    dt_bias, a_log, d_skip, out_gain, w_out,
):
    count = lax.axis_size("tensor")
    x, g = x_in[0], out_grad[0]
    length, width = x.shape
    inner = w_x.shape[1]
    heads = w_dt.shape[1]
    bcw = w_bc.shape[1]
    state_n = bcw // 2
    blocks = length // BLOCK
    chunks = length // CHUNK
    last = blocks - 1
    pairs = 2 * blocks
    all_steps = pairs + 2 * count - 3
    n_fwd = (blocks + 4) // 2
    n_bwd = blocks
    rest = all_steps - n_fwd - n_bwd
    wdt = w_dt.T
    per_head = (dt_bias[None, :], a_log[None, :], d_skip[None, :])
    x4 = x.reshape(blocks, 4, BLOCK // 4, width)
    g4 = g.reshape(blocks, 4, BLOCK // 4, width)
    shape = jax.ShapeDtypeStruct
    anywhere = pl.BlockSpec(memory_space=pl.ANY)
    pair_shape = (blocks, 4, BLOCK // 4, width)
    carry_shape = shape((4, BLOCK // 4, width), BF16)
    res_shape = shape(pair_shape, BF16)

    def params(ident):
        return pltpu.CompilerParams(
            vmem_limit_bytes=62 * 2**20, dimension_semantics=("arbitrary",), collective_id=ident, has_side_effects=True
        )

    def cost(flops, moved):
        return pl.CostEstimate(flops=flops, bytes_accessed=moved, transcendentals=0)

    weights = (w_z, w_x, w_bc, wdt, w_out, norm_gain, bias_x, out_gain, bias_bc, conv_x, conv_bc, *per_head)
    z, p, xc, ys, pbc, bc, dtr, dn, st, yp, scal, gout, carry, res_y, res_x = pl.pallas_call(
        functools.partial(forward_kernel, heads, count, pairs, n_fwd, blocks),
        grid=(blocks,),
        in_specs=[
            rows_spec(BLOCK, width),
            rows_spec(BLOCK, width),
            pl.BlockSpec((1, BLOCK), lambda i: (0, i)),
            *[whole_spec(w) for w in weights],
        ],
        out_specs=[
            rows_spec(BLOCK, inner),
            rows_spec(BLOCK, inner),
            rows_spec(BLOCK, inner),
            rows_spec(BLOCK, inner),
            rows_spec(BLOCK, bcw),
            rows_spec(BLOCK, bcw),
            rows_spec(BLOCK, LANES),
            rows_spec(BLOCK, inner),
            pl.BlockSpec((PIECES, state_n, inner), lambda i: (i, 0, 0)),
            pl.BlockSpec((1, 4, BLOCK // 4, width), lambda i: (i, 0, 0, 0)),
            fixed_spec(chunks, 8, CHUNK),
            fixed_spec(2 * inner, width // 2),
            anywhere,
            anywhere,
            anywhere,
        ],
        out_shape=[
            shape((length, inner), F32),
            shape((length, inner), F32),
            shape((length, inner), BF16),
            shape((length, inner), F32),
            shape((length, bcw), F32),
            shape((length, bcw), F32),
            shape((length, LANES), F32),
            shape((length, inner), F32),
            shape((chunks, state_n, inner), BF16),
            shape(pair_shape, BF16),
            shape((chunks, 8, CHUNK), F32),
            shape((2 * inner, width // 2), BF16),
            carry_shape,
            res_shape,
            res_shape,
        ],
        scratch_shapes=[
            pltpu.VMEM((8, LANES), F32),
            pltpu.VMEM((LANES, width), BF16),
            pltpu.VMEM((BLOCK + 8, inner), F32),
            pltpu.VMEM((BLOCK + 8, bcw), F32),
            pltpu.VMEM((BLOCK + 8, 1), F32),
            pltpu.VMEM((state_n, inner), F32),
            pltpu.VMEM((2, BLOCK, inner), F32),
            pltpu.VMEM((2, BLOCK, width), BF16),
            pltpu.VMEM((inner, width), F32),
            pltpu.VMEM((blocks, PIECES, 8, CHUNK), F32),
            pltpu.VMEM((count - 1, blocks, PIECES, 8, CHUNK), F32),
            pltpu.SemaphoreType.DMA((count - 1, blocks)),
            pltpu.SemaphoreType.DMA((count - 1, blocks)),
            pltpu.VMEM((n_fwd, 4, BLOCK // 4, width), BF16),
            *line_scratch(n_fwd, width),
        ],
        compiler_params=params(0),
        cost_estimate=cost(9 * 10**10, 10**8),
        name="forward_scan",
    )(x, g, segments, *weights)

    weights = (w_z, w_x, w_bc, wdt, norm_gain, out_gain, conv_x, conv_bc, *per_head)
    n_in = 13 + len(weights)
    bits = lax.axis_size("dp").bit_length() - 1
    used = (width + bcw) // LANES * 8 + count * (slot_rows(inner) + dt_rows(width))
    pack_rows = -(-used // 256) * 256
    xp, gz, gx, gbc, pack, carry, gout, res_y, res_x = pl.pallas_call(
        functools.partial(backward_kernel, heads, count, pairs, n_fwd, n_bwd),
        grid=(blocks,),
        in_specs=[
            rows_spec(BLOCK, inner, last),
            rows_spec(BLOCK, inner, last),
            rows_spec(BLOCK, inner, last),
            rows_spec(BLOCK, inner, last),
            rows_spec(BLOCK, bcw, last),
            rows_spec(BLOCK, bcw, last),
            rows_spec(BLOCK, LANES, last),
            rows_spec(BLOCK, inner, last),
            pl.BlockSpec((PIECES, state_n, inner), lambda i: (last - i, 0, 0)),
            pl.BlockSpec((1, BLOCK), lambda i: (0, jnp.maximum(last - i - 1, 0))),
            pl.BlockSpec((1, BLOCK), lambda i: (0, last - i)),
            pl.BlockSpec((PIECES, 8, CHUNK), lambda i: (last - i, 0, 0)),
            rows_spec(BLOCK, width, last),
            *[whole_spec(w) for w in weights],
            *[anywhere] * 7,
        ],
        out_specs=[
            pl.BlockSpec((1, 4, BLOCK // 4, width), lambda i: (last - i, 0, 0, 0)),
            *[anywhere] * 8,
        ],
        out_shape=[
            shape(pair_shape, BF16),
            shape((width, inner), BF16),
            shape((width, inner), BF16),
            shape((width, bcw), BF16),
            shape((pack_rows, LANES), F32),
            carry_shape,
            shape((2 * inner, width // 2), BF16),
            res_shape,
            res_shape,
        ],
        scratch_shapes=[
            pltpu.VMEM((8, LANES), F32),
            pltpu.VMEM((LANES, width), BF16),
            pltpu.VMEM((BLOCK + 8, inner), F32),
            pltpu.VMEM((BLOCK + 8, bcw), F32),
            pltpu.VMEM((BLOCK + 8, 1), F32),
            pltpu.VMEM((state_n, inner), F32),
            pltpu.VMEM((BLOCK, inner), BF16),
            pltpu.VMEM((BLOCK, inner), BF16),
            pltpu.VMEM((BLOCK, LANES), BF16),
            pltpu.VMEM((BLOCK, bcw), BF16),
            pltpu.VMEM((width, inner), F32),
            pltpu.VMEM((width, inner), F32),
            pltpu.VMEM((bcw // LANES, width, LANES), F32),
            pltpu.VMEM((width, LANES), F32),
            pltpu.VMEM((8, width), F32),
            pltpu.VMEM((8, inner), F32),
            pltpu.VMEM((8, bcw), F32),
            pltpu.VMEM((8, LANES), F32),
            pltpu.VMEM((pack_rows, LANES), F32),
            pltpu.VMEM((width, bcw), BF16),
            pltpu.VMEM((2, 256, inner), BF16),
            pltpu.SemaphoreType.DMA((4,)),
            pltpu.VMEM((blocks, 4, BLOCK // 4, width), BF16),
            pltpu.SemaphoreType.DMA,
            *finals_scratch(width),
            *cube_scratch(2 * inner, width // 2, bits, BF16),
            *line_scratch(n_bwd, width),
        ],
        input_output_aliases={n_in + 5: 7, n_in + 6: 8},
        compiler_params=params(1),
        cost_estimate=cost(12 * 10**10, 10**8),
        name="backward_scan",
    )(z, p, xc, ys, pbc, bc, dtr, dn, st, segments, segments, scal, x, *weights, yp, x4, g4, carry, gout, res_y, res_x)

    left = pairs - (n_fwd + n_bwd - (count - 1))
    res_y, res_x, gz, gx, gbc, pack = pl.pallas_call(
        functools.partial(line_kernel, count, pairs, n_fwd + n_bwd, rest),
        grid=(rest,),
        in_specs=[anywhere] * 3 + [whole_spec(norm_gain)] + [anywhere] * 7,
        out_specs=[anywhere] * 6,
        out_shape=[
            res_shape,
            res_shape,
            shape((width, inner), BF16),
            shape((width, inner), BF16),
            shape((width, bcw), BF16),
            shape((pack_rows, LANES), F32),
        ],
        scratch_shapes=[
            pltpu.VMEM((left, 4, BLOCK // 4, width), BF16),
            pltpu.SemaphoreType.DMA,
            *finals_scratch(width),
            *cube_scratch(width, inner, bits, BF16),
            *cube_scratch(width, inner, bits, BF16),
            *cube_scratch(width, bcw, bits, BF16),
            *cube_scratch(pack_rows, LANES, bits, F32),
            *cross_scratch(count, width >> bits, bcw, BF16),
            *cross_scratch(count, pack_rows >> bits, LANES, F32),
            *line_scratch(rest, width),
        ],
        input_output_aliases={9: 0, 10: 1},
        compiler_params=params(2),
        cost_estimate=cost(10**11, 3 * 10**8),
        name="line_sums",
    )(xp, x4, g4, norm_gain, carry, gz, gx, gbc, pack, res_y, res_x)

    wide = width // blocks
    tall = inner // blocks
    outs = pl.pallas_call(
        functools.partial(finish_kernel, heads, count),
        grid=(blocks,),
        in_specs=[
            rows_spec(BLOCK, width),
            rows_spec(BLOCK, width),
            rows_spec(BLOCK, width),
            pl.BlockSpec((PIECES, 8, CHUNK), lambda i: (i, 0, 0)),
            rows_spec(wide, inner),
            rows_spec(wide, inner),
            rows_spec(tall, width // 2),
            pl.BlockSpec((tall, width // 2), lambda i: (i + blocks, 0)),
            rows_spec(wide, bcw),
            whole_spec(pack),
        ],
        out_specs=[
            rows_spec(BLOCK, width),
            rows_spec(BLOCK, width),
            rows_spec(wide, inner),
            rows_spec(wide, inner),
            rows_spec(tall, width),
            rows_spec(wide, bcw),
            fixed_spec(heads, width),
            fixed_spec(width),
            fixed_spec(4, inner),
            fixed_spec(inner),
            fixed_spec(inner),
            fixed_spec(1, heads),
            fixed_spec(4, bcw),
            fixed_spec(bcw),
            fixed_spec(1, heads),
            fixed_spec(1, heads),
        ],
        out_shape=[
            shape((length, width), BF16),
            shape((length, width), BF16),
            shape((width, inner), F32),
            shape((width, inner), F32),
            shape((inner, width), F32),
            shape((width, bcw), F32),
            shape((heads, width), F32),
            shape((width,), F32),
            shape((4, inner), F32),
            shape((inner,), F32),
            shape((inner,), F32),
            shape((1, heads), F32),
            shape((4, bcw), F32),
            shape((bcw,), F32),
            shape((1, heads), F32),
            shape((1, heads), F32),
        ],
        compiler_params=pltpu.CompilerParams(vmem_limit_bytes=60 * 2**20, dimension_semantics=("arbitrary",)),
        name="finish",
    )(x, res_y.reshape(length, width), res_x.reshape(length, width), scal, gz, gx, gout, gout, gbc, pack)
    result, grad_x, gz, gx, gout, grad_wbc, grad_wdt, ng, cx, bx, og, ds, cbc, bbc, dtb, al = outs
    return (
        result[None], grad_x[None], ng, gz, gx, grad_wbc, grad_wdt.T, cx, cbc, bx, bbc, dtb[0], al[0], ds[0],
        og, gout,
    )


def solution(mesh):
    tensor_last = P(None, "tensor")
    in_specs = (
        P("dp", None, None), P("dp", None), P("dp", None, None), P(), tensor_last, tensor_last, P(), tensor_last,
        tensor_last, P(), P("tensor"), P(), P("tensor"), P("tensor"), P("tensor"), P("tensor"), P("tensor", None),
    )
    out_specs = (
        P("dp", None, None), P("dp", None, None), P(), tensor_last, tensor_last, P(), tensor_last, tensor_last, P(),
        P("tensor"), P(), P("tensor"), P("tensor"), P("tensor"), P("tensor"), P("tensor", None),
    )
    return jax.shard_map(on_device, mesh=mesh, in_specs=in_specs, out_specs=out_specs, check_vma=False)
```

```python
import functools

import jax
import jax.numpy as jnp
from jax import lax
from jax.experimental import pallas as pl
from jax.experimental.pallas import tpu as pltpu
from jax.sharding import PartitionSpec as P

EPS = 1e-05
CHUNK = 128
BLOCK = 256
PIECES = BLOCK // CHUNK
LANES = 128
ROWS = CHUNK // 2
LAG = 2
RING = 4
F32 = jnp.float32
BF16 = jnp.bfloat16
HIGHEST = lax.Precision.HIGHEST
MESH = pl.DeviceIdType.MESH


def dot(a, b, precision=None):
    return lax.dot_general(a, b, (((1,), (0,)), ((), ())), precision=precision, preferred_element_type=F32)


def dot_t(a, b):
    return lax.dot_general(a, b, (((1,), (1,)), ((), ())), preferred_element_type=F32)


def tdot(a, b):
    return lax.dot_general(a, b, (((0,), (0,)), ((), ())), preferred_element_type=F32)


def sigmoid(v):
    return 1.0 / (1.0 + jnp.exp(-v))


def softplus(v):
    e = jnp.exp(-jnp.abs(v))
    series = e * (1.0 - e * (0.5 - e * (1.0 / 3.0 - e * 0.25)))
    return jnp.maximum(v, 0.0) + jnp.where(e < 0.03, series, jnp.log(1.0 + e))


def iotas(rows, cols):
    return (
        lax.broadcasted_iota(jnp.int32, (rows, cols), 0),
        lax.broadcasted_iota(jnp.int32, (rows, cols), 1),
    )


def fill_expand(expand, heads):
    r, c = iotas(*expand.shape)
    expand[...] = (lax.rem(r, LANES) == c // (expand.shape[1] // heads)).astype(BF16)


def spread(columns, expand):
    high = columns.astype(BF16)
    low = (columns - high.astype(F32)).astype(BF16)
    return dot(jnp.concatenate([high, low], axis=1), expand[...])


def decays(la, seg_col, seg_row):
    r, c = iotas(CHUNK, CHUNK)
    cum = dot((r >= c).astype(F32), la, HIGHEST)
    visible = (r >= c) & (seg_col == seg_row)
    return cum, cum.T, visible


def decay_matrix(cum, cum_t, visible, head):
    gap = cum[:, head : head + 1] - cum_t[head : head + 1, :]
    return jnp.exp(jnp.where(visible, gap, -1e30))


def split_pair(values):
    low = lax.broadcasted_iota(jnp.int32, values.shape, 1) < LANES // 2
    zero = jnp.zeros_like(values)
    return jnp.where(low, values, zero), jnp.where(low, zero, values)


def conv_taps(hist, weight, same, rows):
    out = hist[8 : 8 + rows, :] * weight[3:4, :]
    for k in range(1, 4):
        out = out + hist[8 - k : 8 - k + rows, :] * same[k - 1] * weight[3 - k : 4 - k, :]
    return out


def columns_of(segr_ref):
    rows = segr_ref.shape[1]
    pieces = []
    for at in range(0, rows, LANES):
        row = segr_ref[:, at : at + LANES].astype(F32)
        pieces.append(jnp.broadcast_to(row, (LANES, LANES)).T[:, 0:1])
    return jnp.concatenate(pieces, axis=0)


def fill_heads(hv, wdt_s, dtb_ref, al_ref, dsk_ref, wdt_ref):
    heads = wdt_ref.shape[0]
    hv[...] = jnp.zeros_like(hv)
    for j, ref in enumerate((dtb_ref, al_ref, dsk_ref)):
        hv[j : j + 1, 0:heads] = ref[...]
    wdt_s[...] = jnp.zeros_like(wdt_s)
    wdt_s[0:heads, :] = wdt_ref[...]


def row_of(ref):
    return ref[...].reshape(1, ref.shape[0])


def inverse_rms(tokens):
    return lax.rsqrt(jnp.sum(tokens * tokens, axis=1, keepdims=True) * (1.0 / tokens.shape[1]) + EPS)


def bring(src, dst, sem):
    copy = pltpu.make_async_copy(src, dst, sem)
    copy.start()
    copy.wait()


def hello(peers, dp_peers=()):
    barrier = pltpu.get_barrier_semaphore()
    for peer in dp_peers:
        pl.semaphore_signal(barrier, inc=1, device_id={"dp": peer}, device_id_type=MESH)
    for peer, there in peers:

        @pl.when(there)
        def _():
            pl.semaphore_signal(barrier, inc=1, device_id={"tensor": peer}, device_id_type=MESH)


def heard(peers, dp_peers=()):
    total = jnp.int32(len(dp_peers))
    for _, there in peers:
        total = total + there.astype(jnp.int32)
    pl.semaphore_wait(pltpu.get_barrier_semaphore(), total)


def neighbours(count):
    me = lax.axis_index("tensor")
    return [(me - 1, me > 0), (me + 1, me < count - 1)]


class Line:
    def __init__(self, count, pairs, first, steps, refs, source, finals=None):
        self.count, self.pairs, self.first, self.steps = count, pairs, first, steps
        self.source, self.finals = source, finals
        (self.res_y, self.res_x, self.land, self.send) = refs[:4]
        (self.red_out, self.red_in, self.bc_out, self.bc_in, self.local) = refs[4:]

    def to_result(self, k, q, act):
        half = self.pairs // 2

        @pl.when(k < half)
        def _():
            act(self.res_y.at[k, q])

        @pl.when(k >= half)
        def _():
            act(self.res_x.at[2 * half - 1 - k, q])

    def flow(self, q):
        me = lax.axis_index("tensor")
        if q == 0:
            return me, me - 1, me + 1
        return self.count - 1 - me, me + 1, me - 1

    def is_pair(self, i):
        return (i >= 0) & (i < self.pairs)

    def red(self, q, ls, toward, src):
        return pltpu.make_async_remote_copy(
            src_ref=src, dst_ref=self.land.at[ls + LAG, q], send_sem=self.red_out.at[q, ls],
            recv_sem=self.red_in.at[q, ls], device_id={"tensor": toward}, device_id_type=MESH,
        )

    def cast(self, q, ls, away, src, there):
        return pltpu.make_async_remote_copy(
            src_ref=src, dst_ref=there, send_sem=self.bc_out.at[q, ls],
            recv_sem=self.bc_in.at[q, ls], device_id={"tensor": away}, device_id_type=MESH,
        )

    def hold(self, q, ls):
        return self.send.at[lax.rem(ls, LAG), q]

    def keep(self, q, ls, there):
        return pltpu.make_async_copy(self.hold(q, ls), there, self.local.at[lax.rem(ls, LAG), q])

    def term(self, s, z):
        return s - LAG * (self.count - 1 - z)

    def back(self, s, z):
        return s - LAG * (self.count - 1 + z)

    def finish_red(self, q, s, ls):
        z, toward, away = self.flow(q)
        n = self.count
        i = self.term(s, z)

        @pl.when(self.is_pair(i) & (z > 0))
        def _():
            self.red(q, ls, toward, self.hold(q, ls)).wait_send()

        @pl.when(self.is_pair(i) & (z == 0))
        def _():
            self.cast(q, ls, away, self.hold(q, ls), self.res_y.at[0, q]).wait_send()
            self.keep(q, ls, self.res_y.at[0, q]).wait()

        @pl.when(self.is_pair(i + LAG) & (z < n - 1))
        def _():
            self.red(q, ls, toward, self.hold(q, ls)).wait_recv()

    def finish_cast(self, q, s, ls):
        z, _, away = self.flow(q)
        n = self.count
        k = self.back(s, z)

        @pl.when(self.is_pair(k) & (z > 0) & (z < n - 1))
        def _():
            self.cast(q, ls, away, self.res_y.at[0, q], self.res_y.at[0, q]).wait_send()

        @pl.when(self.is_pair(k + LAG) & (z > 0))
        def _():
            self.cast(q, ls, away, self.res_y.at[0, q], self.res_y.at[0, q]).wait_recv()

    def step(self, ls):
        n = self.count
        ls = jnp.int32(ls)
        s = self.first + ls
        for q in range(2):

            @pl.when(ls >= LAG)
            def _():
                self.finish_cast(q, s - LAG, ls - LAG)

            z, toward, away = self.flow(q)
            k = self.back(s, z)

            @pl.when(self.is_pair(k) & (z > 0) & (z < n - 1))
            def _():
                self.to_result(k, q, lambda there: self.cast(q, ls, away, there, there).start())

        for q in range(2):
            z, toward, away = self.flow(q)
            i = self.term(s, z)

            @pl.when(ls >= LAG)
            def _():
                self.finish_red(q, s - LAG, ls - LAG)

            @pl.when(self.is_pair(i))
            def _():
                mine = self.source(q, i)
                place = lax.rem(ls, LAG)

                @pl.when(z == n - 1)
                def _():
                    self.red(q, ls, toward, mine).start()

                @pl.when((z > 0) & (z < n - 1))
                def _():
                    self.send[place, q] = (mine[...].astype(F32) + self.land[ls, q].astype(F32)).astype(BF16)
                    self.red(q, ls, toward, self.hold(q, ls)).start()

                @pl.when(z == 0)
                def _():
                    total = mine[...].astype(F32) + self.land[ls, q].astype(F32)
                    if self.finals is None:
                        self.send[place, q] = total.astype(BF16)
                    else:
                        self.finals.last(q, i, total, self.hold(q, ls))

                    def give(there):
                        self.cast(q, ls, away, self.hold(q, ls), there).start()
                        self.keep(q, ls, there).start()

                    self.to_result(i, q, give)
                    if self.finals is not None:

                        @pl.when(ls + 1 < self.steps)
                        def _():
                            self.finals.fetch(q, i + 1)

    def held(self, q, s):
        z, _, _ = self.flow(q)
        return self.is_pair(self.term(s, z)) & (z < self.count - 1)

    def each_held(self, s, src, act):
        for q in range(2):
            for d in range(LAG):

                @pl.when(self.held(q, s + d))
                def _():
                    act(pltpu.make_async_copy(*src(d, q), self.local.at[d, q]))

    def open(self, carry):
        self.each_held(self.first, lambda d, q: (carry.at[d, q], self.land.at[d, q]), lambda copy: copy.start())
        for q in range(2):
            z, _, _ = self.flow(q)

            @pl.when(z == 0)
            def _():
                self.finals.fetch(q, jnp.int32(self.first - LAG * (self.count - 1)))

    def opened(self, carry):
        self.each_held(self.first, lambda d, q: (carry.at[d, q], self.land.at[d, q]), lambda copy: copy.wait())

    def close(self, carry):
        for d in range(LAG):
            ls = self.steps - LAG + d
            for q in range(2):
                self.finish_cast(q, self.first + ls, jnp.int32(ls))
                self.finish_red(q, self.first + ls, jnp.int32(ls))
        if carry is None:
            return
        left = (self.first + self.steps, lambda d, q: (self.land.at[self.steps + d, q], carry.at[d, q]))
        self.each_held(*left, lambda copy: copy.start())
        self.each_held(*left, lambda copy: copy.wait())


def line_scratch(steps, width):
    return [
        pltpu.VMEM((steps + LAG, 2, ROWS, width), BF16),
        pltpu.VMEM((LAG, 2, ROWS, width), BF16),
        pltpu.SemaphoreType.DMA((2, steps)),
        pltpu.SemaphoreType.DMA((2, steps)),
        pltpu.SemaphoreType.DMA((2, steps)),
        pltpu.SemaphoreType.DMA((2, steps)),
        pltpu.SemaphoreType.DMA((LAG, 2)),
    ]


class Finals:
    def __init__(self, pairs, x_any, g_any, gain, rows, sems):
        self.pairs, self.half, self.x_any, self.g_any, self.gain, self.rows, self.sems = (
            pairs, pairs // 2, x_any, g_any, gain, rows, sems,
        )

    def copies(self, q, i):
        b = 2 * self.half - 1 - i
        return [
            pltpu.make_async_copy(src.at[b, q], self.rows.at[q, j], self.sems.at[q, j])
            for j, src in enumerate((self.x_any, self.g_any))
        ]

    def fetch(self, q, i):
        @pl.when((i >= self.half) & (i < self.pairs))
        def _():
            for copy in self.copies(q, i):
                copy.start()

    def last(self, q, i, total, out):
        @pl.when(i < self.half)
        def _():
            out[...] = total.astype(BF16)

        @pl.when(i >= self.half)
        def _():
            for copy in self.copies(q, i):
                copy.wait()
            x = self.rows[q, 0].astype(F32)
            r1 = inverse_rms(x)
            scaled = total * self.gain
            across = jnp.sum(scaled * x, axis=1, keepdims=True) * (1.0 / x.shape[1])
            out[...] = (self.rows[q, 1].astype(F32) + r1 * scaled - x * (r1 * r1 * r1 * across)).astype(BF16)


def finals_scratch(width):
    return [pltpu.VMEM((2, 2, ROWS, width), BF16), pltpu.SemaphoreType.DMA((2, 2))]


def dp_bits():
    me = lax.axis_index("dp")
    bits = []
    for b in range(lax.axis_size("dp").bit_length() - 1):
        bit = lax.rem(me // 2**b, 2)
        bits.append((bit, me + (1 - 2 * bit) * 2**b))
    return bits


class Cube:
    def __init__(self, order, refs, across=None):
        self.order, self.across = order, across
        (self.src, self.out, self.total, self.send, self.land, self.out_sem, self.in_sem, self.local) = refs
        self.rows = self.src.shape[0]
        self.bits = dp_bits()
        self.events = 2 * len(order) + (1 if across is None else 2)

    def start_of(self, depth):
        at = 0
        for j in range(depth):
            at = at + self.bits[self.order[j]][0] * (self.rows >> (j + 1))
        return at

    def span(self, at, size):
        return pl.ds(pl.multiple_of(at, 8 if self.src.dtype == F32 else 16), size)

    def inside(self, depth):
        return self.start_of(depth) - self.start_of(1)

    def own_half(self):
        mine = self.src.at[self.span(self.start_of(1), self.rows // 2), :]
        return pltpu.make_async_copy(mine, self.send.at[pl.ds(0, self.rows // 2), :], self.local)

    def halving(self, j):
        size = self.rows >> (j + 1)
        bit, partner = self.bits[self.order[j]]
        theirs = self.start_of(j) + (1 - bit) * size
        src = self.src.at[self.span(theirs, size), :] if j == 0 else self.send.at[pl.ds(0, size), :]
        return pltpu.make_async_remote_copy(
            src_ref=src, dst_ref=self.land.at[pl.ds(self.rows - 2 * size, size), :], send_sem=self.out_sem.at[j],
            recv_sem=self.in_sem.at[j], device_id={"dp": partner}, device_id_type=MESH,
        )

    def doubling(self, j):
        count = len(self.order)
        size = self.rows >> (count - j)
        _, partner = self.bits[self.order[count - 1 - j]]
        mine = self.out.at[self.span(self.start_of(count - j), size), :]
        return pltpu.make_async_remote_copy(
            src_ref=mine, dst_ref=mine, send_sem=self.out_sem.at[count + j], recv_sem=self.in_sem.at[count + j],
            device_id={"dp": partner}, device_id_type=MESH,
        )

    def crossing(self, d):
        mine, land, out_sem, in_sem, peers = self.across
        return pltpu.make_async_remote_copy(
            src_ref=mine, dst_ref=land.at[d - 1], send_sem=out_sem.at[d - 1],
            recv_sem=in_sem.at[d - 1], device_id={"tensor": peers[d - 1]}, device_id_type=MESH,
        )

    def turn(self, part):
        count = len(self.order)
        size = self.rows >> count
        bring(part, self.out.at[self.span(self.start_of(count), size), :], self.local)
        self.doubling(0).start()

    def event(self, e):
        count = len(self.order)
        if e == 0:
            self.halving(0).start()
            self.own_half().start()
            return
        if e <= count:
            if e == 1:
                self.own_half().wait()
            self.halving(e - 1).wait()
            size = self.rows >> e
            at = self.inside(e)
            for r in range(0, size, 192):
                tile = min(192, size - r)
                landed = self.land[self.rows - 2 * size + r : self.rows - 2 * size + r + tile, :].astype(F32)
                here = self.span(at + r, tile)
                if e == 1:
                    self.total[here, :] = self.send[r : r + tile, :].astype(F32) + landed
                else:
                    self.total[here, :] = self.total[here, :] + landed
            if e < count:
                bit, _ = self.bits[self.order[e]]
                at = at + (1 - bit) * (size // 2)
                size = size // 2
            part = self.total[self.span(at, size), :]
            if e == count and self.across is not None:
                self.across[0][...] = part.astype(self.across[0].dtype)
                for d in range(1, len(self.across[4]) + 1):
                    self.crossing(d).start()
                return
            self.send[0:size, :] = part.astype(self.send.dtype)
            if e < count:
                self.halving(e).start()
            else:
                self.turn(self.send.at[pl.ds(0, size), :])
            return
        if self.across is not None:
            if e == count + 1:
                size = self.rows >> count
                total = self.total[self.span(self.inside(count), size), :]
                for d in range(1, len(self.across[4]) + 1):
                    self.crossing(d).wait()
                    total = total + self.across[1][d - 1].astype(F32)
                self.across[0][...] = total.astype(self.across[0].dtype)
                self.turn(self.across[0])
                return
            e = e - 1
        self.doubling(e - count - 1).wait()
        if e < 2 * count:
            self.doubling(e - count).start()


def cube_scratch(rows, cols, bits, dtype):
    return [
        pltpu.VMEM((rows // 2, cols), F32),
        pltpu.VMEM((rows // 2, cols), dtype),
        pltpu.VMEM((rows - (rows >> bits), cols), dtype),
        pltpu.SemaphoreType.DMA((2 * bits,)),
        pltpu.SemaphoreType.DMA((2 * bits,)),
        pltpu.SemaphoreType.DMA,
    ]


def cross_scratch(count, rows, cols, dtype):
    return [
        pltpu.VMEM((rows, cols), dtype),
        pltpu.VMEM((count - 1, rows, cols), dtype),
        pltpu.SemaphoreType.DMA((count - 1,)),
        pltpu.SemaphoreType.DMA((count - 1,)),
    ]


def tensor_peers(count):
    me = lax.axis_index("tensor")
    return [lax.rem(me + d, count) for d in range(1, count)]


def line_kernel(
    count, pairs, first, steps, xp_ref, x_any, g_any, ng_ref, carry_ref, gz_ref, gx_ref, gb_ref, pk_ref, sh_ref, res_y_in, res_x_in,
    res_y, res_x, oz_ref, ox_ref, ob_ref, op_ref, os_ref, part, part_sem, rows, sems, *scratch,
):
    del res_y_in, res_x_in
    half = pairs // 2
    order = list(range(len(dp_bits())))
    other = order[:1] + order[:0:-1]
    peers = tensor_peers(count)
    cubes = [
        Cube(order, (gz_ref, oz_ref, *scratch[0:6])),
        Cube(other, (gx_ref, ox_ref, *scratch[6:12])),
        Cube(other, (gb_ref, ob_ref, *scratch[12:18]), (*scratch[30:34], peers)),
        Cube(order, (pk_ref, op_ref, *scratch[18:24])),
        Cube(order, (sh_ref, os_ref, *scratch[24:30]), (*scratch[34:38], peers)),
    ]
    finals = Finals(pairs, x_any, g_any, row_of(ng_ref), rows, sems)
    line = Line(
        count, pairs, first, steps, (res_y, res_x, *scratch[38:]), lambda q, i: part.at[2 * half - 1 - i, q], finals
    )
    at = pl.program_id(0)

    @pl.when(at == 0)
    def _():
        terms = pltpu.make_async_copy(xp_ref.at[pl.ds(0, part.shape[0])], part, part_sem)
        everyone = [(peer, peer >= 0) for peer in peers], [partner for _, partner in dp_bits()]
        hello(*everyone)
        terms.start()
        line.open(carry_ref)
        line.opened(carry_ref)
        terms.wait()
        heard(*everyone)

    if len(order) == 3:
        times = [0, 1, 4, 5, 6, 9, 10], [0, 1, 4, 5, 6, 9, 10], [0, 1, 4, 6, 8, 10, 11, 11]
    else:
        times = (range(2 * len(order) + 2),) * 3
    for cube, when in zip(cubes, (*times, times[0], times[2])):
        for e in range(cube.events):

            @pl.when(at == min(when[e], steps - 1))
            def _():
                cube.event(e)

    line.step(at)

    @pl.when(at == steps - 1)
    def _():
        line.close(None)


def finish_kernel(
    heads, x_ref, y_ref, dx_ref, scal_ref, gz_ref, gx_ref, go_ref, go2_ref, gb_ref, pack_ref, shared_ref,
    yo_ref, xo_ref, oz_ref, ox_ref, oo_ref, wbc_ref, wdt_ref, ng_ref, cx_ref, bx_ref, og_ref, ds_ref, cbc_ref, bbc_ref,
    dtb_ref, al_ref,
):
    inner = cx_ref.shape[1]
    width, bcw = x_ref.shape[1], wbc_ref.shape[1]
    for piece in range(x_ref.shape[0] // CHUNK):
        span = slice(piece * CHUNK, (piece + 1) * CHUNK)
        r2 = jnp.concatenate([scal_ref[piece], jnp.zeros((CHUNK - 8, CHUNK), F32)], axis=0).T[:, 0:1]
        yo_ref[span, :] = (x_ref[span, :].astype(F32) + r2 * y_ref[span, :].astype(F32)).astype(BF16)
    xo_ref[...] = dx_ref[...]
    oz_ref[...] = gz_ref[...].astype(F32)
    ox_ref[...] = gx_ref[...].astype(F32)
    oo_ref[:, 0 : width // 2] = go_ref[...].astype(F32)
    oo_ref[:, width // 2 :] = go2_ref[...].astype(F32)
    wbc_ref[...] = gb_ref[...].astype(F32)

    @pl.when(pl.program_id(0) == 0)
    def _():
        for j in range(width // LANES):
            wdt_ref[:, j * LANES : (j + 1) * LANES] = pack_ref[16 * j : 16 * j + 16, :][0:heads, :]

        def put(ref, row):
            ref[...] = row.reshape(ref.shape)

        def side_by_side(ref, at, pieces, rows=8):
            return jnp.concatenate([ref[at + 8 * j : at + 8 * j + rows, :] for j in range(pieces)], axis=1)

        put(ng_ref, side_by_side(shared_ref, 0, width // LANES, 1))
        rows = side_by_side(shared_ref, width // LANES * 8, bcw // LANES)
        cbc_ref[...] = rows[0:4, :]
        put(bbc_ref, rows[4:5, :])
        rows = side_by_side(pack_ref, dt_rows(width), inner // LANES)
        cx_ref[...] = rows[0:4, :]
        put(bx_ref, rows[4:5, :])
        put(og_ref, rows[6:7, :])
        lane = lax.broadcasted_iota(jnp.int32, (1, heads), 1)
        skip = jnp.zeros((1, heads), F32)
        for h in range(heads):
            head = jnp.sum(rows[5:6, h * 64 : h * 64 + 64], axis=1, keepdims=True)
            skip = jnp.where(lane == h, head, skip)
        ds_ref[...] = skip
        at = dt_rows(width) + inner // LANES * 8
        rows = pack_ref[at : at + 8, :]
        dtb_ref[...] = rows[0:1, 0:heads]
        al_ref[...] = rows[1:2, 0:heads]


def forward_kernel(
    heads, count, pairs, steps, blocks,
    x_ref, g_ref, segr_ref, wz_ref, wx_ref, wbc_ref, wdt_ref, wo_any, ng_ref, bx_ref, og_ref, bbc_ref, cx_ref, cbc_ref,
    dtb_ref, al_ref, dsk_ref,
    z_ref, p_ref, xc_ref, ys_ref, pbc_ref, bc_ref, dtr_ref, dn_ref, st_ref, yp_ref, scal_ref, wout_ref,
    carry_out, res_y, res_x,
    wo_ref, w_sem, hv_ref, wdt_s, expand, hist, hist_bc, segs, state, scaled_s, g_s, acc_out, stat_mine, stat_land, stat_out, stat_in, part, *scratch,
):
    rows, width = x_ref.shape
    inner = z_ref.shape[1]
    block = pl.program_id(0)
    me = lax.axis_index("tensor")
    ng, bx, og, bbc = row_of(ng_ref), row_of(bx_ref), row_of(og_ref), row_of(bbc_ref)

    line = Line(count, pairs, 0, steps, (res_y, res_x, *scratch), lambda q, i: part.at[i, q])

    load = pltpu.make_async_copy(wo_any, wo_ref, w_sem)
    everyone = [(peer, peer >= 0) for peer in tensor_peers(count)]

    @pl.when(block == 0)
    def _():
        hello(everyone)
        load.start()
        fill_heads(hv_ref, wdt_s, dtb_ref, al_ref, dsk_ref, wdt_ref)
        fill_expand(expand, heads)
        hist[0:8, :] = jnp.zeros((8, hist.shape[1]), F32)
        hist_bc[0:8, :] = jnp.zeros((8, hist_bc.shape[1]), F32)
        segs[0:8, :] = jnp.full((8, 1), -1.0, F32)
        state[...] = jnp.zeros_like(state)
        acc_out[...] = jnp.zeros_like(acc_out)

    x = x_ref[...].astype(F32)
    xn = (x * inverse_rms(x) * ng).astype(BF16)
    z_ref[...] = dot(xn, wz_ref[...])
    xc = dot(xn, wx_ref[...])
    bc = dot(xn, wbc_ref[...])
    dtr = dot_t(xn, wdt_s[...])
    xc_ref[...] = xc.astype(BF16)
    bc_ref[...] = bc
    dtr_ref[...] = dtr
    seg_all = columns_of(segr_ref)
    segs[8 : 8 + rows, :] = seg_all
    hist[8 : 8 + rows, :] = xc
    hist_bc[8 : 8 + rows, :] = bc
    same = [(segs[8 - k : 8 - k + rows, :] == seg_all).astype(F32) for k in range(1, 4)]
    p_ref[...] = conv_taps(hist, cx_ref, same, rows) + bx
    pbc_ref[...] = conv_taps(hist_bc, cbc_ref, same, rows) + bbc
    g = g_ref[...]
    g_s[lax.rem(block, RING)] = g
    dt_all = softplus(dtr + hv_ref[0:1, :])
    la_all = -jnp.exp(hv_ref[1:2, :]) * dt_all
    dsk = spread(hv_ref[...], expand)[2:3, :]
    row_i, lane_i = iotas(CHUNK, LANES)
    squares = []
    for piece in range(PIECES):
        at = pl.ds(piece * CHUNK, CHUNK)
        span = slice(piece * CHUNK, (piece + 1) * CHUNK)
        seg_col = seg_all[span, :]
        keep = (seg_col == segs[7 + piece * CHUNK : 8 + piece * CHUNK, :]).astype(F32)
        tail = (seg_col == seg_col[CHUNK - 1 : CHUNK, :]).astype(F32)
        dt = dt_all[span, :]
        cum, cum_t, visible = decays(la_all[span, :], seg_col, segr_ref[:, span].astype(F32))
        p = p_ref[at, :]
        u = p * sigmoid(p)
        pbc = pbc_ref[at, :]
        bcu = (pbc * sigmoid(pbc)).astype(BF16)
        n = bcu.shape[1] // 2
        b, c = bcu[:, :n], bcu[:, n:]
        scores = dot_t(c, b)
        last = cum[CHUNK - 1 : CHUNK, :]
        flows = [dt, jnp.exp(cum) * keep, jnp.exp(last - cum) * tail]
        flows.append(jnp.broadcast_to(jnp.exp(last) * keep[CHUNK - 1 : CHUNK, :], (8, LANES)))
        wide = spread(jnp.concatenate(flows, axis=0), expand)
        dt_x, enter_x, end_x = (wide[k * CHUNK : (k + 1) * CHUNK, :] for k in range(3))
        carry = wide[3 * CHUNK : 3 * CHUNK + 1, :]
        v = dt_x * u
        v_low = v.astype(BF16)
        pieces = []
        for pair in range(heads // 2):
            mats = [
                (scores * decay_matrix(cum, cum_t, visible, 2 * pair + k)).astype(BF16)
                for k in range(2)
            ]
            halves = split_pair(v_low[:, pair * LANES : (pair + 1) * LANES])
            pieces.append(dot(jnp.concatenate(mats, axis=1), jnp.concatenate(halves, axis=0)))
        inside = jnp.concatenate(pieces, axis=1)
        old = state[...]
        old_low = old.astype(BF16)
        st_ref[piece] = old_low
        entering = dot(c, old_low) * enter_x
        state[...] = old * carry + tdot(b, (end_x * v).astype(BF16))
        ys = inside + entering + dsk * u
        ys_ref[at, :] = ys
        z = z_ref[at, :]
        gated = ys * (z * sigmoid(z))
        scaled = gated * og
        scaled_s[lax.rem(block, RING), at, :] = scaled
        if piece == 0:

            @pl.when(block == 0)
            def _():
                heard(everyone)
                load.wait()

        y_part = dot(scaled.astype(BF16), wo_ref[...]).astype(BF16)
        for q in range(2):
            yp_ref[piece, q] = y_part[q * ROWS : q * ROWS + ROWS, :]

        @pl.when(block * PIECES + piece < part.shape[0])
        def _():
            for q in range(2):
                at_pair = jnp.minimum(block * PIECES + piece, part.shape[0] - 1)
                part[at_pair, q] = y_part[q * ROWS : q * ROWS + ROWS, :]

        if piece == 0:
            line.step(jnp.where(block < 4, 2 * block, block + 3))
        else:

            @pl.when((block < 3) | (block == blocks - 1))
            def _():
                line.step(jnp.where(block < 3, 2 * block + 1, steps - 1))

        squares.append(jnp.sum(gated * gated, axis=1, keepdims=True))

    dn = dot_t(g, wo_ref[...])
    dn_ref[...] = dn
    for piece in range(PIECES):
        span = slice(piece * CHUNK, (piece + 1) * CHUNK)
        across = jnp.sum(dn[span, :] * scaled_s[lax.rem(block, RING), span, :], axis=1, keepdims=True)
        both = jnp.where(lane_i == 0, squares[piece], jnp.where(lane_i == 1, across, 0.0))
        stat_mine[block, piece] = both.T[0:8, :]
    hist[0:8, :] = hist[rows : rows + 8, :]
    hist_bc[0:8, :] = hist_bc[rows : rows + 8, :]
    segs[0:8, :] = segs[rows : rows + 8, :]

    def stat_copy(d, b):
        return pltpu.make_async_remote_copy(
            src_ref=stat_mine.at[b], dst_ref=stat_land.at[d - 1, b], send_sem=stat_out.at[d - 1, b],
            recv_sem=stat_in.at[d - 1, b], device_id={"tensor": lax.rem(me + d, count)}, device_id_type=MESH,
        )

    def settle(b):
        total = stat_mine[b]
        for d in range(1, count):
            stat_copy(d, b).wait()
            total = total + stat_land[d - 1, b]
        place = lax.rem(b, RING)
        low = []
        for piece in range(PIECES):
            r2 = lax.rsqrt(total[piece, 0:1, :] * (1.0 / (inner * count)) + EPS)
            k2 = r2 * r2 * r2 * (total[piece, 1:2, :] * (1.0 / (inner * count)))
            both = jnp.where(row_i == 0, r2, jnp.where(row_i == 1, k2, 0.0))
            scal_ref[b * PIECES + piece] = both[0:8, :]
            low.append((scaled_s[place, piece * CHUNK : (piece + 1) * CHUNK, :] * both.T[:, 0:1]).astype(BF16))
        normed = jnp.concatenate(low, axis=0)
        up = g_s[place]
        for c in range(0, inner, 256):
            acc_out[c : c + 256, :] += tdot(normed[:, c : c + 256], up)

    for d in range(1, count):
        stat_copy(d, block).start()

    @pl.when(block >= RING - 1)
    def _():
        settle(block - (RING - 1))

    @pl.when(block == blocks - 1)
    def _():
        for b in range(1, RING):
            settle(blocks - RING + b)
        for c in range(0, inner, 256):
            low = acc_out[c : c + 256, :].astype(BF16)
            wout_ref[c : c + 256, :] = low[:, 0 : width // 2]
            wout_ref[inner + c : inner + c + 256, :] = low[:, width // 2 :]
        line.close(carry_out)


def backward_kernel(
    heads, count, pairs, first, steps,
    z_ref, p_ref, xc_ref, ys_ref, pbc_ref, bc_ref, dtr_ref, dn_ref, st_ref, segp_ref, segr_ref, scal_ref, x_ref,
    wz_any, wx_any, wbc_any, wdt_ref, ng_ref, og_ref, cx_ref, cbc_ref, dtb_ref, al_ref, dsk_ref, y_ref, x_any, g_any, carry_ref, go_ref, res_y_in, res_x_in,
    xp_ref, gz_ref, gx_ref, gb_ref, pack_ref, shared_ref, carry_out, go_sum, res_y, res_x,
    wz_ref, wx_ref, wbc_ref, w_sem, hv_ref, wdt_s, expand, ahead, ahead_bc, segs, d_state, dz_s, dx_s, ddt_s, dbc_s, acc_z, acc_x, acc_bc, acc_dt,
    a1536, a768, a256, a128, rest, shared, stage, stage_sem, part, part_sem, rows_s, rows_sem, *scratch,
):
    del res_y_in, res_x_in
    rows, inner = z_ref.shape
    width = x_ref.shape[1]
    block = pl.program_id(0)
    blocks = steps // PIECES - 1
    half = pairs // 2
    me = lax.axis_index("tensor")
    ng, og = row_of(ng_ref), row_of(og_ref)

    finals = Finals(pairs, x_any, g_any, ng, rows_s, rows_sem)
    line = Line(
        count, pairs, first, steps, (res_y, res_x, *scratch[6:]), lambda q, i: part.at[lax.rem(i, half), q], finals
    )
    loads = [
        pltpu.make_async_copy(src, dst, w_sem.at[j])
        for j, (src, dst) in enumerate(((wz_any, wz_ref), (wx_any, wx_ref), (wbc_any, wbc_ref)))
    ]
    cube = Cube(list(range(len(dp_bits()))), (go_ref, go_sum, *scratch[0:6]))
    old = first - LAG * (count - 1)

    @pl.when(block == 0)
    def _():
        terms = pltpu.make_async_copy(y_ref.at[pl.ds(old, half - old)], part.at[pl.ds(old, half - old)], part_sem)
        everyone = neighbours(count), [partner for _, partner in dp_bits()]
        hello(*everyone)
        terms.start()
        line.open(carry_ref)
        for load in loads:
            load.start()
        line.opened(carry_ref)
        terms.wait()
        heard(*everyone)
        line.step(0)
        fill_heads(hv_ref, wdt_s, dtb_ref, al_ref, dsk_ref, wdt_ref)
        fill_expand(expand, heads)
        ahead[rows : rows + 8, :] = jnp.zeros((8, ahead.shape[1]), F32)
        ahead_bc[rows : rows + 8, :] = jnp.zeros((8, ahead_bc.shape[1]), F32)
        segs[rows : rows + 8, :] = jnp.full((8, 1), -1.0, F32)
        for ref in (d_state, acc_z, acc_x, acc_bc, acc_dt, a1536, a768, a256, a128, rest, shared):
            ref[...] = jnp.zeros_like(ref)

    @pl.when(block > 0)
    def _():
        line.step(2 * block + 1)

    seg_all = columns_of(segr_ref)
    segs[0:rows, :] = seg_all
    before = jnp.where(block == blocks - 1, -1.0, segp_ref[:, rows - 1 : rows].astype(F32))
    r, c_ = iotas(CHUNK, CHUNK)
    both_ways = jnp.concatenate([(r <= c_).astype(F32), (r > c_).astype(F32)], axis=1)
    all_r, all_l = iotas(heads * CHUNK, LANES)
    pick = (all_r // CHUNK == all_l).astype(BF16)
    decay_rate = -jnp.exp(hv_ref[1:2, :])
    dsk = spread(hv_ref[...], expand)[2:3, :]
    for piece in reversed(range(PIECES)):
        at = pl.ds(piece * CHUNK, CHUNK)
        span = slice(piece * CHUNK, (piece + 1) * CHUNK)
        seg_col = seg_all[span, :]
        prev = seg_all[piece * CHUNK - 1 : piece * CHUNK, :] if piece else before
        keep = (seg_col == prev).astype(F32)
        tail = (seg_col == seg_col[CHUNK - 1 : CHUNK, :]).astype(F32)
        scal = jnp.concatenate([scal_ref[piece], jnp.zeros((CHUNK - 8, CHUNK), F32)], axis=0).T
        r2 = scal[:, 0:1]
        k2 = scal[:, 1:2]
        pre = dtr_ref[at, :] + hv_ref[0:1, :]
        dt = softplus(pre)
        la = decay_rate * dt
        cum, cum_t, visible = decays(la, seg_col, segr_ref[:, span].astype(F32))
        z = z_ref[at, :]
        ys = ys_ref[at, :]
        sz = sigmoid(z)
        silu = z * sz
        gated = ys * silu
        dn = dn_ref[at, :]
        d_gated = r2 * og * dn - gated * k2
        a768[6:7, :] += jnp.sum(dn * gated * r2, axis=0, keepdims=True)
        dz_s[at, :] = (d_gated * ys * (sz * (1.0 + z * (1.0 - sz)))).astype(BF16)
        dy = d_gated * silu
        dy_low = dy.astype(BF16)
        p = p_ref[at, :]
        sp = sigmoid(p)
        u = p * sp
        a768[5:6, :] += jnp.sum(dy * u, axis=0, keepdims=True)
        pbc = pbc_ref[at, :]
        spbc = sigmoid(pbc)
        bcu = (pbc * spbc).astype(BF16)
        n = bcu.shape[1] // 2
        b, c = bcu[:, :n], bcu[:, n:]
        scores = dot_t(c, b)
        last = cum[CHUNK - 1 : CHUNK, :]
        flows = [dt, jnp.exp(cum) * keep, jnp.exp(last - cum) * tail]
        flows.append(jnp.broadcast_to(jnp.exp(last) * keep[CHUNK - 1 : CHUNK, :], (8, LANES)))
        wide = spread(jnp.concatenate(flows, axis=0), expand)
        dt_x, enter_x, end_x = (wide[k * CHUNK : (k + 1) * CHUNK, :] for k in range(3))
        carry = wide[3 * CHUNK : 3 * CHUNK + 1, :]
        v = dt_x * u
        v_low = v.astype(BF16)
        d_scores = jnp.zeros((CHUNK, CHUNK), F32)
        pieces, weighed = [], []
        for pair in range(heads // 2):
            lanes = slice(pair * LANES, (pair + 1) * LANES)
            dy_halves = jnp.concatenate(split_pair(dy_low[:, lanes]), axis=0)
            grads = dot_t(dy_halves, v_low[:, lanes])
            mats = []
            for k in range(2):
                decay = decay_matrix(cum, cum_t, visible, 2 * pair + k)
                grad = grads[k * CHUNK : (k + 1) * CHUNK, :]
                mat = scores * decay
                d_scores = d_scores + grad * decay
                weighed.append((grad * mat).astype(BF16))
                mats.append(mat.astype(BF16))
            pieces.append(tdot(jnp.concatenate(mats, axis=0), dy_halves))
        old_low = st_ref[piece]
        if piece == 0:
            line.step(2 * block + 2)
        else:

            @pl.when(block == 0)
            def _():
                line.step(1)

        d_cum = dot(jnp.concatenate(weighed, axis=1), pick) - tdot(jnp.concatenate(weighed, axis=0), pick)
        ds = d_state[...]
        ds_low = ds.astype(BF16)
        dv_state = end_x * dot(b, ds_low)
        dv = jnp.concatenate(pieces, axis=1) + dv_state
        dy_enter = enter_x * dy
        dy_enter_low = dy_enter.astype(BF16)
        d_b = dot_t((end_x * v).astype(BF16), ds_low)
        d_c = dot_t(dy_enter_low, old_low)
        flow = jnp.broadcast_to(jnp.sum(ds * old_low.astype(F32) * carry, axis=0, keepdims=True), (8, inner))
        flow_low = flow.astype(BF16)
        products = [dy_enter * dot(c, old_low), dv_state * v, dv * u, flow, flow - flow_low.astype(F32)]
        sums = dot_t(jnp.concatenate(products, axis=0).astype(BF16), expand[0:LANES, :])
        e, f, d_dt = (sums[k * CHUNK : (k + 1) * CHUNK, :] for k in range(3))
        flow = sums[3 * CHUNK : 3 * CHUNK + 1, :] + sums[3 * CHUNK + 8 : 3 * CHUNK + 9, :]
        d_state[...] = carry * ds + tdot(c, dy_enter_low)
        d_scores_low = d_scores.astype(BF16)
        d_c = d_c + dot(d_scores_low, b)
        d_b = d_b + tdot(d_scores_low, c)
        d_la = dot(both_ways, jnp.concatenate([d_cum + e, f], axis=0), HIGHEST) + flow
        d_dt = d_la * decay_rate + d_dt
        d_pre = d_dt * sigmoid(pre)
        ddt_s[at, :] = d_pre.astype(BF16)
        a128[0:1, :] += jnp.sum(d_pre, axis=0, keepdims=True)
        a128[1:2, :] += jnp.sum(d_la * la, axis=0, keepdims=True)
        du = dt_x * dv + dsk * dy
        ahead[at, :] = du * (sp * (1.0 + p * (1.0 - sp)))
        d_bcu = jnp.concatenate([d_b, d_c], axis=1)
        ahead_bc[at, :] = d_bcu * (spbc * (1.0 + pbc * (1.0 - spbc)))

    for e in range(cube.events):

        @pl.when(block == min(e, blocks - 1))
        def _():
            cube.event(e)

    same = [(segs[k : k + rows, :] == seg_all).astype(F32) for k in range(1, 4)]
    for hist, weight, raw, out, acc in (
        (ahead, cx_ref, xc_ref, dx_s, a768),
        (ahead_bc, cbc_ref, bc_ref, dbc_s, a256),
    ):
        value = raw[...].astype(F32)
        dp = hist[0:rows, :]
        acc[4:5, :] += jnp.sum(dp, axis=0, keepdims=True)
        acc[3:4, :] += jnp.sum(dp * value, axis=0, keepdims=True)
        total = dp * weight[3:4, :]
        for k in range(1, 4):
            later = hist[k : k + rows, :] * same[k - 1]
            total = total + later * weight[3 - k : 4 - k, :]
            acc[3 - k : 4 - k, :] += jnp.sum(later * value, axis=0, keepdims=True)
        out[...] = total.astype(BF16)
        hist[rows : rows + 8, :] = hist[0:8, :]
    segs[rows : rows + 8, :] = segs[0:8, :]

    @pl.when(block == 0)
    def _():
        for load in loads:
            load.wait()

    partial = dot_t(dz_s[...], wz_ref[...]) + dot_t(dx_s[...], wx_ref[...])
    partial = partial + dot(ddt_s[...], wdt_s[...]) + dot_t(dbc_s[...], wbc_ref[...])
    for piece in range(PIECES):
        low = partial[piece * CHUNK : (piece + 1) * CHUNK, :].astype(BF16)
        for q in range(2):
            xp_ref[piece, q] = low[q * ROWS : q * ROWS + ROWS, :]
            part[PIECES * block + PIECES - 1 - piece, q] = low[q * ROWS : q * ROWS + ROWS, :]

    x = x_ref[...].astype(F32)
    xr = x * inverse_rms(x)
    a1536[0:1, :] += jnp.sum(partial * xr, axis=0, keepdims=True)
    xn = (xr * ng).astype(BF16)
    for w in range(0, width, 512):
        left = xn[:, w : w + 512]
        acc_z[w : w + 512, :] += tdot(left, dz_s[...])
        acc_x[w : w + 512, :] += tdot(left, dx_s[...])
        for j in range(acc_bc.shape[0]):
            acc_bc[j, w : w + 512, :] += tdot(left, dbc_s[:, j * LANES : (j + 1) * LANES])
        acc_dt[w : w + 512, :] += tdot(left, ddt_s[...])
    @pl.when(block == blocks - 1)
    def _():
        bits = [(acc_z, gz_ref, w) for w in range(0, width, 256)] + [(acc_x, gx_ref, w) for w in range(0, width, 256)]
        copies = []
        for j, (acc, out, w) in enumerate(bits):
            if j >= 2:
                copies[j - 2].wait()
            stage[j % 2] = acc[w : w + 256, :].astype(BF16)
            copies.append(pltpu.make_async_copy(stage.at[j % 2], out.at[pl.ds(w, 256), :], stage_sem.at[j % 2]))
            copies[j].start()
        line.step(steps - 1)
        copies[-2].wait()
        copies[-1].wait()
        for j in range(width // LANES):
            rest[16 * j : 16 * j + 16, :] = acc_dt[j * LANES : (j + 1) * LANES, :].T[0:16, :]
        base = dt_rows(width)
        for acc, out in ((a768, rest), (a128, rest), (a1536, shared), (a256, shared)):
            if acc is a1536:
                base = 0
            for j in range(acc.shape[1] // LANES):
                out[base : base + 8, :] = acc[:, j * LANES : (j + 1) * LANES]
                base += 8
        packed = [
            pltpu.make_async_copy(rest, pack_ref, stage_sem.at[2]),
            pltpu.make_async_copy(shared, shared_ref, stage_sem.at[3]),
        ]
        for j in range(acc_bc.shape[0]):
            there = gb_ref.at[:, pl.ds(j * LANES, LANES)]
            packed.append(pltpu.make_async_copy(acc_bc.at[j], there, stage_sem.at[4 + j]))
        for copy in packed:
            copy.start()
        for copy in packed:
            copy.wait()
        line.close(carry_out)


def dt_rows(width):
    return width // LANES * 16


def slot_rows(inner):
    return (inner // LANES + 1) * 8


def rows_spec(block, cols, last=None):
    if last is None:
        return pl.BlockSpec((block, cols), lambda i: (i, 0))
    return pl.BlockSpec((block, cols), lambda i: (last - i, 0))


def whole_spec(array):
    return pl.BlockSpec(array.shape, lambda i: (0,) * array.ndim, pipeline_mode=pl.Buffered(1))


def fixed_spec(*dims):
    return pl.BlockSpec(dims, lambda i: (0,) * len(dims))


def on_device(
    x_in, segments, out_grad, norm_gain, w_z, w_x, w_bc, w_dt, conv_x, conv_bc, bias_x, bias_bc,
    dt_bias, a_log, d_skip, out_gain, w_out,
):
    count = lax.axis_size("tensor")
    x, g = x_in[0], out_grad[0]
    length, width = x.shape
    inner = w_x.shape[1]
    heads = w_dt.shape[1]
    bcw = w_bc.shape[1]
    state_n = bcw // 2
    blocks = length // BLOCK
    chunks = length // CHUNK
    last = blocks - 1
    pairs = 2 * chunks
    all_steps = pairs + LAG * (2 * count - 3)
    n_fwd = blocks + 4
    n_bwd = chunks + 2
    rest = all_steps - n_fwd - n_bwd
    wdt = w_dt.T
    per_head = (dt_bias[None, :], a_log[None, :], d_skip[None, :])
    x4 = x.reshape(chunks, 2, ROWS, width)
    g4 = g.reshape(chunks, 2, ROWS, width)
    shape = jax.ShapeDtypeStruct
    anywhere = pl.BlockSpec(memory_space=pl.ANY)
    pair_shape = (chunks, 2, ROWS, width)
    carry_shape = shape((LAG, 2, ROWS, width), BF16)
    res_shape = shape(pair_shape, BF16)

    def params(ident):
        return pltpu.CompilerParams(
            vmem_limit_bytes=62 * 2**20, dimension_semantics=("arbitrary",), collective_id=ident, has_side_effects=True
        )

    def cost(flops, moved):
        return pl.CostEstimate(flops=flops, bytes_accessed=moved, transcendentals=0)

    weights = (w_z, w_x, w_bc, wdt, w_out, norm_gain, bias_x, out_gain, bias_bc, conv_x, conv_bc, *per_head)
    z, p, xc, ys, pbc, bc, dtr, dn, st, yp, scal, gout, carry, res_y, res_x = pl.pallas_call(
        functools.partial(forward_kernel, heads, count, pairs, n_fwd, blocks),
        grid=(blocks,),
        in_specs=[
            rows_spec(BLOCK, width),
            rows_spec(BLOCK, width),
            pl.BlockSpec((1, BLOCK), lambda i: (0, i)),
            *[anywhere if w is w_out else whole_spec(w) for w in weights],
        ],
        out_specs=[
            rows_spec(BLOCK, inner),
            rows_spec(BLOCK, inner),
            rows_spec(BLOCK, inner),
            rows_spec(BLOCK, inner),
            rows_spec(BLOCK, bcw),
            rows_spec(BLOCK, bcw),
            rows_spec(BLOCK, LANES),
            rows_spec(BLOCK, inner),
            pl.BlockSpec((PIECES, state_n, inner), lambda i: (i, 0, 0)),
            pl.BlockSpec((PIECES, 2, ROWS, width), lambda i: (i, 0, 0, 0)),
            fixed_spec(chunks, 8, CHUNK),
            fixed_spec(2 * inner, width // 2),
            anywhere,
            anywhere,
            anywhere,
        ],
        out_shape=[
            shape((length, inner), F32),
            shape((length, inner), F32),
            shape((length, inner), BF16),
            shape((length, inner), F32),
            shape((length, bcw), F32),
            shape((length, bcw), F32),
            shape((length, LANES), F32),
            shape((length, inner), F32),
            shape((chunks, state_n, inner), BF16),
            shape(pair_shape, BF16),
            shape((chunks, 8, CHUNK), F32),
            shape((2 * inner, width // 2), BF16),
            carry_shape,
            res_shape,
            res_shape,
        ],
        scratch_shapes=[
            pltpu.VMEM(w_out.shape, BF16),
            pltpu.SemaphoreType.DMA,
            pltpu.VMEM((8, LANES), F32),
            pltpu.VMEM((LANES, width), BF16),
            pltpu.VMEM((2 * LANES, inner), BF16),
            pltpu.VMEM((BLOCK + 8, inner), F32),
            pltpu.VMEM((BLOCK + 8, bcw), F32),
            pltpu.VMEM((BLOCK + 8, 1), F32),
            pltpu.VMEM((state_n, inner), F32),
            pltpu.VMEM((RING, BLOCK, inner), F32),
            pltpu.VMEM((RING, BLOCK, width), BF16),
            pltpu.VMEM((inner, width), F32),
            pltpu.VMEM((blocks, PIECES, 8, CHUNK), F32),
            pltpu.VMEM((count - 1, blocks, PIECES, 8, CHUNK), F32),
            pltpu.SemaphoreType.DMA((count - 1, blocks)),
            pltpu.SemaphoreType.DMA((count - 1, blocks)),
            pltpu.VMEM((n_fwd, 2, ROWS, width), BF16),
            *line_scratch(n_fwd, width),
        ],
        compiler_params=params(0),
        cost_estimate=cost(9 * 10**10, 10**8),
        name="forward_scan",
    )(x, g, segments, *weights)

    weights = (w_z, w_x, w_bc, wdt, norm_gain, out_gain, conv_x, conv_bc, *per_head)
    n_in = 13 + len(weights)
    bits = lax.axis_size("dp").bit_length() - 1
    unit = 8 << bits
    pack_rows = -(-(dt_rows(width) + slot_rows(inner)) // unit) * unit
    shared_rows = -(-((width + bcw) // LANES * 8) // unit) * unit
    kind = F32 if (width >> bits) % 16 else BF16
    xp, gz, gx, gbc, pack, shared, carry, gout, res_y, res_x = pl.pallas_call(
        functools.partial(backward_kernel, heads, count, pairs, n_fwd, n_bwd),
        grid=(blocks,),
        in_specs=[
            rows_spec(BLOCK, inner, last),
            rows_spec(BLOCK, inner, last),
            rows_spec(BLOCK, inner, last),
            rows_spec(BLOCK, inner, last),
            rows_spec(BLOCK, bcw, last),
            rows_spec(BLOCK, bcw, last),
            rows_spec(BLOCK, LANES, last),
            rows_spec(BLOCK, inner, last),
            pl.BlockSpec((PIECES, state_n, inner), lambda i: (last - i, 0, 0)),
            pl.BlockSpec((1, BLOCK), lambda i: (0, jnp.maximum(last - i - 1, 0))),
            pl.BlockSpec((1, BLOCK), lambda i: (0, last - i)),
            pl.BlockSpec((PIECES, 8, CHUNK), lambda i: (last - i, 0, 0)),
            rows_spec(BLOCK, width, last),
            *[anywhere] * 3,
            *[whole_spec(w) for w in weights[3:]],
            *[anywhere] * 7,
        ],
        out_specs=[
            pl.BlockSpec((PIECES, 2, ROWS, width), lambda i: (last - i, 0, 0, 0)),
            *[anywhere] * 9,
        ],
        out_shape=[
            shape(pair_shape, BF16),
            shape((width, inner), BF16),
            shape((width, inner), BF16),
            shape((width, bcw), F32),
            shape((pack_rows, LANES), F32),
            shape((shared_rows, LANES), F32),
            carry_shape,
            shape((2 * inner, width // 2), BF16),
            res_shape,
            res_shape,
        ],
        scratch_shapes=[
            *[pltpu.VMEM(w.shape, BF16) for w in weights[:3]],
            pltpu.SemaphoreType.DMA((3,)),
            pltpu.VMEM((8, LANES), F32),
            pltpu.VMEM((LANES, width), BF16),
            pltpu.VMEM((2 * LANES, inner), BF16),
            pltpu.VMEM((BLOCK + 8, inner), F32),
            pltpu.VMEM((BLOCK + 8, bcw), F32),
            pltpu.VMEM((BLOCK + 8, 1), F32),
            pltpu.VMEM((state_n, inner), F32),
            pltpu.VMEM((BLOCK, inner), BF16),
            pltpu.VMEM((BLOCK, inner), BF16),
            pltpu.VMEM((BLOCK, LANES), BF16),
            pltpu.VMEM((BLOCK, bcw), BF16),
            pltpu.VMEM((width, inner), F32),
            pltpu.VMEM((width, inner), F32),
            pltpu.VMEM((bcw // LANES, width, LANES), F32),
            pltpu.VMEM((width, LANES), F32),
            pltpu.VMEM((8, width), F32),
            pltpu.VMEM((8, inner), F32),
            pltpu.VMEM((8, bcw), F32),
            pltpu.VMEM((8, LANES), F32),
            pltpu.VMEM((pack_rows, LANES), F32),
            pltpu.VMEM((shared_rows, LANES), F32),
            pltpu.VMEM((2, 256, inner), BF16),
            pltpu.SemaphoreType.DMA((4 + bcw // LANES,)),
            pltpu.VMEM((chunks, 2, ROWS, width), BF16),
            pltpu.SemaphoreType.DMA,
            *finals_scratch(width),
            *cube_scratch(2 * inner, width // 2, bits, BF16),
            *line_scratch(n_bwd, width),
        ],
        input_output_aliases={n_in + 5: 8, n_in + 6: 9},
        compiler_params=params(1),
        cost_estimate=cost(12 * 10**10, 10**8),
        name="backward_scan",
    )(z, p, xc, ys, pbc, bc, dtr, dn, st, segments, segments, scal, x, *weights, yp, x4, g4, carry, gout, res_y, res_x)

    left = pairs - (n_fwd + n_bwd - LAG * (count - 1))
    res_y, res_x, gz, gx, gbc, pack, shared = pl.pallas_call(
        functools.partial(line_kernel, count, pairs, n_fwd + n_bwd, rest),
        grid=(rest,),
        in_specs=[anywhere] * 3 + [whole_spec(norm_gain)] + [anywhere] * 8,
        out_specs=[anywhere] * 7,
        out_shape=[
            res_shape,
            res_shape,
            shape((width, inner), BF16),
            shape((width, inner), BF16),
            shape((width, bcw), kind),
            shape((pack_rows, LANES), F32),
            shape((shared_rows, LANES), F32),
        ],
        scratch_shapes=[
            pltpu.VMEM((left, 2, ROWS, width), BF16),
            pltpu.SemaphoreType.DMA,
            *finals_scratch(width),
            *cube_scratch(width, inner, bits, BF16),
            *cube_scratch(width, inner, bits, BF16),
            *cube_scratch(width, bcw, bits, F32),
            *cube_scratch(pack_rows, LANES, bits, F32),
            *cube_scratch(shared_rows, LANES, bits, F32),
            *cross_scratch(count, width >> bits, bcw, kind),
            *cross_scratch(count, shared_rows >> bits, LANES, F32),
            *line_scratch(rest, width),
        ],
        input_output_aliases={10: 0, 11: 1},
        compiler_params=params(2),
        cost_estimate=cost(10**11, 3 * 10**8),
        name="line_sums",
    )(xp, x4, g4, norm_gain, carry, gz, gx, gbc, pack, shared, res_y, res_x)

    wide = width // blocks
    tall = inner // blocks
    outs = pl.pallas_call(
        functools.partial(finish_kernel, heads),
        grid=(blocks,),
        in_specs=[
            rows_spec(BLOCK, width),
            rows_spec(BLOCK, width),
            rows_spec(BLOCK, width),
            pl.BlockSpec((PIECES, 8, CHUNK), lambda i: (i, 0, 0)),
            rows_spec(wide, inner),
            rows_spec(wide, inner),
            rows_spec(tall, width // 2),
            pl.BlockSpec((tall, width // 2), lambda i: (i + blocks, 0)),
            rows_spec(wide, bcw),
            whole_spec(pack),
            whole_spec(shared),
        ],
        out_specs=[
            rows_spec(BLOCK, width),
            rows_spec(BLOCK, width),
            rows_spec(wide, inner),
            rows_spec(wide, inner),
            rows_spec(tall, width),
            rows_spec(wide, bcw),
            fixed_spec(heads, width),
            fixed_spec(width),
            fixed_spec(4, inner),
            fixed_spec(inner),
            fixed_spec(inner),
            fixed_spec(1, heads),
            fixed_spec(4, bcw),
            fixed_spec(bcw),
            fixed_spec(1, heads),
            fixed_spec(1, heads),
        ],
        out_shape=[
            shape((length, width), BF16),
            shape((length, width), BF16),
            shape((width, inner), F32),
            shape((width, inner), F32),
            shape((inner, width), F32),
            shape((width, bcw), F32),
            shape((heads, width), F32),
            shape((width,), F32),
            shape((4, inner), F32),
            shape((inner,), F32),
            shape((inner,), F32),
            shape((1, heads), F32),
            shape((4, bcw), F32),
            shape((bcw,), F32),
            shape((1, heads), F32),
            shape((1, heads), F32),
        ],
        compiler_params=pltpu.CompilerParams(vmem_limit_bytes=60 * 2**20, dimension_semantics=("arbitrary",)),
        name="finish",
    )(x, res_y.reshape(length, width), res_x.reshape(length, width), scal, gz, gx, gout, gout, gbc, pack, shared)
    result, grad_x, gz, gx, gout, grad_wbc, grad_wdt, ng, cx, bx, og, ds, cbc, bbc, dtb, al = outs
    return (
        result[None], grad_x[None], ng, gz, gx, grad_wbc, grad_wdt.T, cx, cbc, bx, bbc, dtb[0], al[0], ds[0],
        og, gout,
    )


def solution(mesh):
    tensor_last = P(None, "tensor")
    in_specs = (
        P("dp", None, None), P("dp", None), P("dp", None, None), P(), tensor_last, tensor_last, P(), tensor_last,
        tensor_last, P(), P("tensor"), P(), P("tensor"), P("tensor"), P("tensor"), P("tensor"), P("tensor", None),
    )
    out_specs = (
        P("dp", None, None), P("dp", None, None), P(), tensor_last, tensor_last, P(), tensor_last, tensor_last, P(),
        P("tensor"), P(), P("tensor"), P("tensor"), P("tensor"), P("tensor"), P("tensor", None),
    )
    return jax.shard_map(on_device, mesh=mesh, in_specs=in_specs, out_specs=out_specs, check_vma=False)
```

```python
import functools

import jax
import jax.numpy as jnp
from jax import lax
from jax.experimental import pallas as pl
from jax.experimental.pallas import tpu as pltpu
from jax.sharding import PartitionSpec as P

EPS = 1e-05
CHUNK = 128
BLOCK = 256
PIECES = BLOCK // CHUNK
LANES = 128
ROWS = CHUNK // 4
PER = CHUNK // (2 * ROWS)
LAG = 2
RING = 4
F32 = jnp.float32
BF16 = jnp.bfloat16
HIGHEST = lax.Precision.HIGHEST
MESH = pl.DeviceIdType.MESH


def dot(a, b, precision=None):
    return lax.dot_general(a, b, (((1,), (0,)), ((), ())), precision=precision, preferred_element_type=F32)


def dot_t(a, b):
    return lax.dot_general(a, b, (((1,), (1,)), ((), ())), preferred_element_type=F32)


def tdot(a, b):
    return lax.dot_general(a, b, (((0,), (0,)), ((), ())), preferred_element_type=F32)


def sigmoid(v):
    return 1.0 / (1.0 + jnp.exp(-v))


def softplus(v):
    e = jnp.exp(-jnp.abs(v))
    series = e * (1.0 - e * (0.5 - e * (1.0 / 3.0 - e * 0.25)))
    return jnp.maximum(v, 0.0) + jnp.where(e < 0.03, series, jnp.log(1.0 + e))


def iotas(rows, cols):
    return (
        lax.broadcasted_iota(jnp.int32, (rows, cols), 0),
        lax.broadcasted_iota(jnp.int32, (rows, cols), 1),
    )


def fill_expand(expand, heads):
    r, c = iotas(*expand.shape)
    expand[...] = (lax.rem(r, LANES) == c // (expand.shape[1] // heads)).astype(BF16)


def spread(columns, expand):
    high = columns.astype(BF16)
    low = (columns - high.astype(F32)).astype(BF16)
    return dot(jnp.concatenate([high, low], axis=1), expand[...])


def decays(la, seg_col, seg_row):
    r, c = iotas(CHUNK, CHUNK)
    cum = dot((r >= c).astype(F32), la, HIGHEST)
    visible = (r >= c) & (seg_col == seg_row)
    return cum, cum.T, visible


def decay_matrix(cum, cum_t, visible, head):
    gap = cum[:, head : head + 1] - cum_t[head : head + 1, :]
    return jnp.exp(jnp.where(visible, gap, -1e30))


def split_pair(values):
    low = lax.broadcasted_iota(jnp.int32, values.shape, 1) < LANES // 2
    zero = jnp.zeros_like(values)
    return jnp.where(low, values, zero), jnp.where(low, zero, values)


def conv_taps(hist, weight, same, rows):
    out = hist[8 : 8 + rows, :] * weight[3:4, :]
    for k in range(1, 4):
        out = out + hist[8 - k : 8 - k + rows, :] * same[k - 1] * weight[3 - k : 4 - k, :]
    return out


def columns_of(segr_ref):
    rows = segr_ref.shape[1]
    pieces = []
    for at in range(0, rows, LANES):
        row = segr_ref[:, at : at + LANES].astype(F32)
        pieces.append(jnp.broadcast_to(row, (LANES, LANES)).T[:, 0:1])
    return jnp.concatenate(pieces, axis=0)


def fill_heads(hv, wdt_s, dtb_ref, al_ref, dsk_ref, wdt_ref):
    heads = wdt_ref.shape[0]
    hv[...] = jnp.zeros_like(hv)
    for j, ref in enumerate((dtb_ref, al_ref, dsk_ref)):
        hv[j : j + 1, 0:heads] = ref[...]
    wdt_s[...] = jnp.zeros_like(wdt_s)
    wdt_s[0:heads, :] = wdt_ref[...]


def row_of(ref):
    return ref[...].reshape(1, ref.shape[0])


def inverse_rms(tokens):
    return lax.rsqrt(jnp.sum(tokens * tokens, axis=1, keepdims=True) * (1.0 / tokens.shape[1]) + EPS)


def bring(src, dst, sem):
    copy = pltpu.make_async_copy(src, dst, sem)
    copy.start()
    copy.wait()


def hello(peers, dp_peers=()):
    barrier = pltpu.get_barrier_semaphore()
    for peer in dp_peers:
        pl.semaphore_signal(barrier, inc=1, device_id={"dp": peer}, device_id_type=MESH)
    for peer, there in peers:

        @pl.when(there)
        def _():
            pl.semaphore_signal(barrier, inc=1, device_id={"tensor": peer}, device_id_type=MESH)


def heard(peers, dp_peers=()):
    total = jnp.int32(len(dp_peers))
    for _, there in peers:
        total = total + there.astype(jnp.int32)
    pl.semaphore_wait(pltpu.get_barrier_semaphore(), total)


def neighbours(count):
    me = lax.axis_index("tensor")
    return [(me - 1, me > 0), (me + 1, me < count - 1)]


class Line:
    def __init__(self, count, pairs, first, steps, refs, source, finals=None):
        self.count, self.pairs, self.first, self.steps = count, pairs, first, steps
        self.source, self.finals = source, finals
        (self.res_y, self.res_x, self.land, self.send) = refs[:4]
        (self.red_out, self.red_in, self.bc_out, self.bc_in, self.local) = refs[4:]

    def to_result(self, k, q, act):
        half = self.pairs // 2

        @pl.when(k < half)
        def _():
            act(self.res_y.at[k, q])

        @pl.when(k >= half)
        def _():
            act(self.res_x.at[2 * half - 1 - k, q])

    def flow(self, q):
        me = lax.axis_index("tensor")
        if q == 0:
            return me, me - 1, me + 1
        return self.count - 1 - me, me + 1, me - 1

    def is_pair(self, i):
        return (i >= 0) & (i < self.pairs)

    def red(self, q, ls, toward, src):
        return pltpu.make_async_remote_copy(
            src_ref=src, dst_ref=self.land.at[ls + LAG, q], send_sem=self.red_out.at[q, ls],
            recv_sem=self.red_in.at[q, ls], device_id={"tensor": toward}, device_id_type=MESH,
        )

    def cast(self, q, ls, away, src, there):
        return pltpu.make_async_remote_copy(
            src_ref=src, dst_ref=there, send_sem=self.bc_out.at[q, ls],
            recv_sem=self.bc_in.at[q, ls], device_id={"tensor": away}, device_id_type=MESH,
        )

    def hold(self, q, ls):
        return self.send.at[lax.rem(ls, LAG), q]

    def keep(self, q, ls, there):
        return pltpu.make_async_copy(self.hold(q, ls), there, self.local.at[lax.rem(ls, LAG), q])

    def term(self, s, z):
        return s - LAG * (self.count - 1 - z)

    def back(self, s, z):
        return s - LAG * (self.count - 1 + z)

    def finish_red(self, q, s, ls):
        z, toward, away = self.flow(q)
        n = self.count
        i = self.term(s, z)

        @pl.when(self.is_pair(i) & (z > 0))
        def _():
            self.red(q, ls, toward, self.hold(q, ls)).wait_send()

        @pl.when(self.is_pair(i) & (z == 0))
        def _():
            self.cast(q, ls, away, self.hold(q, ls), self.res_y.at[0, q]).wait_send()
            self.keep(q, ls, self.res_y.at[0, q]).wait()

        @pl.when(self.is_pair(i + LAG) & (z < n - 1))
        def _():
            self.red(q, ls, toward, self.hold(q, ls)).wait_recv()

    def finish_cast(self, q, s, ls):
        z, _, away = self.flow(q)
        n = self.count
        k = self.back(s, z)

        @pl.when(self.is_pair(k) & (z > 0) & (z < n - 1))
        def _():
            self.cast(q, ls, away, self.res_y.at[0, q], self.res_y.at[0, q]).wait_send()

        @pl.when(self.is_pair(k + LAG) & (z > 0))
        def _():
            self.cast(q, ls, away, self.res_y.at[0, q], self.res_y.at[0, q]).wait_recv()

    def step(self, ls):
        n = self.count
        ls = jnp.int32(ls)
        s = self.first + ls
        for q in range(2):

            @pl.when(ls >= LAG)
            def _():
                self.finish_cast(q, s - LAG, ls - LAG)

            z, toward, away = self.flow(q)
            k = self.back(s, z)

            @pl.when(self.is_pair(k) & (z > 0) & (z < n - 1))
            def _():
                self.to_result(k, q, lambda there: self.cast(q, ls, away, there, there).start())

        for q in range(2):
            z, toward, away = self.flow(q)
            i = self.term(s, z)

            @pl.when(ls >= LAG)
            def _():
                self.finish_red(q, s - LAG, ls - LAG)

            @pl.when(self.is_pair(i))
            def _():
                mine = self.source(q, i)
                place = lax.rem(ls, LAG)

                @pl.when(z == n - 1)
                def _():
                    self.red(q, ls, toward, mine).start()

                @pl.when((z > 0) & (z < n - 1))
                def _():
                    self.send[place, q] = (mine[...].astype(F32) + self.land[ls, q].astype(F32)).astype(BF16)
                    self.red(q, ls, toward, self.hold(q, ls)).start()

                @pl.when(z == 0)
                def _():
                    total = mine[...].astype(F32) + self.land[ls, q].astype(F32)
                    if self.finals is None:
                        self.send[place, q] = total.astype(BF16)
                    else:
                        self.finals.last(q, i, total, self.hold(q, ls))

                    def give(there):
                        self.cast(q, ls, away, self.hold(q, ls), there).start()
                        self.keep(q, ls, there).start()

                    self.to_result(i, q, give)
                    if self.finals is not None:

                        @pl.when(ls + 1 < self.steps)
                        def _():
                            self.finals.fetch(q, i + 1)

    def held(self, q, s):
        z, _, _ = self.flow(q)
        return self.is_pair(self.term(s, z)) & (z < self.count - 1)

    def each_held(self, s, src, act):
        for q in range(2):
            for d in range(LAG):

                @pl.when(self.held(q, s + d))
                def _():
                    act(pltpu.make_async_copy(*src(d, q), self.local.at[d, q]))

    def open(self, carry):
        self.each_held(self.first, lambda d, q: (carry.at[d, q], self.land.at[d, q]), lambda copy: copy.start())
        for q in range(2):
            z, _, _ = self.flow(q)

            @pl.when(z == 0)
            def _():
                self.finals.fetch(q, jnp.int32(self.first - LAG * (self.count - 1)))

    def opened(self, carry):
        self.each_held(self.first, lambda d, q: (carry.at[d, q], self.land.at[d, q]), lambda copy: copy.wait())

    def close(self, carry):
        for d in range(LAG):
            ls = self.steps - LAG + d
            for q in range(2):
                self.finish_cast(q, self.first + ls, jnp.int32(ls))
                self.finish_red(q, self.first + ls, jnp.int32(ls))
        if carry is None:
            return
        left = (self.first + self.steps, lambda d, q: (self.land.at[self.steps + d, q], carry.at[d, q]))
        self.each_held(*left, lambda copy: copy.start())
        self.each_held(*left, lambda copy: copy.wait())


def line_scratch(steps, width):
    return [
        pltpu.VMEM((steps + LAG, 2, ROWS, width), BF16),
        pltpu.VMEM((LAG, 2, ROWS, width), BF16),
        pltpu.SemaphoreType.DMA((2, steps)),
        pltpu.SemaphoreType.DMA((2, steps)),
        pltpu.SemaphoreType.DMA((2, steps)),
        pltpu.SemaphoreType.DMA((2, steps)),
        pltpu.SemaphoreType.DMA((LAG, 2)),
    ]


class Finals:
    def __init__(self, pairs, x_any, g_any, gain, rows, sems):
        self.pairs, self.half, self.x_any, self.g_any, self.gain, self.rows, self.sems = (
            pairs, pairs // 2, x_any, g_any, gain, rows, sems,
        )

    def copies(self, q, i):
        b = 2 * self.half - 1 - i
        return [
            pltpu.make_async_copy(src.at[b, q], self.rows.at[q, j], self.sems.at[q, j])
            for j, src in enumerate((self.x_any, self.g_any))
        ]

    def fetch(self, q, i):
        @pl.when((i >= self.half) & (i < self.pairs))
        def _():
            for copy in self.copies(q, i):
                copy.start()

    def last(self, q, i, total, out):
        @pl.when(i < self.half)
        def _():
            out[...] = total.astype(BF16)

        @pl.when(i >= self.half)
        def _():
            for copy in self.copies(q, i):
                copy.wait()
            x = self.rows[q, 0].astype(F32)
            r1 = inverse_rms(x)
            scaled = total * self.gain
            across = jnp.sum(scaled * x, axis=1, keepdims=True) * (1.0 / x.shape[1])
            out[...] = (self.rows[q, 1].astype(F32) + r1 * scaled - x * (r1 * r1 * r1 * across)).astype(BF16)


def finals_scratch(width):
    return [pltpu.VMEM((2, 2, ROWS, width), BF16), pltpu.SemaphoreType.DMA((2, 2))]


def dp_bits():
    me = lax.axis_index("dp")
    bits = []
    for b in range(lax.axis_size("dp").bit_length() - 1):
        bit = lax.rem(me // 2**b, 2)
        bits.append((bit, me + (1 - 2 * bit) * 2**b))
    return bits


class Cube:
    def __init__(self, order, refs, across=None):
        self.order, self.across = order, across
        (self.src, self.out, self.total, self.send, self.land, self.out_sem, self.in_sem, self.local) = refs
        self.rows = self.src.shape[0]
        self.bits = dp_bits()
        self.events = 2 * len(order) + (1 if across is None else 2)

    def start_of(self, depth):
        at = 0
        for j in range(depth):
            at = at + self.bits[self.order[j]][0] * (self.rows >> (j + 1))
        return at

    def span(self, at, size):
        return pl.ds(pl.multiple_of(at, 8 if self.src.dtype == F32 else 16), size)

    def inside(self, depth):
        return self.start_of(depth) - self.start_of(1)

    def own_half(self):
        mine = self.src.at[self.span(self.start_of(1), self.rows // 2), :]
        return pltpu.make_async_copy(mine, self.send.at[pl.ds(0, self.rows // 2), :], self.local)

    def halving(self, j):
        size = self.rows >> (j + 1)
        bit, partner = self.bits[self.order[j]]
        theirs = self.start_of(j) + (1 - bit) * size
        src = self.src.at[self.span(theirs, size), :] if j == 0 else self.send.at[pl.ds(0, size), :]
        return pltpu.make_async_remote_copy(
            src_ref=src, dst_ref=self.land.at[pl.ds(self.rows - 2 * size, size), :], send_sem=self.out_sem.at[j],
            recv_sem=self.in_sem.at[j], device_id={"dp": partner}, device_id_type=MESH,
        )

    def doubling(self, j):
        count = len(self.order)
        size = self.rows >> (count - j)
        _, partner = self.bits[self.order[count - 1 - j]]
        mine = self.out.at[self.span(self.start_of(count - j), size), :]
        return pltpu.make_async_remote_copy(
            src_ref=mine, dst_ref=mine, send_sem=self.out_sem.at[count + j], recv_sem=self.in_sem.at[count + j],
            device_id={"dp": partner}, device_id_type=MESH,
        )

    def crossing(self, d):
        mine, land, out_sem, in_sem, peers = self.across
        return pltpu.make_async_remote_copy(
            src_ref=mine, dst_ref=land.at[d - 1], send_sem=out_sem.at[d - 1],
            recv_sem=in_sem.at[d - 1], device_id={"tensor": peers[d - 1]}, device_id_type=MESH,
        )

    def turn(self, part):
        count = len(self.order)
        size = self.rows >> count
        bring(part, self.out.at[self.span(self.start_of(count), size), :], self.local)
        self.doubling(0).start()

    def event(self, e):
        count = len(self.order)
        if e == 0:
            self.halving(0).start()
            self.own_half().start()
            return
        if e <= count:
            if e == 1:
                self.own_half().wait()
            self.halving(e - 1).wait()
            size = self.rows >> e
            at = self.inside(e)
            for r in range(0, size, 192):
                tile = min(192, size - r)
                landed = self.land[self.rows - 2 * size + r : self.rows - 2 * size + r + tile, :].astype(F32)
                here = self.span(at + r, tile)
                if e == 1:
                    self.total[here, :] = self.send[r : r + tile, :].astype(F32) + landed
                else:
                    self.total[here, :] = self.total[here, :] + landed
            if e < count:
                bit, _ = self.bits[self.order[e]]
                at = at + (1 - bit) * (size // 2)
                size = size // 2
            part = self.total[self.span(at, size), :]
            if e == count and self.across is not None:
                self.across[0][...] = part.astype(self.across[0].dtype)
                for d in range(1, len(self.across[4]) + 1):
                    self.crossing(d).start()
                return
            self.send[0:size, :] = part.astype(self.send.dtype)
            if e < count:
                self.halving(e).start()
            else:
                self.turn(self.send.at[pl.ds(0, size), :])
            return
        if self.across is not None:
            if e == count + 1:
                size = self.rows >> count
                total = self.total[self.span(self.inside(count), size), :]
                for d in range(1, len(self.across[4]) + 1):
                    self.crossing(d).wait()
                    total = total + self.across[1][d - 1].astype(F32)
                self.across[0][...] = total.astype(self.across[0].dtype)
                self.turn(self.across[0])
                return
            e = e - 1
        self.doubling(e - count - 1).wait()
        if e < 2 * count:
            self.doubling(e - count).start()


def cube_scratch(rows, cols, bits, dtype):
    return [
        pltpu.VMEM((rows // 2, cols), F32),
        pltpu.VMEM((rows // 2, cols), dtype),
        pltpu.VMEM((rows - (rows >> bits), cols), dtype),
        pltpu.SemaphoreType.DMA((2 * bits,)),
        pltpu.SemaphoreType.DMA((2 * bits,)),
        pltpu.SemaphoreType.DMA,
    ]


def cross_scratch(count, rows, cols, dtype):
    return [
        pltpu.VMEM((rows, cols), dtype),
        pltpu.VMEM((count - 1, rows, cols), dtype),
        pltpu.SemaphoreType.DMA((count - 1,)),
        pltpu.SemaphoreType.DMA((count - 1,)),
    ]


def tensor_peers(count):
    me = lax.axis_index("tensor")
    return [lax.rem(me + d, count) for d in range(1, count)]


def line_kernel(
    count, pairs, first, steps, xp_ref, x_any, g_any, ng_ref, carry_ref, gz_ref, gx_ref, gb_ref, pk_ref, sh_ref, res_y_in, res_x_in,
    res_y, res_x, oz_ref, ox_ref, ob_ref, op_ref, os_ref, part, part_sem, rows, sems, *scratch,
):
    del res_y_in, res_x_in
    half = pairs // 2
    order = list(range(len(dp_bits())))
    other = order[:1] + order[:0:-1]
    peers = tensor_peers(count)
    cubes = [
        Cube(order, (gz_ref, oz_ref, *scratch[0:6])),
        Cube(other, (gx_ref, ox_ref, *scratch[6:12])),
        Cube(order, (pk_ref, op_ref, *scratch[12:18])),
        Cube(order, (sh_ref, os_ref, *scratch[18:24]), (*scratch[24:28], peers)),
    ]
    tall = gb_ref.shape[0] // 2
    for j, way in enumerate((order, other)):
        rows_j = pl.ds(j * tall, tall)
        refs = scratch[28 + 10 * j : 38 + 10 * j]
        cubes.append(Cube(way, (gb_ref.at[rows_j, :], ob_ref.at[rows_j, :], *refs[0:6]), (*refs[6:10], peers)))

    finals = Finals(pairs, x_any, g_any, row_of(ng_ref), rows, sems)
    line = Line(
        count, pairs, first, steps, (res_y, res_x, *scratch[48:]), lambda q, i: part.at[2 * half - 1 - i, q], finals
    )
    at = pl.program_id(0)

    @pl.when(at == 0)
    def _():
        terms = pltpu.make_async_copy(xp_ref.at[pl.ds(0, part.shape[0])], part, part_sem)
        everyone = [(peer, peer >= 0) for peer in peers], [partner for _, partner in dp_bits()]
        hello(*everyone)
        terms.start()
        line.open(carry_ref)
        line.opened(carry_ref)
        terms.wait()
        heard(*everyone)

    if len(order) == 3:
        times = [0, 2, 7, 9, 11, 15, 17], [0, 2, 7, 9, 12, 15, 17, 18]
    else:
        times = (range(2 * len(order) + 2),) * 2
    for cube in cubes:
        when = times[0] if cube.across is None else times[1]
        for e in range(cube.events):

            @pl.when(at == min(when[e], steps - 1))
            def _():
                cube.event(e)

    line.step(at)

    @pl.when(at == steps - 1)
    def _():
        line.close(None)


def finish_kernel(
    heads, x_ref, y_ref, dx_ref, scal_ref, gz_ref, gx_ref, go_ref, go2_ref, gb_ref, pack_ref, shared_ref,
    yo_ref, xo_ref, oz_ref, ox_ref, oo_ref, wbc_ref, wdt_ref, ng_ref, cx_ref, bx_ref, og_ref, ds_ref, cbc_ref, bbc_ref,
    dtb_ref, al_ref,
):
    inner = cx_ref.shape[1]
    width, bcw = x_ref.shape[1], wbc_ref.shape[1]
    for piece in range(x_ref.shape[0] // CHUNK):
        span = slice(piece * CHUNK, (piece + 1) * CHUNK)
        r2 = jnp.concatenate([scal_ref[piece], jnp.zeros((CHUNK - 8, CHUNK), F32)], axis=0).T[:, 0:1]
        yo_ref[span, :] = (x_ref[span, :].astype(F32) + r2 * y_ref[span, :].astype(F32)).astype(BF16)
    xo_ref[...] = dx_ref[...]
    oz_ref[...] = gz_ref[...].astype(F32)
    ox_ref[...] = gx_ref[...].astype(F32)
    oo_ref[:, 0 : width // 2] = go_ref[...].astype(F32)
    oo_ref[:, width // 2 :] = go2_ref[...].astype(F32)
    wbc_ref[...] = gb_ref[...].astype(F32)

    @pl.when(pl.program_id(0) == 0)
    def _():
        for j in range(width // LANES):
            wdt_ref[:, j * LANES : (j + 1) * LANES] = pack_ref[16 * j : 16 * j + 16, :][0:heads, :]

        def put(ref, row):
            ref[...] = row.reshape(ref.shape)

        def side_by_side(ref, at, pieces, rows=8):
            return jnp.concatenate([ref[at + 8 * j : at + 8 * j + rows, :] for j in range(pieces)], axis=1)

        put(ng_ref, side_by_side(shared_ref, 0, width // LANES, 1))
        rows = side_by_side(shared_ref, width // LANES * 8, bcw // LANES)
        cbc_ref[...] = rows[0:4, :]
        put(bbc_ref, rows[4:5, :])
        rows = side_by_side(pack_ref, dt_rows(width), inner // LANES)
        cx_ref[...] = rows[0:4, :]
        put(bx_ref, rows[4:5, :])
        put(og_ref, rows[6:7, :])
        lane = lax.broadcasted_iota(jnp.int32, (1, heads), 1)
        skip = jnp.zeros((1, heads), F32)
        for h in range(heads):
            head = jnp.sum(rows[5:6, h * 64 : h * 64 + 64], axis=1, keepdims=True)
            skip = jnp.where(lane == h, head, skip)
        ds_ref[...] = skip
        at = dt_rows(width) + inner // LANES * 8
        rows = pack_ref[at : at + 8, :]
        dtb_ref[...] = rows[0:1, 0:heads]
        al_ref[...] = rows[1:2, 0:heads]


def forward_kernel(
    heads, count, pairs, steps, blocks,
    x_ref, g_ref, segr_ref, wz_ref, wx_ref, wbc_ref, wdt_ref, wo_any, ng_ref, bx_ref, og_ref, bbc_ref, cx_ref, cbc_ref,
    dtb_ref, al_ref, dsk_ref,
    z_ref, p_ref, xc_ref, ys_ref, pbc_ref, bc_ref, dtr_ref, dn_ref, st_ref, yp_ref, scal_ref, wout_ref,
    carry_out, res_y, res_x,
    wo_ref, w_sem, hv_ref, wdt_s, expand, hist, hist_bc, segs, state, scaled_s, g_s, acc_out, stat_mine, stat_land, stat_out, stat_in, part, *scratch,
):
    rows, width = x_ref.shape
    inner = z_ref.shape[1]
    block = pl.program_id(0)
    me = lax.axis_index("tensor")
    ng, bx, og, bbc = row_of(ng_ref), row_of(bx_ref), row_of(og_ref), row_of(bbc_ref)

    line = Line(count, pairs, 0, steps, (res_y, res_x, *scratch), lambda q, i: part.at[i, q])

    load = pltpu.make_async_copy(wo_any, wo_ref, w_sem)
    everyone = [(peer, peer >= 0) for peer in tensor_peers(count)]

    @pl.when(block == 0)
    def _():
        hello(everyone)
        load.start()
        fill_heads(hv_ref, wdt_s, dtb_ref, al_ref, dsk_ref, wdt_ref)
        fill_expand(expand, heads)
        hist[0:8, :] = jnp.zeros((8, hist.shape[1]), F32)
        hist_bc[0:8, :] = jnp.zeros((8, hist_bc.shape[1]), F32)
        segs[0:8, :] = jnp.full((8, 1), -1.0, F32)
        state[...] = jnp.zeros_like(state)
        acc_out[...] = jnp.zeros_like(acc_out)

    x = x_ref[...].astype(F32)
    xn = (x * inverse_rms(x) * ng).astype(BF16)
    z_ref[...] = dot(xn, wz_ref[...])
    xc = dot(xn, wx_ref[...])
    bc = dot(xn, wbc_ref[...])
    dtr = dot_t(xn, wdt_s[...])
    xc_ref[...] = xc.astype(BF16)
    bc_ref[...] = bc
    dtr_ref[...] = dtr
    seg_all = columns_of(segr_ref)
    segs[8 : 8 + rows, :] = seg_all
    hist[8 : 8 + rows, :] = xc
    hist_bc[8 : 8 + rows, :] = bc
    same = [(segs[8 - k : 8 - k + rows, :] == seg_all).astype(F32) for k in range(1, 4)]
    p_ref[...] = conv_taps(hist, cx_ref, same, rows) + bx
    pbc_ref[...] = conv_taps(hist_bc, cbc_ref, same, rows) + bbc
    g = g_ref[...]
    g_s[lax.rem(block, RING)] = g
    dt_all = softplus(dtr + hv_ref[0:1, :])
    la_all = -jnp.exp(hv_ref[1:2, :]) * dt_all
    dsk = spread(hv_ref[...], expand)[2:3, :]
    row_i, lane_i = iotas(CHUNK, LANES)
    squares = []
    for piece in range(PIECES):
        at = pl.ds(piece * CHUNK, CHUNK)
        span = slice(piece * CHUNK, (piece + 1) * CHUNK)
        seg_col = seg_all[span, :]
        keep = (seg_col == segs[7 + piece * CHUNK : 8 + piece * CHUNK, :]).astype(F32)
        tail = (seg_col == seg_col[CHUNK - 1 : CHUNK, :]).astype(F32)
        dt = dt_all[span, :]
        cum, cum_t, visible = decays(la_all[span, :], seg_col, segr_ref[:, span].astype(F32))
        p = p_ref[at, :]
        u = p * sigmoid(p)
        pbc = pbc_ref[at, :]
        bcu = (pbc * sigmoid(pbc)).astype(BF16)
        n = bcu.shape[1] // 2
        b, c = bcu[:, :n], bcu[:, n:]
        scores = dot_t(c, b)
        last = cum[CHUNK - 1 : CHUNK, :]
        flows = [dt, jnp.exp(cum) * keep, jnp.exp(last - cum) * tail]
        flows.append(jnp.broadcast_to(jnp.exp(last) * keep[CHUNK - 1 : CHUNK, :], (8, LANES)))
        wide = spread(jnp.concatenate(flows, axis=0), expand)
        dt_x, enter_x, end_x = (wide[k * CHUNK : (k + 1) * CHUNK, :] for k in range(3))
        carry = wide[3 * CHUNK : 3 * CHUNK + 1, :]
        v = dt_x * u
        v_low = v.astype(BF16)
        pieces = []
        for pair in range(heads // 2):
            mats = [
                (scores * decay_matrix(cum, cum_t, visible, 2 * pair + k)).astype(BF16)
                for k in range(2)
            ]
            halves = split_pair(v_low[:, pair * LANES : (pair + 1) * LANES])
            pieces.append(dot(jnp.concatenate(mats, axis=1), jnp.concatenate(halves, axis=0)))
        if piece:

            @pl.when(block < 2)
            def _():
                line.step(4 * block + 1)

        inside = jnp.concatenate(pieces, axis=1)
        old = state[...]
        old_low = old.astype(BF16)
        st_ref[piece] = old_low
        entering = dot(c, old_low) * enter_x
        state[...] = old * carry + tdot(b, (end_x * v).astype(BF16))
        ys = inside + entering + dsk * u
        ys_ref[at, :] = ys
        z = z_ref[at, :]
        gated = ys * (z * sigmoid(z))
        scaled = gated * og
        scaled_s[lax.rem(block, RING), at, :] = scaled
        if piece == 0:

            @pl.when(block == 0)
            def _():
                heard(everyone)
                load.wait()

        y_part = dot(scaled.astype(BF16), wo_ref[...]).astype(BF16)
        for r in range(PER):
            for q in range(2):
                low = y_part[(2 * r + q) * ROWS : (2 * r + q + 1) * ROWS, :]
                yp_ref[piece * PER + r, q] = low
                part[(block * PIECES + piece) * PER + r, q] = low

        later = jnp.where(block < 4, 3 * block + 2 + piece, 2 * block + 6 + piece)
        line.step(jnp.where(block < 2, 4 * block + 2 * piece, later))

        squares.append(jnp.sum(gated * gated, axis=1, keepdims=True))

    dn = dot_t(g, wo_ref[...])
    dn_ref[...] = dn
    for piece in range(PIECES):
        span = slice(piece * CHUNK, (piece + 1) * CHUNK)
        across = jnp.sum(dn[span, :] * scaled_s[lax.rem(block, RING), span, :], axis=1, keepdims=True)
        both = jnp.where(lane_i == 0, squares[piece], jnp.where(lane_i == 1, across, 0.0))
        stat_mine[block, piece] = both.T[0:8, :]
    hist[0:8, :] = hist[rows : rows + 8, :]
    hist_bc[0:8, :] = hist_bc[rows : rows + 8, :]
    segs[0:8, :] = segs[rows : rows + 8, :]

    def stat_copy(d, b):
        return pltpu.make_async_remote_copy(
            src_ref=stat_mine.at[b], dst_ref=stat_land.at[d - 1, b], send_sem=stat_out.at[d - 1, b],
            recv_sem=stat_in.at[d - 1, b], device_id={"tensor": lax.rem(me + d, count)}, device_id_type=MESH,
        )

    def settle(b):
        total = stat_mine[b]
        for d in range(1, count):
            stat_copy(d, b).wait()
            total = total + stat_land[d - 1, b]
        place = lax.rem(b, RING)
        low = []
        for piece in range(PIECES):
            r2 = lax.rsqrt(total[piece, 0:1, :] * (1.0 / (inner * count)) + EPS)
            k2 = r2 * r2 * r2 * (total[piece, 1:2, :] * (1.0 / (inner * count)))
            both = jnp.where(row_i == 0, r2, jnp.where(row_i == 1, k2, 0.0))
            scal_ref[b * PIECES + piece] = both[0:8, :]
            low.append((scaled_s[place, piece * CHUNK : (piece + 1) * CHUNK, :] * both.T[:, 0:1]).astype(BF16))
        normed = jnp.concatenate(low, axis=0)
        up = g_s[place]
        for c in range(0, inner, 256):
            acc_out[c : c + 256, :] += tdot(normed[:, c : c + 256], up)

    for d in range(1, count):
        stat_copy(d, block).start()

    @pl.when(block < 4)
    def _():
        line.step(jnp.where(block < 2, 4 * block + 3, 3 * block + 4))

    @pl.when(block >= RING - 1)
    def _():
        settle(block - (RING - 1))

    @pl.when(block == blocks - 1)
    def _():
        for b in range(1, RING):
            settle(blocks - RING + b)
        for c in range(0, inner, 256):
            low = acc_out[c : c + 256, :].astype(BF16)
            wout_ref[c : c + 256, :] = low[:, 0 : width // 2]
            wout_ref[inner + c : inner + c + 256, :] = low[:, width // 2 :]
        line.close(carry_out)


def backward_kernel(
    heads, count, pairs, first, steps,
    z_ref, p_ref, xc_ref, ys_ref, pbc_ref, bc_ref, dtr_ref, dn_ref, st_ref, segp_ref, segr_ref, scal_ref, x_ref,
    wz_any, wx_any, wbc_any, wdt_ref, ng_ref, og_ref, cx_ref, cbc_ref, dtb_ref, al_ref, dsk_ref, y_ref, x_any, g_any, carry_ref, go_ref, res_y_in, res_x_in,
    xp_ref, gz_ref, gx_ref, gb_ref, pack_ref, shared_ref, carry_out, go_sum, res_y, res_x,
    wz_ref, wx_ref, wbc_ref, w_sem, hv_ref, wdt_s, expand, ahead, ahead_bc, segs, d_state, dz_s, dx_s, ddt_s, dbc_s, acc_z, acc_x, acc_bc, acc_dt,
    a1536, a768, a256, a128, rest, shared, stage, stage_sem, part, part_sem, rows_s, rows_sem, *scratch,
):
    del res_y_in, res_x_in
    rows, inner = z_ref.shape
    width = x_ref.shape[1]
    block = pl.program_id(0)
    blocks = steps // (PIECES * PER)
    half = pairs // 2
    me = lax.axis_index("tensor")
    ng, og = row_of(ng_ref), row_of(og_ref)

    finals = Finals(pairs, x_any, g_any, ng, rows_s, rows_sem)
    line = Line(
        count, pairs, first, steps, (res_y, res_x, *scratch[6:]), lambda q, i: part.at[lax.rem(i, half), q], finals
    )
    loads = [
        pltpu.make_async_copy(src, dst, w_sem.at[j])
        for j, (src, dst) in enumerate(((wz_any, wz_ref), (wx_any, wx_ref), (wbc_any, wbc_ref)))
    ]
    cube = Cube(list(range(len(dp_bits()))), (go_ref, go_sum, *scratch[0:6]))
    old = first - LAG * (count - 1)

    @pl.when(block == 0)
    def _():
        terms = pltpu.make_async_copy(y_ref.at[pl.ds(old, half - old)], part.at[pl.ds(old, half - old)], part_sem)
        everyone = neighbours(count), [partner for _, partner in dp_bits()]
        hello(*everyone)
        terms.start()
        line.open(carry_ref)
        for load in loads:
            load.start()
        line.opened(carry_ref)
        terms.wait()
        heard(*everyone)
        line.step(0)
        fill_heads(hv_ref, wdt_s, dtb_ref, al_ref, dsk_ref, wdt_ref)
        fill_expand(expand, heads)
        ahead[rows : rows + 8, :] = jnp.zeros((8, ahead.shape[1]), F32)
        ahead_bc[rows : rows + 8, :] = jnp.zeros((8, ahead_bc.shape[1]), F32)
        segs[rows : rows + 8, :] = jnp.full((8, 1), -1.0, F32)
        for ref in (d_state, acc_z, acc_x, acc_bc, acc_dt, a1536, a768, a256, a128, rest, shared):
            ref[...] = jnp.zeros_like(ref)

    @pl.when(block > 0)
    def _():
        line.step(4 * block)

    seg_all = columns_of(segr_ref)
    segs[0:rows, :] = seg_all
    before = jnp.where(block == blocks - 1, -1.0, segp_ref[:, rows - 1 : rows].astype(F32))
    r, c_ = iotas(CHUNK, CHUNK)
    both_ways = jnp.concatenate([(r <= c_).astype(F32), (r > c_).astype(F32)], axis=1)
    all_r, all_l = iotas(heads * CHUNK, LANES)
    pick = (all_r // CHUNK == all_l).astype(BF16)
    decay_rate = -jnp.exp(hv_ref[1:2, :])
    dsk = spread(hv_ref[...], expand)[2:3, :]
    for piece in reversed(range(PIECES)):
        at = pl.ds(piece * CHUNK, CHUNK)
        span = slice(piece * CHUNK, (piece + 1) * CHUNK)
        seg_col = seg_all[span, :]
        prev = seg_all[piece * CHUNK - 1 : piece * CHUNK, :] if piece else before
        keep = (seg_col == prev).astype(F32)
        tail = (seg_col == seg_col[CHUNK - 1 : CHUNK, :]).astype(F32)
        scal = jnp.concatenate([scal_ref[piece], jnp.zeros((CHUNK - 8, CHUNK), F32)], axis=0).T
        r2 = scal[:, 0:1]
        k2 = scal[:, 1:2]
        pre = dtr_ref[at, :] + hv_ref[0:1, :]
        dt = softplus(pre)
        la = decay_rate * dt
        cum, cum_t, visible = decays(la, seg_col, segr_ref[:, span].astype(F32))
        z = z_ref[at, :]
        ys = ys_ref[at, :]
        sz = sigmoid(z)
        silu = z * sz
        gated = ys * silu
        dn = dn_ref[at, :]
        d_gated = r2 * og * dn - gated * k2
        a768[6:7, :] += jnp.sum(dn * gated * r2, axis=0, keepdims=True)
        dz_s[at, :] = (d_gated * ys * (sz * (1.0 + z * (1.0 - sz)))).astype(BF16)
        dy = d_gated * silu
        dy_low = dy.astype(BF16)
        p = p_ref[at, :]
        sp = sigmoid(p)
        u = p * sp
        a768[5:6, :] += jnp.sum(dy * u, axis=0, keepdims=True)
        pbc = pbc_ref[at, :]
        spbc = sigmoid(pbc)
        bcu = (pbc * spbc).astype(BF16)
        n = bcu.shape[1] // 2
        b, c = bcu[:, :n], bcu[:, n:]
        scores = dot_t(c, b)
        last = cum[CHUNK - 1 : CHUNK, :]
        flows = [dt, jnp.exp(cum) * keep, jnp.exp(last - cum) * tail]
        flows.append(jnp.broadcast_to(jnp.exp(last) * keep[CHUNK - 1 : CHUNK, :], (8, LANES)))
        wide = spread(jnp.concatenate(flows, axis=0), expand)
        dt_x, enter_x, end_x = (wide[k * CHUNK : (k + 1) * CHUNK, :] for k in range(3))
        carry = wide[3 * CHUNK : 3 * CHUNK + 1, :]
        v = dt_x * u
        v_low = v.astype(BF16)
        d_scores = jnp.zeros((CHUNK, CHUNK), F32)
        pieces, weighed = [], []
        for pair in range(heads // 2):
            lanes = slice(pair * LANES, (pair + 1) * LANES)
            dy_halves = jnp.concatenate(split_pair(dy_low[:, lanes]), axis=0)
            grads = dot_t(dy_halves, v_low[:, lanes])
            mats = []
            for k in range(2):
                decay = decay_matrix(cum, cum_t, visible, 2 * pair + k)
                grad = grads[k * CHUNK : (k + 1) * CHUNK, :]
                mat = scores * decay
                d_scores = d_scores + grad * decay
                weighed.append((grad * mat).astype(BF16))
                mats.append(mat.astype(BF16))
            pieces.append(tdot(jnp.concatenate(mats, axis=0), dy_halves))
        old_low = st_ref[piece]
        line.step(4 * block + 2 - piece)
        d_cum = dot(jnp.concatenate(weighed, axis=1), pick) - tdot(jnp.concatenate(weighed, axis=0), pick)
        ds = d_state[...]
        ds_low = ds.astype(BF16)
        dv_state = end_x * dot(b, ds_low)
        dv = jnp.concatenate(pieces, axis=1) + dv_state
        dy_enter = enter_x * dy
        dy_enter_low = dy_enter.astype(BF16)
        d_b = dot_t((end_x * v).astype(BF16), ds_low)
        d_c = dot_t(dy_enter_low, old_low)
        flow = jnp.broadcast_to(jnp.sum(ds * old_low.astype(F32) * carry, axis=0, keepdims=True), (8, inner))
        flow_low = flow.astype(BF16)
        products = [dy_enter * dot(c, old_low), dv_state * v, dv * u, flow, flow - flow_low.astype(F32)]
        sums = dot_t(jnp.concatenate(products, axis=0).astype(BF16), expand[0:LANES, :])
        e, f, d_dt = (sums[k * CHUNK : (k + 1) * CHUNK, :] for k in range(3))
        flow = sums[3 * CHUNK : 3 * CHUNK + 1, :] + sums[3 * CHUNK + 8 : 3 * CHUNK + 9, :]
        d_state[...] = carry * ds + tdot(c, dy_enter_low)
        d_scores_low = d_scores.astype(BF16)
        d_c = d_c + dot(d_scores_low, b)
        d_b = d_b + tdot(d_scores_low, c)
        d_la = dot(both_ways, jnp.concatenate([d_cum + e, f], axis=0), HIGHEST) + flow
        d_dt = d_la * decay_rate + d_dt
        d_pre = d_dt * sigmoid(pre)
        ddt_s[at, :] = d_pre.astype(BF16)
        a128[0:1, :] += jnp.sum(d_pre, axis=0, keepdims=True)
        a128[1:2, :] += jnp.sum(d_la * la, axis=0, keepdims=True)
        du = dt_x * dv + dsk * dy
        ahead[at, :] = du * (sp * (1.0 + p * (1.0 - sp)))
        d_bcu = jnp.concatenate([d_b, d_c], axis=1)
        ahead_bc[at, :] = d_bcu * (spbc * (1.0 + pbc * (1.0 - spbc)))

    for e in range(cube.events):

        @pl.when(block == min(e, blocks - 1))
        def _():
            cube.event(e)

    same = [(segs[k : k + rows, :] == seg_all).astype(F32) for k in range(1, 4)]
    for hist, weight, raw, out, acc in (
        (ahead, cx_ref, xc_ref, dx_s, a768),
        (ahead_bc, cbc_ref, bc_ref, dbc_s, a256),
    ):
        value = raw[...].astype(F32)
        dp = hist[0:rows, :]
        acc[4:5, :] += jnp.sum(dp, axis=0, keepdims=True)
        acc[3:4, :] += jnp.sum(dp * value, axis=0, keepdims=True)
        total = dp * weight[3:4, :]
        for k in range(1, 4):
            later = hist[k : k + rows, :] * same[k - 1]
            total = total + later * weight[3 - k : 4 - k, :]
            acc[3 - k : 4 - k, :] += jnp.sum(later * value, axis=0, keepdims=True)
        out[...] = total.astype(BF16)
        hist[rows : rows + 8, :] = hist[0:8, :]
    segs[rows : rows + 8, :] = segs[0:8, :]

    @pl.when(block == 0)
    def _():
        for load in loads:
            load.wait()

    partial = dot_t(dz_s[...], wz_ref[...]) + dot_t(dx_s[...], wx_ref[...])
    partial = partial + dot(ddt_s[...], wdt_s[...]) + dot_t(dbc_s[...], wbc_ref[...])
    for piece in range(PIECES):
        low = partial[piece * CHUNK : (piece + 1) * CHUNK, :].astype(BF16)
        for r in range(PER):
            for q in range(2):
                part_low = low[(2 * r + q) * ROWS : (2 * r + q + 1) * ROWS, :]
                xp_ref[piece * PER + r, q] = part_low
                part[(block + 1) * PIECES * PER - 1 - piece * PER - r, q] = part_low

    line.step(4 * block + 3)
    x = x_ref[...].astype(F32)
    xr = x * inverse_rms(x)
    a1536[0:1, :] += jnp.sum(partial * xr, axis=0, keepdims=True)
    xn = (xr * ng).astype(BF16)
    for w in range(0, width, 512):
        left = xn[:, w : w + 512]
        acc_z[w : w + 512, :] += tdot(left, dz_s[...])
        acc_x[w : w + 512, :] += tdot(left, dx_s[...])
        for j in range(acc_bc.shape[0]):
            acc_bc[j, w : w + 512, :] += tdot(left, dbc_s[:, j * LANES : (j + 1) * LANES])
        acc_dt[w : w + 512, :] += tdot(left, ddt_s[...])
    @pl.when(block == blocks - 1)
    def _():
        bits = [(acc_z, gz_ref, w) for w in range(0, width, 256)] + [(acc_x, gx_ref, w) for w in range(0, width, 256)]
        copies = []
        for j, (acc, out, w) in enumerate(bits):
            if j >= 2:
                copies[j - 2].wait()
            stage[j % 2] = acc[w : w + 256, :].astype(BF16)
            copies.append(pltpu.make_async_copy(stage.at[j % 2], out.at[pl.ds(w, 256), :], stage_sem.at[j % 2]))
            copies[j].start()
        copies[-2].wait()
        copies[-1].wait()
        for j in range(width // LANES):
            rest[16 * j : 16 * j + 16, :] = acc_dt[j * LANES : (j + 1) * LANES, :].T[0:16, :]
        base = dt_rows(width)
        for acc, out in ((a768, rest), (a128, rest), (a1536, shared), (a256, shared)):
            if acc is a1536:
                base = 0
            for j in range(acc.shape[1] // LANES):
                out[base : base + 8, :] = acc[:, j * LANES : (j + 1) * LANES]
                base += 8
        packed = [
            pltpu.make_async_copy(rest, pack_ref, stage_sem.at[2]),
            pltpu.make_async_copy(shared, shared_ref, stage_sem.at[3]),
        ]
        for j in range(acc_bc.shape[0]):
            there = gb_ref.at[:, pl.ds(j * LANES, LANES)]
            packed.append(pltpu.make_async_copy(acc_bc.at[j], there, stage_sem.at[4 + j]))
        for copy in packed:
            copy.start()
        for copy in packed:
            copy.wait()
        line.close(carry_out)


def dt_rows(width):
    return width // LANES * 16


def slot_rows(inner):
    return (inner // LANES + 1) * 8


def rows_spec(block, cols, last=None):
    if last is None:
        return pl.BlockSpec((block, cols), lambda i: (i, 0))
    return pl.BlockSpec((block, cols), lambda i: (last - i, 0))


def whole_spec(array):
    return pl.BlockSpec(array.shape, lambda i: (0,) * array.ndim, pipeline_mode=pl.Buffered(1))


def fixed_spec(*dims):
    return pl.BlockSpec(dims, lambda i: (0,) * len(dims))


def on_device(
    x_in, segments, out_grad, norm_gain, w_z, w_x, w_bc, w_dt, conv_x, conv_bc, bias_x, bias_bc,
    dt_bias, a_log, d_skip, out_gain, w_out,
):
    count = lax.axis_size("tensor")
    x, g = x_in[0], out_grad[0]
    length, width = x.shape
    inner = w_x.shape[1]
    heads = w_dt.shape[1]
    bcw = w_bc.shape[1]
    state_n = bcw // 2
    blocks = length // BLOCK
    chunks = length // CHUNK
    last = blocks - 1
    pairs = length // ROWS
    all_steps = pairs + LAG * (2 * count - 3)
    n_fwd = 2 * blocks + 6
    n_bwd = pairs // 2
    rest = all_steps - n_fwd - n_bwd
    wdt = w_dt.T
    per_head = (dt_bias[None, :], a_log[None, :], d_skip[None, :])
    x4 = x.reshape(pairs // 2, 2, ROWS, width)
    g4 = g.reshape(pairs // 2, 2, ROWS, width)
    shape = jax.ShapeDtypeStruct
    anywhere = pl.BlockSpec(memory_space=pl.ANY)
    pair_shape = (pairs // 2, 2, ROWS, width)
    carry_shape = shape((LAG, 2, ROWS, width), BF16)
    res_shape = shape(pair_shape, BF16)

    def params(ident):
        return pltpu.CompilerParams(
            vmem_limit_bytes=62 * 2**20, dimension_semantics=("arbitrary",), collective_id=ident, has_side_effects=True
        )

    def cost(flops, moved):
        return pl.CostEstimate(flops=flops, bytes_accessed=moved, transcendentals=0)

    weights = (w_z, w_x, w_bc, wdt, w_out, norm_gain, bias_x, out_gain, bias_bc, conv_x, conv_bc, *per_head)
    z, p, xc, ys, pbc, bc, dtr, dn, st, yp, scal, gout, carry, res_y, res_x = pl.pallas_call(
        functools.partial(forward_kernel, heads, count, pairs, n_fwd, blocks),
        grid=(blocks,),
        in_specs=[
            rows_spec(BLOCK, width),
            rows_spec(BLOCK, width),
            pl.BlockSpec((1, BLOCK), lambda i: (0, i)),
            *[anywhere if w is w_out else whole_spec(w) for w in weights],
        ],
        out_specs=[
            rows_spec(BLOCK, inner),
            rows_spec(BLOCK, inner),
            rows_spec(BLOCK, inner),
            rows_spec(BLOCK, inner),
            rows_spec(BLOCK, bcw),
            rows_spec(BLOCK, bcw),
            rows_spec(BLOCK, LANES),
            rows_spec(BLOCK, inner),
            pl.BlockSpec((PIECES, state_n, inner), lambda i: (i, 0, 0)),
            pl.BlockSpec((PIECES * PER, 2, ROWS, width), lambda i: (i, 0, 0, 0)),
            fixed_spec(chunks, 8, CHUNK),
            fixed_spec(2 * inner, width // 2),
            anywhere,
            anywhere,
            anywhere,
        ],
        out_shape=[
            shape((length, inner), F32),
            shape((length, inner), F32),
            shape((length, inner), BF16),
            shape((length, inner), F32),
            shape((length, bcw), F32),
            shape((length, bcw), F32),
            shape((length, LANES), F32),
            shape((length, inner), F32),
            shape((chunks, state_n, inner), BF16),
            shape(pair_shape, BF16),
            shape((chunks, 8, CHUNK), F32),
            shape((2 * inner, width // 2), BF16),
            carry_shape,
            res_shape,
            res_shape,
        ],
        scratch_shapes=[
            pltpu.VMEM(w_out.shape, BF16),
            pltpu.SemaphoreType.DMA,
            pltpu.VMEM((8, LANES), F32),
            pltpu.VMEM((LANES, width), BF16),
            pltpu.VMEM((2 * LANES, inner), BF16),
            pltpu.VMEM((BLOCK + 8, inner), F32),
            pltpu.VMEM((BLOCK + 8, bcw), F32),
            pltpu.VMEM((BLOCK + 8, 1), F32),
            pltpu.VMEM((state_n, inner), F32),
            pltpu.VMEM((RING, BLOCK, inner), F32),
            pltpu.VMEM((RING, BLOCK, width), BF16),
            pltpu.VMEM((inner, width), F32),
            pltpu.VMEM((blocks, PIECES, 8, CHUNK), F32),
            pltpu.VMEM((count - 1, blocks, PIECES, 8, CHUNK), F32),
            pltpu.SemaphoreType.DMA((count - 1, blocks)),
            pltpu.SemaphoreType.DMA((count - 1, blocks)),
            pltpu.VMEM(pair_shape, BF16),
            *line_scratch(n_fwd, width),
        ],
        compiler_params=params(0),
        cost_estimate=cost(9 * 10**10, 10**8),
        name="forward_scan",
    )(x, g, segments, *weights)

    weights = (w_z, w_x, w_bc, wdt, norm_gain, out_gain, conv_x, conv_bc, *per_head)
    n_in = 13 + len(weights)
    bits = lax.axis_size("dp").bit_length() - 1
    unit = 8 << bits
    pack_rows = -(-(dt_rows(width) + slot_rows(inner)) // unit) * unit
    shared_rows = -(-((width + bcw) // LANES * 8) // unit) * unit
    kind = F32 if (width // 2 >> bits) % 16 else BF16
    xp, gz, gx, gbc, pack, shared, carry, gout, res_y, res_x = pl.pallas_call(
        functools.partial(backward_kernel, heads, count, pairs, n_fwd, n_bwd),
        grid=(blocks,),
        in_specs=[
            rows_spec(BLOCK, inner, last),
            rows_spec(BLOCK, inner, last),
            rows_spec(BLOCK, inner, last),
            rows_spec(BLOCK, inner, last),
            rows_spec(BLOCK, bcw, last),
            rows_spec(BLOCK, bcw, last),
            rows_spec(BLOCK, LANES, last),
            rows_spec(BLOCK, inner, last),
            pl.BlockSpec((PIECES, state_n, inner), lambda i: (last - i, 0, 0)),
            pl.BlockSpec((1, BLOCK), lambda i: (0, jnp.maximum(last - i - 1, 0))),
            pl.BlockSpec((1, BLOCK), lambda i: (0, last - i)),
            pl.BlockSpec((PIECES, 8, CHUNK), lambda i: (last - i, 0, 0)),
            rows_spec(BLOCK, width, last),
            *[anywhere] * 3,
            *[whole_spec(w) for w in weights[3:]],
            *[anywhere] * 7,
        ],
        out_specs=[
            pl.BlockSpec((PIECES * PER, 2, ROWS, width), lambda i: (last - i, 0, 0, 0)),
            *[anywhere] * 9,
        ],
        out_shape=[
            shape(pair_shape, BF16),
            shape((width, inner), BF16),
            shape((width, inner), BF16),
            shape((width, bcw), F32),
            shape((pack_rows, LANES), F32),
            shape((shared_rows, LANES), F32),
            carry_shape,
            shape((2 * inner, width // 2), BF16),
            res_shape,
            res_shape,
        ],
        scratch_shapes=[
            *[pltpu.VMEM(w.shape, BF16) for w in weights[:3]],
            pltpu.SemaphoreType.DMA((3,)),
            pltpu.VMEM((8, LANES), F32),
            pltpu.VMEM((LANES, width), BF16),
            pltpu.VMEM((2 * LANES, inner), BF16),
            pltpu.VMEM((BLOCK + 8, inner), F32),
            pltpu.VMEM((BLOCK + 8, bcw), F32),
            pltpu.VMEM((BLOCK + 8, 1), F32),
            pltpu.VMEM((state_n, inner), F32),
            pltpu.VMEM((BLOCK, inner), BF16),
            pltpu.VMEM((BLOCK, inner), BF16),
            pltpu.VMEM((BLOCK, LANES), BF16),
            pltpu.VMEM((BLOCK, bcw), BF16),
            pltpu.VMEM((width, inner), F32),
            pltpu.VMEM((width, inner), F32),
            pltpu.VMEM((bcw // LANES, width, LANES), F32),
            pltpu.VMEM((width, LANES), F32),
            pltpu.VMEM((8, width), F32),
            pltpu.VMEM((8, inner), F32),
            pltpu.VMEM((8, bcw), F32),
            pltpu.VMEM((8, LANES), F32),
            pltpu.VMEM((pack_rows, LANES), F32),
            pltpu.VMEM((shared_rows, LANES), F32),
            pltpu.VMEM((2, 256, inner), BF16),
            pltpu.SemaphoreType.DMA((4 + bcw // LANES,)),
            pltpu.VMEM(pair_shape, BF16),
            pltpu.SemaphoreType.DMA,
            *finals_scratch(width),
            *cube_scratch(2 * inner, width // 2, bits, BF16),
            *line_scratch(n_bwd, width),
        ],
        input_output_aliases={n_in + 5: 8, n_in + 6: 9},
        compiler_params=params(1),
        cost_estimate=cost(12 * 10**10, 10**8),
        name="backward_scan",
    )(z, p, xc, ys, pbc, bc, dtr, dn, st, segments, segments, scal, x, *weights, yp, x4, g4, carry, gout, res_y, res_x)

    left = pairs - (n_fwd + n_bwd - LAG * (count - 1))
    res_y, res_x, gz, gx, gbc, pack, shared = pl.pallas_call(
        functools.partial(line_kernel, count, pairs, n_fwd + n_bwd, rest),
        grid=(rest,),
        in_specs=[anywhere] * 3 + [whole_spec(norm_gain)] + [anywhere] * 8,
        out_specs=[anywhere] * 7,
        out_shape=[
            res_shape,
            res_shape,
            shape((width, inner), BF16),
            shape((width, inner), BF16),
            shape((width, bcw), kind),
            shape((pack_rows, LANES), F32),
            shape((shared_rows, LANES), F32),
        ],
        scratch_shapes=[
            pltpu.VMEM((left, 2, ROWS, width), BF16),
            pltpu.SemaphoreType.DMA,
            *finals_scratch(width),
            *cube_scratch(width, inner, bits, BF16),
            *cube_scratch(width, inner, bits, BF16),
            *cube_scratch(pack_rows, LANES, bits, F32),
            *cube_scratch(shared_rows, LANES, bits, F32),
            *cross_scratch(count, shared_rows >> bits, LANES, F32),
            *cube_scratch(width // 2, bcw, bits, F32),
            *cross_scratch(count, width // 2 >> bits, bcw, kind),
            *cube_scratch(width // 2, bcw, bits, F32),
            *cross_scratch(count, width // 2 >> bits, bcw, kind),
            *line_scratch(rest, width),
        ],
        input_output_aliases={10: 0, 11: 1},
        compiler_params=params(2),
        cost_estimate=cost(10**11, 3 * 10**8),
        name="line_sums",
    )(xp, x4, g4, norm_gain, carry, gz, gx, gbc, pack, shared, res_y, res_x)

    wide = width // blocks
    tall = inner // blocks
    outs = pl.pallas_call(
        functools.partial(finish_kernel, heads),
        grid=(blocks,),
        in_specs=[
            rows_spec(BLOCK, width),
            rows_spec(BLOCK, width),
            rows_spec(BLOCK, width),
            pl.BlockSpec((PIECES, 8, CHUNK), lambda i: (i, 0, 0)),
            rows_spec(wide, inner),
            rows_spec(wide, inner),
            rows_spec(tall, width // 2),
            pl.BlockSpec((tall, width // 2), lambda i: (i + blocks, 0)),
            rows_spec(wide, bcw),
            whole_spec(pack),
            whole_spec(shared),
        ],
        out_specs=[
            rows_spec(BLOCK, width),
            rows_spec(BLOCK, width),
            rows_spec(wide, inner),
            rows_spec(wide, inner),
            rows_spec(tall, width),
            rows_spec(wide, bcw),
            fixed_spec(heads, width),
            fixed_spec(width),
            fixed_spec(4, inner),
            fixed_spec(inner),
            fixed_spec(inner),
            fixed_spec(1, heads),
            fixed_spec(4, bcw),
            fixed_spec(bcw),
            fixed_spec(1, heads),
            fixed_spec(1, heads),
        ],
        out_shape=[
            shape((length, width), BF16),
            shape((length, width), BF16),
            shape((width, inner), F32),
            shape((width, inner), F32),
            shape((inner, width), F32),
            shape((width, bcw), F32),
            shape((heads, width), F32),
            shape((width,), F32),
            shape((4, inner), F32),
            shape((inner,), F32),
            shape((inner,), F32),
            shape((1, heads), F32),
            shape((4, bcw), F32),
            shape((bcw,), F32),
            shape((1, heads), F32),
            shape((1, heads), F32),
        ],
        compiler_params=pltpu.CompilerParams(vmem_limit_bytes=60 * 2**20, dimension_semantics=("arbitrary",)),
        name="finish",
    )(x, res_y.reshape(length, width), res_x.reshape(length, width), scal, gz, gx, gout, gout, gbc, pack, shared)
    result, grad_x, gz, gx, gout, grad_wbc, grad_wdt, ng, cx, bx, og, ds, cbc, bbc, dtb, al = outs
    return (
        result[None], grad_x[None], ng, gz, gx, grad_wbc, grad_wdt.T, cx, cbc, bx, bbc, dtb[0], al[0], ds[0],
        og, gout,
    )


def solution(mesh):
    tensor_last = P(None, "tensor")
    in_specs = (
        P("dp", None, None), P("dp", None), P("dp", None, None), P(), tensor_last, tensor_last, P(), tensor_last,
        tensor_last, P(), P("tensor"), P(), P("tensor"), P("tensor"), P("tensor"), P("tensor"), P("tensor", None),
    )
    out_specs = (
        P("dp", None, None), P("dp", None, None), P(), tensor_last, tensor_last, P(), tensor_last, tensor_last, P(),
        P("tensor"), P(), P("tensor"), P("tensor"), P("tensor"), P("tensor"), P("tensor", None),
    )
    return jax.shard_map(on_device, mesh=mesh, in_specs=in_specs, out_specs=out_specs, check_vma=False)
```

```python
import functools

import jax
import jax.numpy as jnp
from jax import lax
from jax.experimental import pallas as pl
from jax.experimental.pallas import tpu as pltpu
from jax.sharding import PartitionSpec as P

EPS = 1e-05
CHUNK = 128
BLOCK = 256
PIECES = BLOCK // CHUNK
LANES = 128
ROWS = CHUNK // 4
PER = CHUNK // (2 * ROWS)
LAG = 2
RING = 4
F32 = jnp.float32
BF16 = jnp.bfloat16
HIGHEST = lax.Precision.HIGHEST
MESH = pl.DeviceIdType.MESH


def dot(a, b, precision=None):
    return lax.dot_general(a, b, (((1,), (0,)), ((), ())), precision=precision, preferred_element_type=F32)


def dot_t(a, b):
    return lax.dot_general(a, b, (((1,), (1,)), ((), ())), preferred_element_type=F32)


def tdot(a, b):
    return lax.dot_general(a, b, (((0,), (0,)), ((), ())), preferred_element_type=F32)


def sigmoid(v):
    return 1.0 / (1.0 + jnp.exp(-v))


def softplus(v):
    e = jnp.exp(-jnp.abs(v))
    series = e * (1.0 - e * (0.5 - e * (1.0 / 3.0 - e * 0.25)))
    return jnp.maximum(v, 0.0) + jnp.where(e < 0.03, series, jnp.log(1.0 + e))


def iotas(rows, cols):
    return (
        lax.broadcasted_iota(jnp.int32, (rows, cols), 0),
        lax.broadcasted_iota(jnp.int32, (rows, cols), 1),
    )


def fill_expand(expand, heads):
    r, c = iotas(*expand.shape)
    expand[...] = (lax.rem(r, LANES) == c // (expand.shape[1] // heads)).astype(BF16)


def spread(columns, expand):
    high = columns.astype(BF16)
    low = (columns - high.astype(F32)).astype(BF16)
    return dot(jnp.concatenate([high, low], axis=1), expand[...])


def decays(la, seg_col, seg_row):
    r, c = iotas(CHUNK, CHUNK)
    cum = dot((r >= c).astype(F32), la, HIGHEST)
    visible = (r >= c) & (seg_col == seg_row)
    return cum, cum.T, visible


def decay_matrix(cum, cum_t, visible, head):
    gap = cum[:, head : head + 1] - cum_t[head : head + 1, :]
    return jnp.exp(jnp.where(visible, gap, -1e30))


def split_pair(values):
    low = lax.broadcasted_iota(jnp.int32, values.shape, 1) < LANES // 2
    zero = jnp.zeros_like(values)
    return jnp.where(low, values, zero), jnp.where(low, zero, values)


def conv_taps(hist, weight, same, rows):
    out = hist[8 : 8 + rows, :] * weight[3:4, :]
    for k in range(1, 4):
        out = out + hist[8 - k : 8 - k + rows, :] * same[k - 1] * weight[3 - k : 4 - k, :]
    return out


def columns_of(segr_ref):
    rows = segr_ref.shape[1]
    pieces = []
    for at in range(0, rows, LANES):
        row = segr_ref[:, at : at + LANES].astype(F32)
        pieces.append(jnp.broadcast_to(row, (LANES, LANES)).T[:, 0:1])
    return jnp.concatenate(pieces, axis=0)


def fill_heads(hv, wdt_s, dtb_ref, al_ref, dsk_ref, wdt_ref):
    heads = wdt_ref.shape[0]
    hv[...] = jnp.zeros_like(hv)
    for j, ref in enumerate((dtb_ref, al_ref, dsk_ref)):
        hv[j : j + 1, 0:heads] = ref[...]
    wdt_s[...] = jnp.zeros_like(wdt_s)
    wdt_s[0:heads, :] = wdt_ref[...]


def row_of(ref):
    return ref[...].reshape(1, ref.shape[0])


def inverse_rms(tokens):
    return lax.rsqrt(jnp.sum(tokens * tokens, axis=1, keepdims=True) * (1.0 / tokens.shape[1]) + EPS)


def bring(src, dst, sem):
    copy = pltpu.make_async_copy(src, dst, sem)
    copy.start()
    copy.wait()


def hello(peers, dp_peers=()):
    barrier = pltpu.get_barrier_semaphore()
    for peer in dp_peers:
        pl.semaphore_signal(barrier, inc=1, device_id={"dp": peer}, device_id_type=MESH)
    for peer, there in peers:

        @pl.when(there)
        def _():
            pl.semaphore_signal(barrier, inc=1, device_id={"tensor": peer}, device_id_type=MESH)


def heard(peers, dp_peers=()):
    total = jnp.int32(len(dp_peers))
    for _, there in peers:
        total = total + there.astype(jnp.int32)
    pl.semaphore_wait(pltpu.get_barrier_semaphore(), total)


def neighbours(count):
    me = lax.axis_index("tensor")
    return [(me - 1, me > 0), (me + 1, me < count - 1)]


class Line:
    def __init__(self, count, pairs, first, steps, refs, source, finals=None):
        self.count, self.pairs, self.first, self.steps = count, pairs, first, steps
        self.source, self.finals = source, finals
        (self.res_y, self.res_x, self.land, self.send) = refs[:4]
        (self.red_out, self.red_in, self.bc_out, self.bc_in, self.local) = refs[4:]

    def to_result(self, k, q, act):
        half = self.pairs // 2

        @pl.when(k < half)
        def _():
            act(self.res_y.at[k, q])

        @pl.when(k >= half)
        def _():
            act(self.res_x.at[2 * half - 1 - k, q])

    def flow(self, q):
        me = lax.axis_index("tensor")
        if q == 0:
            return me, me - 1, me + 1
        return self.count - 1 - me, me + 1, me - 1

    def is_pair(self, i):
        return (i >= 0) & (i < self.pairs)

    def red(self, q, ls, toward, src):
        return pltpu.make_async_remote_copy(
            src_ref=src, dst_ref=self.land.at[ls + LAG, q], send_sem=self.red_out.at[q, ls],
            recv_sem=self.red_in.at[q, ls], device_id={"tensor": toward}, device_id_type=MESH,
        )

    def cast(self, q, ls, away, src, there):
        return pltpu.make_async_remote_copy(
            src_ref=src, dst_ref=there, send_sem=self.bc_out.at[q, ls],
            recv_sem=self.bc_in.at[q, ls], device_id={"tensor": away}, device_id_type=MESH,
        )

    def hold(self, q, ls):
        return self.send.at[lax.rem(ls, LAG), q]

    def keep(self, q, ls, there):
        return pltpu.make_async_copy(self.hold(q, ls), there, self.local.at[lax.rem(ls, LAG), q])

    def term(self, s, z):
        return s - LAG * (self.count - 1 - z)

    def back(self, s, z):
        return s - LAG * (self.count - 1 + z)

    def finish_red(self, q, s, ls):
        z, toward, away = self.flow(q)
        n = self.count
        i = self.term(s, z)

        @pl.when(self.is_pair(i) & (z > 0))
        def _():
            self.red(q, ls, toward, self.hold(q, ls)).wait_send()

        @pl.when(self.is_pair(i) & (z == 0))
        def _():
            self.cast(q, ls, away, self.hold(q, ls), self.res_y.at[0, q]).wait_send()
            self.keep(q, ls, self.res_y.at[0, q]).wait()

        @pl.when(self.is_pair(i + LAG) & (z < n - 1))
        def _():
            self.red(q, ls, toward, self.hold(q, ls)).wait_recv()

    def finish_cast(self, q, s, ls):
        z, _, away = self.flow(q)
        n = self.count
        k = self.back(s, z)

        @pl.when(self.is_pair(k) & (z > 0) & (z < n - 1))
        def _():
            self.cast(q, ls, away, self.res_y.at[0, q], self.res_y.at[0, q]).wait_send()

        @pl.when(self.is_pair(k + LAG) & (z > 0))
        def _():
            self.cast(q, ls, away, self.res_y.at[0, q], self.res_y.at[0, q]).wait_recv()

    def step(self, ls):
        n = self.count
        ls = jnp.int32(ls)
        s = self.first + ls
        for q in range(2):

            @pl.when(ls >= LAG)
            def _():
                self.finish_cast(q, s - LAG, ls - LAG)

            z, toward, away = self.flow(q)
            k = self.back(s, z)

            @pl.when(self.is_pair(k) & (z > 0) & (z < n - 1))
            def _():
                self.to_result(k, q, lambda there: self.cast(q, ls, away, there, there).start())

        for q in range(2):
            z, toward, away = self.flow(q)
            i = self.term(s, z)

            @pl.when(ls >= LAG)
            def _():
                self.finish_red(q, s - LAG, ls - LAG)

            @pl.when(self.is_pair(i))
            def _():
                mine = self.source(q, i)
                place = lax.rem(ls, LAG)

                @pl.when(z == n - 1)
                def _():
                    self.red(q, ls, toward, mine).start()

                @pl.when((z > 0) & (z < n - 1))
                def _():
                    self.send[place, q] = (mine[...].astype(F32) + self.land[ls, q].astype(F32)).astype(BF16)
                    self.red(q, ls, toward, self.hold(q, ls)).start()

                @pl.when(z == 0)
                def _():
                    total = mine[...].astype(F32) + self.land[ls, q].astype(F32)
                    if self.finals is None:
                        self.send[place, q] = total.astype(BF16)
                    else:
                        self.finals.last(q, i, total, self.hold(q, ls))

                    def give(there):
                        self.cast(q, ls, away, self.hold(q, ls), there).start()
                        self.keep(q, ls, there).start()

                    self.to_result(i, q, give)
                    if self.finals is not None:

                        @pl.when(ls + 1 < self.steps)
                        def _():
                            self.finals.fetch(q, i + 1)

    def held(self, q, s):
        z, _, _ = self.flow(q)
        return self.is_pair(self.term(s, z)) & (z < self.count - 1)

    def each_held(self, s, src, act):
        for q in range(2):
            for d in range(LAG):

                @pl.when(self.held(q, s + d))
                def _():
                    act(pltpu.make_async_copy(*src(d, q), self.local.at[d, q]))

    def open(self, carry):
        self.each_held(self.first, lambda d, q: (carry.at[d, q], self.land.at[d, q]), lambda copy: copy.start())
        for q in range(2):
            z, _, _ = self.flow(q)

            @pl.when(z == 0)
            def _():
                self.finals.fetch(q, jnp.int32(self.first - LAG * (self.count - 1)))

    def opened(self, carry):
        self.each_held(self.first, lambda d, q: (carry.at[d, q], self.land.at[d, q]), lambda copy: copy.wait())

    def close(self, carry):
        for d in range(LAG):
            ls = self.steps - LAG + d
            for q in range(2):
                self.finish_cast(q, self.first + ls, jnp.int32(ls))
                self.finish_red(q, self.first + ls, jnp.int32(ls))
        if carry is None:
            return
        left = (self.first + self.steps, lambda d, q: (self.land.at[self.steps + d, q], carry.at[d, q]))
        self.each_held(*left, lambda copy: copy.start())
        self.each_held(*left, lambda copy: copy.wait())


def line_scratch(steps, width):
    return [
        pltpu.VMEM((steps + LAG, 2, ROWS, width), BF16),
        pltpu.VMEM((LAG, 2, ROWS, width), BF16),
        pltpu.SemaphoreType.DMA((2, steps)),
        pltpu.SemaphoreType.DMA((2, steps)),
        pltpu.SemaphoreType.DMA((2, steps)),
        pltpu.SemaphoreType.DMA((2, steps)),
        pltpu.SemaphoreType.DMA((LAG, 2)),
    ]


class Finals:
    def __init__(self, pairs, x_any, g_any, gain, rows, sems):
        self.pairs, self.half, self.x_any, self.g_any, self.gain, self.rows, self.sems = (
            pairs, pairs // 2, x_any, g_any, gain, rows, sems,
        )

    def copies(self, q, i):
        b = 2 * self.half - 1 - i
        return [
            pltpu.make_async_copy(src.at[b, q], self.rows.at[q, j], self.sems.at[q, j])
            for j, src in enumerate((self.x_any, self.g_any))
        ]

    def fetch(self, q, i):
        @pl.when((i >= self.half) & (i < self.pairs))
        def _():
            for copy in self.copies(q, i):
                copy.start()

    def last(self, q, i, total, out):
        @pl.when(i < self.half)
        def _():
            out[...] = total.astype(BF16)

        @pl.when(i >= self.half)
        def _():
            for copy in self.copies(q, i):
                copy.wait()
            x = self.rows[q, 0].astype(F32)
            r1 = inverse_rms(x)
            scaled = total * self.gain
            across = jnp.sum(scaled * x, axis=1, keepdims=True) * (1.0 / x.shape[1])
            out[...] = (self.rows[q, 1].astype(F32) + r1 * scaled - x * (r1 * r1 * r1 * across)).astype(BF16)


def finals_scratch(width):
    return [pltpu.VMEM((2, 2, ROWS, width), BF16), pltpu.SemaphoreType.DMA((2, 2))]


def dp_bits():
    me = lax.axis_index("dp")
    bits = []
    for b in range(lax.axis_size("dp").bit_length() - 1):
        bit = lax.rem(me // 2**b, 2)
        bits.append((bit, me + (1 - 2 * bit) * 2**b))
    return bits


class Cube:
    def __init__(self, order, refs, across=None):
        self.order, self.across = order, across
        (self.src, self.out, self.total, self.send, self.land, self.out_sem, self.in_sem, self.local) = refs
        self.rows = self.src.shape[0]
        self.bits = dp_bits()
        self.events = 2 * len(order) + (1 if across is None else 2)

    def start_of(self, depth):
        at = 0
        for j in range(depth):
            at = at + self.bits[self.order[j]][0] * (self.rows >> (j + 1))
        return at

    def span(self, at, size):
        return pl.ds(pl.multiple_of(at, 8 if self.src.dtype == F32 else 16), size)

    def inside(self, depth):
        return self.start_of(depth) - self.start_of(1)

    def own_half(self):
        mine = self.src.at[self.span(self.start_of(1), self.rows // 2), :]
        return pltpu.make_async_copy(mine, self.send.at[pl.ds(0, self.rows // 2), :], self.local)

    def halving(self, j):
        size = self.rows >> (j + 1)
        bit, partner = self.bits[self.order[j]]
        theirs = self.start_of(j) + (1 - bit) * size
        src = self.src.at[self.span(theirs, size), :] if j == 0 else self.send.at[pl.ds(0, size), :]
        return pltpu.make_async_remote_copy(
            src_ref=src, dst_ref=self.land.at[pl.ds(self.rows - 2 * size, size), :], send_sem=self.out_sem.at[j],
            recv_sem=self.in_sem.at[j], device_id={"dp": partner}, device_id_type=MESH,
        )

    def doubling(self, j):
        count = len(self.order)
        size = self.rows >> (count - j)
        _, partner = self.bits[self.order[count - 1 - j]]
        mine = self.out.at[self.span(self.start_of(count - j), size), :]
        return pltpu.make_async_remote_copy(
            src_ref=mine, dst_ref=mine, send_sem=self.out_sem.at[count + j], recv_sem=self.in_sem.at[count + j],
            device_id={"dp": partner}, device_id_type=MESH,
        )

    def crossing(self, d):
        mine, land, out_sem, in_sem, peers = self.across
        return pltpu.make_async_remote_copy(
            src_ref=mine, dst_ref=land.at[d], send_sem=out_sem.at[d - 1],
            recv_sem=in_sem.at[d - 1], device_id={"tensor": peers[d - 1]}, device_id_type=MESH,
        )

    def turn(self, part):
        count = len(self.order)
        size = self.rows >> count
        bring(part, self.out.at[self.span(self.start_of(count), size), :], self.local)
        self.doubling(0).start()

    def event(self, e):
        count = len(self.order)
        if e == 0:
            self.halving(0).start()
            self.own_half().start()
            return
        if e <= count:
            if e == 1:
                self.own_half().wait()
            self.halving(e - 1).wait()
            size = self.rows >> e
            at = self.inside(e)
            for r in range(0, size, 192):
                tile = min(192, size - r)
                landed = self.land[self.rows - 2 * size + r : self.rows - 2 * size + r + tile, :].astype(F32)
                here = self.span(at + r, tile)
                if e == 1:
                    self.total[here, :] = self.send[r : r + tile, :].astype(F32) + landed
                else:
                    self.total[here, :] = self.total[here, :] + landed
            if e < count:
                bit, _ = self.bits[self.order[e]]
                at = at + (1 - bit) * (size // 2)
                size = size // 2
            part = self.total[self.span(at, size), :]
            if e == count and self.across is not None:
                self.across[0][...] = part.astype(self.across[0].dtype)
                for d in range(1, len(self.across[4]) + 1):
                    self.crossing(d).start()
                return
            self.send[0:size, :] = part.astype(self.send.dtype)
            if e < count:
                self.halving(e).start()
            else:
                self.turn(self.send.at[pl.ds(0, size), :])
            return
        if self.across is not None:
            if e == count + 1:
                mine, land, _, _, peers = self.across
                ranks = len(peers) + 1
                for d in range(1, ranks):
                    self.crossing(d).wait()
                land[0] = mine[...]
                me = lax.axis_index("tensor")
                total = land[me].astype(F32)
                for rank in range(1, ranks):
                    total = total + land[lax.rem(me - rank + ranks, ranks)].astype(F32)
                mine[...] = total.astype(mine.dtype)
                self.turn(mine)
                return
            e = e - 1
        self.doubling(e - count - 1).wait()
        if e < 2 * count:
            self.doubling(e - count).start()


def cube_scratch(rows, cols, bits, dtype):
    return [
        pltpu.VMEM((rows // 2, cols), F32),
        pltpu.VMEM((rows // 2, cols), dtype),
        pltpu.VMEM((rows - (rows >> bits), cols), dtype),
        pltpu.SemaphoreType.DMA((2 * bits,)),
        pltpu.SemaphoreType.DMA((2 * bits,)),
        pltpu.SemaphoreType.DMA,
    ]


def cross_scratch(count, rows, cols, dtype):
    return [
        pltpu.VMEM((rows, cols), dtype),
        pltpu.VMEM((count, rows, cols), dtype),
        pltpu.SemaphoreType.DMA((count - 1,)),
        pltpu.SemaphoreType.DMA((count - 1,)),
    ]


def tensor_peers(count):
    me = lax.axis_index("tensor")
    return [lax.rem(me + d, count) for d in range(1, count)]


def line_kernel(
    count, pairs, first, steps, xp_ref, x_any, g_any, ng_ref, carry_ref, gz_ref, gx_ref, gb_ref, pk_ref, sh_ref, res_y_in, res_x_in,
    res_y, res_x, oz_ref, ox_ref, ob_ref, op_ref, os_ref, part, part_sem, rows, sems, *scratch,
):
    del res_y_in, res_x_in
    half = pairs // 2
    order = list(range(len(dp_bits())))
    other = order[:1] + order[:0:-1]
    peers = tensor_peers(count)
    cubes = [
        Cube(order, (gz_ref, oz_ref, *scratch[0:6])),
        Cube(other, (gx_ref, ox_ref, *scratch[6:12])),
        Cube(order, (pk_ref, op_ref, *scratch[12:18])),
        Cube(order, (sh_ref, os_ref, *scratch[18:24]), (*scratch[24:28], peers)),
    ]
    tall = gb_ref.shape[0] // 2
    for j, way in enumerate((order, other)):
        rows_j = pl.ds(j * tall, tall)
        refs = scratch[28 + 10 * j : 38 + 10 * j]
        cubes.append(Cube(way, (gb_ref.at[rows_j, :], ob_ref.at[rows_j, :], *refs[0:6]), (*refs[6:10], peers)))

    finals = Finals(pairs, x_any, g_any, row_of(ng_ref), rows, sems)
    line = Line(
        count, pairs, first, steps, (res_y, res_x, *scratch[48:]), lambda q, i: part.at[2 * half - 1 - i, q], finals
    )
    at = pl.program_id(0)

    @pl.when(at == 0)
    def _():
        terms = pltpu.make_async_copy(xp_ref.at[pl.ds(0, part.shape[0])], part, part_sem)
        everyone = [(peer, peer >= 0) for peer in peers], [partner for _, partner in dp_bits()]
        hello(*everyone)
        terms.start()
        line.open(carry_ref)
        line.opened(carry_ref)
        terms.wait()
        heard(*everyone)

    if len(order) == 3:
        first_times, other_times = [0, 2, 6, 8, 10, 14, 16], [0, 3, 7, 9, 11, 15, 17]
        across_times = [0, 4, 8, 9, 12, 15, 16, 17]
    else:
        first_times = other_times = across_times = range(2 * len(order) + 2)
    for cube in cubes:
        when = other_times if cube is cubes[1] else first_times
        if cube.across is not None:
            when = across_times
        for e in range(cube.events):

            @pl.when(at == min(when[e], steps - 1))
            def _():
                cube.event(e)

    line.step(at)

    @pl.when(at == steps - 1)
    def _():
        line.close(None)


def finish_kernel(
    heads, x_ref, y_ref, dx_ref, scal_ref, gz_ref, gx_ref, go_ref, go2_ref, gb_ref, pack_ref, shared_ref,
    yo_ref, xo_ref, oz_ref, ox_ref, oo_ref, wbc_ref, wdt_ref, ng_ref, cx_ref, bx_ref, og_ref, ds_ref, cbc_ref, bbc_ref,
    dtb_ref, al_ref,
):
    inner = cx_ref.shape[1]
    width, bcw = x_ref.shape[1], wbc_ref.shape[1]
    for piece in range(x_ref.shape[0] // CHUNK):
        span = slice(piece * CHUNK, (piece + 1) * CHUNK)
        r2 = jnp.concatenate([scal_ref[piece], jnp.zeros((CHUNK - 8, CHUNK), F32)], axis=0).T[:, 0:1]
        yo_ref[span, :] = (x_ref[span, :].astype(F32) + r2 * y_ref[span, :].astype(F32)).astype(BF16)
    xo_ref[...] = dx_ref[...]
    oz_ref[...] = gz_ref[...].astype(F32)
    ox_ref[...] = gx_ref[...].astype(F32)
    oo_ref[:, 0 : width // 2] = go_ref[...].astype(F32)
    oo_ref[:, width // 2 :] = go2_ref[...].astype(F32)
    wbc_ref[...] = gb_ref[...].astype(F32)

    @pl.when(pl.program_id(0) == 0)
    def _():
        for j in range(width // LANES):
            wdt_ref[:, j * LANES : (j + 1) * LANES] = pack_ref[16 * j : 16 * j + 16, :][0:heads, :]

        def put(ref, row):
            ref[...] = row.reshape(ref.shape)

        def side_by_side(ref, at, pieces, rows=8):
            return jnp.concatenate([ref[at + 8 * j : at + 8 * j + rows, :] for j in range(pieces)], axis=1)

        put(ng_ref, side_by_side(shared_ref, 0, width // LANES, 1))
        rows = side_by_side(shared_ref, width // LANES * 8, bcw // LANES)
        cbc_ref[...] = rows[0:4, :]
        put(bbc_ref, rows[4:5, :])
        rows = side_by_side(pack_ref, dt_rows(width), inner // LANES)
        cx_ref[...] = rows[0:4, :]
        put(bx_ref, rows[4:5, :])
        put(og_ref, rows[6:7, :])
        lane = lax.broadcasted_iota(jnp.int32, (1, heads), 1)
        skip = jnp.zeros((1, heads), F32)
        for h in range(heads):
            head = jnp.sum(rows[5:6, h * 64 : h * 64 + 64], axis=1, keepdims=True)
            skip = jnp.where(lane == h, head, skip)
        ds_ref[...] = skip
        at = dt_rows(width) + inner // LANES * 8
        rows = pack_ref[at : at + 8, :]
        dtb_ref[...] = rows[0:1, 0:heads]
        al_ref[...] = rows[1:2, 0:heads]


def forward_kernel(
    heads, count, pairs, steps, blocks,
    x_ref, g_ref, segr_ref, wz_any, wx_ref, wbc_ref, wdt_ref, wo_any, ng_ref, bx_ref, og_ref, bbc_ref, cx_ref, cbc_ref,
    dtb_ref, al_ref, dsk_ref,
    z_ref, p_ref, xc_ref, ys_ref, pbc_ref, bc_ref, dtr_ref, dn_ref, st_ref, yp_ref, scal_ref, wout_ref,
    carry_out, res_y, res_x,
    wz_ref, wo_ref, w_sem, hv_ref, wdt_s, expand, hist, hist_bc, segs, state, scaled_s, g_s, acc_out, stat_mine, stat_land, stat_out, stat_in, part, *scratch,
):
    rows, width = x_ref.shape
    inner = z_ref.shape[1]
    block = pl.program_id(0)
    me = lax.axis_index("tensor")
    ng, bx, og, bbc = row_of(ng_ref), row_of(bx_ref), row_of(og_ref), row_of(bbc_ref)

    line = Line(count, pairs, 0, steps, (res_y, res_x, *scratch), lambda q, i: part.at[i, q])

    load_z = pltpu.make_async_copy(wz_any, wz_ref, w_sem.at[0])
    load = pltpu.make_async_copy(wo_any, wo_ref, w_sem.at[1])
    everyone = [(peer, peer >= 0) for peer in tensor_peers(count)]

    @pl.when(block == 0)
    def _():
        hello(everyone)
        load_z.start()
        load.start()
        fill_heads(hv_ref, wdt_s, dtb_ref, al_ref, dsk_ref, wdt_ref)
        fill_expand(expand, heads)
        hist[0:8, :] = jnp.zeros((8, hist.shape[1]), F32)
        hist_bc[0:8, :] = jnp.zeros((8, hist_bc.shape[1]), F32)
        segs[0:8, :] = jnp.full((8, 1), -1.0, F32)
        state[...] = jnp.zeros_like(state)
        acc_out[...] = jnp.zeros_like(acc_out)

    x = x_ref[...].astype(F32)
    xn = (x * inverse_rms(x) * ng).astype(BF16)
    xc = dot(xn, wx_ref[...])
    bc = dot(xn, wbc_ref[...])
    dtr = dot_t(xn, wdt_s[...])
    xc_ref[...] = xc.astype(BF16)
    bc_ref[...] = bc
    dtr_ref[...] = dtr
    seg_all = columns_of(segr_ref)
    segs[8 : 8 + rows, :] = seg_all
    hist[8 : 8 + rows, :] = xc
    hist_bc[8 : 8 + rows, :] = bc
    same = [(segs[8 - k : 8 - k + rows, :] == seg_all).astype(F32) for k in range(1, 4)]
    p_ref[...] = conv_taps(hist, cx_ref, same, rows) + bx
    pbc_ref[...] = conv_taps(hist_bc, cbc_ref, same, rows) + bbc
    @pl.when(block == 0)
    def _():
        load_z.wait()

    z_ref[...] = dot(xn, wz_ref[...])
    g = g_ref[...]
    g_s[lax.rem(block, RING)] = g
    dt_all = softplus(dtr + hv_ref[0:1, :])
    la_all = -jnp.exp(hv_ref[1:2, :]) * dt_all
    dsk = spread(hv_ref[...], expand)[2:3, :]
    row_i, lane_i = iotas(CHUNK, LANES)
    squares = []
    for piece in range(PIECES):
        at = pl.ds(piece * CHUNK, CHUNK)
        span = slice(piece * CHUNK, (piece + 1) * CHUNK)
        seg_col = seg_all[span, :]
        keep = (seg_col == segs[7 + piece * CHUNK : 8 + piece * CHUNK, :]).astype(F32)
        tail = (seg_col == seg_col[CHUNK - 1 : CHUNK, :]).astype(F32)
        dt = dt_all[span, :]
        cum, cum_t, visible = decays(la_all[span, :], seg_col, segr_ref[:, span].astype(F32))
        p = p_ref[at, :]
        u = p * sigmoid(p)
        pbc = pbc_ref[at, :]
        bcu = (pbc * sigmoid(pbc)).astype(BF16)
        n = bcu.shape[1] // 2
        b, c = bcu[:, :n], bcu[:, n:]
        scores = dot_t(c, b)
        last = cum[CHUNK - 1 : CHUNK, :]
        flows = [dt, jnp.exp(cum) * keep, jnp.exp(last - cum) * tail]
        flows.append(jnp.broadcast_to(jnp.exp(last) * keep[CHUNK - 1 : CHUNK, :], (8, LANES)))
        wide = spread(jnp.concatenate(flows, axis=0), expand)
        dt_x, enter_x, end_x = (wide[k * CHUNK : (k + 1) * CHUNK, :] for k in range(3))
        carry = wide[3 * CHUNK : 3 * CHUNK + 1, :]
        v = dt_x * u
        v_low = v.astype(BF16)
        pieces = []
        for pair in range(heads // 2):
            mats = [
                (scores * decay_matrix(cum, cum_t, visible, 2 * pair + k)).astype(BF16)
                for k in range(2)
            ]
            halves = split_pair(v_low[:, pair * LANES : (pair + 1) * LANES])
            pieces.append(dot(jnp.concatenate(mats, axis=1), jnp.concatenate(halves, axis=0)))
        if piece:

            @pl.when(block < 2)
            def _():
                line.step(4 * block + 1)

        inside = jnp.concatenate(pieces, axis=1)
        old = state[...]
        old_low = old.astype(BF16)
        st_ref[piece] = old_low
        entering = dot(c, old_low) * enter_x
        state[...] = old * carry + tdot(b, (end_x * v).astype(BF16))
        ys = inside + entering + dsk * u
        ys_ref[at, :] = ys
        z = z_ref[at, :]
        gated = ys * (z * sigmoid(z))
        scaled = gated * og
        scaled_s[lax.rem(block, RING), at, :] = scaled
        if piece == 0:

            @pl.when(block == 0)
            def _():
                heard(everyone)
                load.wait()

        y_part = dot(scaled.astype(BF16), wo_ref[...]).astype(BF16)
        for r in range(PER):
            for q in range(2):
                low = y_part[(2 * r + q) * ROWS : (2 * r + q + 1) * ROWS, :]
                yp_ref[piece * PER + r, q] = low
                part[(block * PIECES + piece) * PER + r, q] = low

        later = jnp.where(block < 4, 3 * block + 2 + piece, 2 * block + 6 + piece)
        line.step(jnp.where(block < 2, 4 * block + 2 * piece, later))

        squares.append(jnp.sum(gated * gated, axis=1, keepdims=True))

    dn = dot_t(g, wo_ref[...])
    dn_ref[...] = dn
    for piece in range(PIECES):
        span = slice(piece * CHUNK, (piece + 1) * CHUNK)
        across = jnp.sum(dn[span, :] * scaled_s[lax.rem(block, RING), span, :], axis=1, keepdims=True)
        both = jnp.where(lane_i == 0, squares[piece], jnp.where(lane_i == 1, across, 0.0))
        stat_mine[block, piece] = both.T[0:8, :]
    hist[0:8, :] = hist[rows : rows + 8, :]
    hist_bc[0:8, :] = hist_bc[rows : rows + 8, :]
    segs[0:8, :] = segs[rows : rows + 8, :]

    def stat_copy(d, b):
        return pltpu.make_async_remote_copy(
            src_ref=stat_mine.at[b], dst_ref=stat_land.at[d, b], send_sem=stat_out.at[d - 1, b],
            recv_sem=stat_in.at[d - 1, b], device_id={"tensor": lax.rem(me + d, count)}, device_id_type=MESH,
        )

    def settle(pair):
        low, up = [], []
        for b in (pair, pair + 1):
            for d in range(1, count):
                stat_copy(d, b).wait()
            stat_land[0, b] = stat_mine[b]
            total = stat_land[me, b]
            for rank in range(1, count):
                total = total + stat_land[lax.rem(me - rank + count, count), b]
            place = lax.rem(b, RING)
            for piece in range(PIECES):
                r2 = lax.rsqrt(total[piece, 0:1, :] * (1.0 / (inner * count)) + EPS)
                k2 = r2 * r2 * r2 * (total[piece, 1:2, :] * (1.0 / (inner * count)))
                both = jnp.where(row_i == 0, r2, jnp.where(row_i == 1, k2, 0.0))
                scal_ref[b * PIECES + piece] = both[0:8, :]
                low.append((scaled_s[place, piece * CHUNK : (piece + 1) * CHUNK, :] * both.T[:, 0:1]).astype(BF16))
            up.append(g_s[place])
        normed = jnp.concatenate(low, axis=0)
        up = jnp.concatenate(up, axis=0)
        for c in range(0, inner, 256):
            acc_out[c : c + 256, :] += tdot(normed[:, c : c + 256], up)

    for d in range(1, count):
        stat_copy(d, block).start()

    @pl.when(block < 4)
    def _():
        line.step(jnp.where(block < 2, 4 * block + 3, 3 * block + 4))

    @pl.when((block >= RING - 1) & (lax.rem(block, 2) == 1))
    def _():
        settle(block - (RING - 1))

    @pl.when(block == blocks - 1)
    def _():
        settle(blocks - 2)
        for c in range(0, inner, 256):
            low = acc_out[c : c + 256, :].astype(BF16)
            wout_ref[c : c + 256, :] = low[:, 0 : width // 2]
            wout_ref[inner + c : inner + c + 256, :] = low[:, width // 2 :]
        line.close(carry_out)


def backward_kernel(
    heads, count, pairs, first, steps,
    z_ref, p_ref, xc_ref, ys_ref, pbc_ref, bc_ref, dtr_ref, dn_ref, st_ref, segp_ref, segr_ref, scal_ref, x_ref,
    wz_any, wx_any, wbc_any, wdt_ref, ng_ref, og_ref, cx_ref, cbc_ref, dtb_ref, al_ref, dsk_ref, y_ref, x_any, g_any, carry_ref, go_ref, res_y_in, res_x_in,
    xp_ref, gz_ref, gx_ref, gb_ref, pack_ref, shared_ref, carry_out, go_sum, res_y, res_x,
    wz_ref, wx_ref, wbc_ref, w_sem, hv_ref, wdt_s, expand, ahead, ahead_bc, segs, d_state, dz_s, dx_s, ddt_s, dbc_s, acc_z, acc_x, acc_bc, acc_dt,
    a1536, a768, a256, a128, rest, shared, stage, stage_sem, part, part_sem, rows_s, rows_sem, *scratch,
):
    del res_y_in, res_x_in
    rows, inner = z_ref.shape
    width = x_ref.shape[1]
    block = pl.program_id(0)
    blocks = steps // (PIECES * PER)
    half = pairs // 2
    me = lax.axis_index("tensor")
    ng, og = row_of(ng_ref), row_of(og_ref)

    finals = Finals(pairs, x_any, g_any, ng, rows_s, rows_sem)
    line = Line(
        count, pairs, first, steps, (res_y, res_x, *scratch[6:]), lambda q, i: part.at[lax.rem(i, half), q], finals
    )
    loads = [
        pltpu.make_async_copy(src, dst, w_sem.at[j])
        for j, (src, dst) in enumerate(((wz_any, wz_ref), (wx_any, wx_ref), (wbc_any, wbc_ref)))
    ]
    cube = Cube(list(range(len(dp_bits()))), (go_ref, go_sum, *scratch[0:6]))
    old = first - LAG * (count - 1)

    @pl.when(block == 0)
    def _():
        terms = pltpu.make_async_copy(y_ref.at[pl.ds(old, half - old)], part.at[pl.ds(old, half - old)], part_sem)
        everyone = neighbours(count), [partner for _, partner in dp_bits()]
        hello(*everyone)
        terms.start()
        line.open(carry_ref)
        for load in loads:
            load.start()
        line.opened(carry_ref)
        terms.wait()
        heard(*everyone)
        line.step(0)
        fill_heads(hv_ref, wdt_s, dtb_ref, al_ref, dsk_ref, wdt_ref)
        fill_expand(expand, heads)
        ahead[rows : rows + 8, :] = jnp.zeros((8, ahead.shape[1]), F32)
        ahead_bc[rows : rows + 8, :] = jnp.zeros((8, ahead_bc.shape[1]), F32)
        segs[rows : rows + 8, :] = jnp.full((8, 1), -1.0, F32)
        for ref in (d_state, acc_z, acc_x, acc_bc, acc_dt, a1536, a768, a256, a128, rest, shared):
            ref[...] = jnp.zeros_like(ref)

    @pl.when(block > 0)
    def _():
        line.step(4 * block)

    seg_all = columns_of(segr_ref)
    segs[0:rows, :] = seg_all
    before = jnp.where(block == blocks - 1, -1.0, segp_ref[:, rows - 1 : rows].astype(F32))
    r, c_ = iotas(CHUNK, CHUNK)
    both_ways = jnp.concatenate([(r <= c_).astype(F32), (r > c_).astype(F32)], axis=1)
    all_r, all_l = iotas(heads * CHUNK, LANES)
    pick = (all_r // CHUNK == all_l).astype(BF16)
    decay_rate = -jnp.exp(hv_ref[1:2, :])
    dsk = spread(hv_ref[...], expand)[2:3, :]
    for piece in reversed(range(PIECES)):
        at = pl.ds(piece * CHUNK, CHUNK)
        span = slice(piece * CHUNK, (piece + 1) * CHUNK)
        seg_col = seg_all[span, :]
        prev = seg_all[piece * CHUNK - 1 : piece * CHUNK, :] if piece else before
        keep = (seg_col == prev).astype(F32)
        tail = (seg_col == seg_col[CHUNK - 1 : CHUNK, :]).astype(F32)
        scal = jnp.concatenate([scal_ref[piece], jnp.zeros((CHUNK - 8, CHUNK), F32)], axis=0).T
        r2 = scal[:, 0:1]
        k2 = scal[:, 1:2]
        pre = dtr_ref[at, :] + hv_ref[0:1, :]
        dt = softplus(pre)
        la = decay_rate * dt
        cum, cum_t, visible = decays(la, seg_col, segr_ref[:, span].astype(F32))
        z = z_ref[at, :]
        ys = ys_ref[at, :]
        sz = sigmoid(z)
        silu = z * sz
        gated = ys * silu
        dn = dn_ref[at, :]
        d_gated = r2 * og * dn - gated * k2
        a768[6:7, :] += jnp.sum(dn * gated * r2, axis=0, keepdims=True)
        dz_s[at, :] = (d_gated * ys * (sz * (1.0 + z * (1.0 - sz)))).astype(BF16)
        dy = d_gated * silu
        dy_low = dy.astype(BF16)
        p = p_ref[at, :]
        sp = sigmoid(p)
        u = p * sp
        a768[5:6, :] += jnp.sum(dy * u, axis=0, keepdims=True)
        pbc = pbc_ref[at, :]
        spbc = sigmoid(pbc)
        bcu = (pbc * spbc).astype(BF16)
        n = bcu.shape[1] // 2
        b, c = bcu[:, :n], bcu[:, n:]
        scores = dot_t(c, b)
        last = cum[CHUNK - 1 : CHUNK, :]
        flows = [dt, jnp.exp(cum) * keep, jnp.exp(last - cum) * tail]
        flows.append(jnp.broadcast_to(jnp.exp(last) * keep[CHUNK - 1 : CHUNK, :], (8, LANES)))
        wide = spread(jnp.concatenate(flows, axis=0), expand)
        dt_x, enter_x, end_x = (wide[k * CHUNK : (k + 1) * CHUNK, :] for k in range(3))
        carry = wide[3 * CHUNK : 3 * CHUNK + 1, :]
        v = dt_x * u
        v_low = v.astype(BF16)
        d_scores = jnp.zeros((CHUNK, CHUNK), F32)
        pieces, weighed = [], []
        for pair in range(heads // 2):
            lanes = slice(pair * LANES, (pair + 1) * LANES)
            dy_halves = jnp.concatenate(split_pair(dy_low[:, lanes]), axis=0)
            grads = dot_t(dy_halves, v_low[:, lanes])
            mats = []
            for k in range(2):
                decay = decay_matrix(cum, cum_t, visible, 2 * pair + k)
                grad = grads[k * CHUNK : (k + 1) * CHUNK, :]
                mat = scores * decay
                d_scores = d_scores + grad * decay
                weighed.append((grad * mat).astype(BF16))
                mats.append(mat.astype(BF16))
            pieces.append(tdot(jnp.concatenate(mats, axis=0), dy_halves))
        old_low = st_ref[piece]
        line.step(4 * block + 2 - piece)
        d_cum = dot(jnp.concatenate(weighed, axis=1), pick) - tdot(jnp.concatenate(weighed, axis=0), pick)
        ds = d_state[...]
        ds_low = ds.astype(BF16)
        dv_state = end_x * dot(b, ds_low)
        dv = jnp.concatenate(pieces, axis=1) + dv_state
        dy_enter = enter_x * dy
        dy_enter_low = dy_enter.astype(BF16)
        d_b = dot_t((end_x * v).astype(BF16), ds_low)
        d_c = dot_t(dy_enter_low, old_low)
        flow = jnp.broadcast_to(jnp.sum(ds * old_low.astype(F32) * carry, axis=0, keepdims=True), (8, inner))
        flow_low = flow.astype(BF16)
        products = [dy_enter * dot(c, old_low), dv_state * v, dv * u, flow, flow - flow_low.astype(F32)]
        sums = dot_t(jnp.concatenate(products, axis=0).astype(BF16), expand[0:LANES, :])
        e, f, d_dt = (sums[k * CHUNK : (k + 1) * CHUNK, :] for k in range(3))
        flow = sums[3 * CHUNK : 3 * CHUNK + 1, :] + sums[3 * CHUNK + 8 : 3 * CHUNK + 9, :]
        d_state[...] = carry * ds + tdot(c, dy_enter_low)
        d_scores_low = d_scores.astype(BF16)
        d_c = d_c + dot(d_scores_low, b)
        d_b = d_b + tdot(d_scores_low, c)
        d_la = dot(both_ways, jnp.concatenate([d_cum + e, f], axis=0), HIGHEST) + flow
        d_dt = d_la * decay_rate + d_dt
        d_pre = d_dt * sigmoid(pre)
        ddt_s[at, :] = d_pre.astype(BF16)
        a128[0:1, :] += jnp.sum(d_pre, axis=0, keepdims=True)
        a128[1:2, :] += jnp.sum(d_la * la, axis=0, keepdims=True)
        du = dt_x * dv + dsk * dy
        ahead[at, :] = du * (sp * (1.0 + p * (1.0 - sp)))
        d_bcu = jnp.concatenate([d_b, d_c], axis=1)
        ahead_bc[at, :] = d_bcu * (spbc * (1.0 + pbc * (1.0 - spbc)))

    for e in range(cube.events):

        @pl.when(block == min(e, blocks - 1))
        def _():
            cube.event(e)

    same = [(segs[k : k + rows, :] == seg_all).astype(F32) for k in range(1, 4)]
    for hist, weight, raw, out, acc in (
        (ahead, cx_ref, xc_ref, dx_s, a768),
        (ahead_bc, cbc_ref, bc_ref, dbc_s, a256),
    ):
        value = raw[...].astype(F32)
        dp = hist[0:rows, :]
        acc[4:5, :] += jnp.sum(dp, axis=0, keepdims=True)
        acc[3:4, :] += jnp.sum(dp * value, axis=0, keepdims=True)
        total = dp * weight[3:4, :]
        for k in range(1, 4):
            later = hist[k : k + rows, :] * same[k - 1]
            total = total + later * weight[3 - k : 4 - k, :]
            acc[3 - k : 4 - k, :] += jnp.sum(later * value, axis=0, keepdims=True)
        out[...] = total.astype(BF16)
        hist[rows : rows + 8, :] = hist[0:8, :]
    segs[rows : rows + 8, :] = segs[0:8, :]

    @pl.when(block == 0)
    def _():
        for load in loads:
            load.wait()

    partial = dot_t(dz_s[...], wz_ref[...]) + dot_t(dx_s[...], wx_ref[...])
    partial = partial + dot(ddt_s[...], wdt_s[...]) + dot_t(dbc_s[...], wbc_ref[...])
    for piece in range(PIECES):
        low = partial[piece * CHUNK : (piece + 1) * CHUNK, :].astype(BF16)
        for r in range(PER):
            for q in range(2):
                part_low = low[(2 * r + q) * ROWS : (2 * r + q + 1) * ROWS, :]
                xp_ref[piece * PER + r, q] = part_low
                part[(block + 1) * PIECES * PER - 1 - piece * PER - r, q] = part_low

    line.step(4 * block + 3)
    x = x_ref[...].astype(F32)
    xr = x * inverse_rms(x)
    a1536[0:1, :] += jnp.sum(partial * xr, axis=0, keepdims=True)
    xn = (xr * ng).astype(BF16)
    for w in range(0, width, 512):
        left = xn[:, w : w + 512]
        acc_z[w : w + 512, :] += tdot(left, dz_s[...])
        acc_x[w : w + 512, :] += tdot(left, dx_s[...])
        for j in range(acc_bc.shape[0]):
            acc_bc[j, w : w + 512, :] += tdot(left, dbc_s[:, j * LANES : (j + 1) * LANES])
        acc_dt[w : w + 512, :] += tdot(left, ddt_s[...])
    @pl.when(block == blocks - 1)
    def _():
        bits = [(acc_z, gz_ref, w) for w in range(0, width, 256)] + [(acc_x, gx_ref, w) for w in range(0, width, 256)]
        line.step(steps - 2)
        copies = []
        for j, (acc, out, w) in enumerate(bits):
            if j >= 2:
                copies[j - 2].wait()
            stage[j % 2] = acc[w : w + 256, :].astype(BF16)
            copies.append(pltpu.make_async_copy(stage.at[j % 2], out.at[pl.ds(w, 256), :], stage_sem.at[j % 2]))
            copies[j].start()
        line.step(steps - 1)
        copies[-2].wait()
        copies[-1].wait()
        for j in range(width // LANES):
            rest[16 * j : 16 * j + 16, :] = acc_dt[j * LANES : (j + 1) * LANES, :].T[0:16, :]
        base = dt_rows(width)
        for acc, out in ((a768, rest), (a128, rest), (a1536, shared), (a256, shared)):
            if acc is a1536:
                base = 0
            for j in range(acc.shape[1] // LANES):
                out[base : base + 8, :] = acc[:, j * LANES : (j + 1) * LANES]
                base += 8
        packed = [
            pltpu.make_async_copy(rest, pack_ref, stage_sem.at[2]),
            pltpu.make_async_copy(shared, shared_ref, stage_sem.at[3]),
        ]
        for j in range(acc_bc.shape[0]):
            there = gb_ref.at[:, pl.ds(j * LANES, LANES)]
            packed.append(pltpu.make_async_copy(acc_bc.at[j], there, stage_sem.at[4 + j]))
        for copy in packed:
            copy.start()
        for copy in packed:
            copy.wait()
        line.close(carry_out)


def dt_rows(width):
    return width // LANES * 16


def slot_rows(inner):
    return (inner // LANES + 1) * 8


def rows_spec(block, cols, last=None):
    if last is None:
        return pl.BlockSpec((block, cols), lambda i: (i, 0))
    return pl.BlockSpec((block, cols), lambda i: (last - i, 0))


def whole_spec(array):
    return pl.BlockSpec(array.shape, lambda i: (0,) * array.ndim, pipeline_mode=pl.Buffered(1))


def fixed_spec(*dims):
    return pl.BlockSpec(dims, lambda i: (0,) * len(dims))


def on_device(
    x_in, segments, out_grad, norm_gain, w_z, w_x, w_bc, w_dt, conv_x, conv_bc, bias_x, bias_bc,
    dt_bias, a_log, d_skip, out_gain, w_out,
):
    count = lax.axis_size("tensor")
    x, g = x_in[0], out_grad[0]
    length, width = x.shape
    inner = w_x.shape[1]
    heads = w_dt.shape[1]
    bcw = w_bc.shape[1]
    state_n = bcw // 2
    blocks = length // BLOCK
    chunks = length // CHUNK
    last = blocks - 1
    pairs = length // ROWS
    all_steps = pairs + LAG * (2 * count - 3)
    n_fwd = 2 * blocks + 6
    n_bwd = pairs // 2 + 2
    rest = all_steps - n_fwd - n_bwd
    wdt = w_dt.T
    per_head = (dt_bias[None, :], a_log[None, :], d_skip[None, :])
    x4 = x.reshape(pairs // 2, 2, ROWS, width)
    g4 = g.reshape(pairs // 2, 2, ROWS, width)
    shape = jax.ShapeDtypeStruct
    anywhere = pl.BlockSpec(memory_space=pl.ANY)
    pair_shape = (pairs // 2, 2, ROWS, width)
    carry_shape = shape((LAG, 2, ROWS, width), BF16)
    res_shape = shape(pair_shape, BF16)

    def params(ident):
        return pltpu.CompilerParams(
            vmem_limit_bytes=62 * 2**20, dimension_semantics=("arbitrary",), collective_id=ident, has_side_effects=True
        )

    def cost(flops, moved):
        return pl.CostEstimate(flops=flops, bytes_accessed=moved, transcendentals=0)

    weights = (w_z, w_x, w_bc, wdt, w_out, norm_gain, bias_x, out_gain, bias_bc, conv_x, conv_bc, *per_head)
    z, p, xc, ys, pbc, bc, dtr, dn, st, yp, scal, gout, carry, res_y, res_x = pl.pallas_call(
        functools.partial(forward_kernel, heads, count, pairs, n_fwd, blocks),
        grid=(blocks,),
        in_specs=[
            rows_spec(BLOCK, width),
            rows_spec(BLOCK, width),
            pl.BlockSpec((1, BLOCK), lambda i: (0, i)),
            *[anywhere if w is w_out or w is w_z else whole_spec(w) for w in weights],
        ],
        out_specs=[
            rows_spec(BLOCK, inner),
            rows_spec(BLOCK, inner),
            rows_spec(BLOCK, inner),
            rows_spec(BLOCK, inner),
            rows_spec(BLOCK, bcw),
            rows_spec(BLOCK, bcw),
            rows_spec(BLOCK, LANES),
            rows_spec(BLOCK, inner),
            pl.BlockSpec((PIECES, state_n, inner), lambda i: (i, 0, 0)),
            pl.BlockSpec((PIECES * PER, 2, ROWS, width), lambda i: (i, 0, 0, 0)),
            fixed_spec(chunks, 8, CHUNK),
            fixed_spec(2 * inner, width // 2),
            anywhere,
            anywhere,
            anywhere,
        ],
        out_shape=[
            shape((length, inner), F32),
            shape((length, inner), F32),
            shape((length, inner), BF16),
            shape((length, inner), F32),
            shape((length, bcw), F32),
            shape((length, bcw), F32),
            shape((length, LANES), F32),
            shape((length, inner), F32),
            shape((chunks, state_n, inner), BF16),
            shape(pair_shape, BF16),
            shape((chunks, 8, CHUNK), F32),
            shape((2 * inner, width // 2), BF16),
            carry_shape,
            res_shape,
            res_shape,
        ],
        scratch_shapes=[
            pltpu.VMEM(w_z.shape, BF16),
            pltpu.VMEM(w_out.shape, BF16),
            pltpu.SemaphoreType.DMA((2,)),
            pltpu.VMEM((8, LANES), F32),
            pltpu.VMEM((LANES, width), BF16),
            pltpu.VMEM((2 * LANES, inner), BF16),
            pltpu.VMEM((BLOCK + 8, inner), F32),
            pltpu.VMEM((BLOCK + 8, bcw), F32),
            pltpu.VMEM((BLOCK + 8, 1), F32),
            pltpu.VMEM((state_n, inner), F32),
            pltpu.VMEM((RING, BLOCK, inner), F32),
            pltpu.VMEM((RING, BLOCK, width), BF16),
            pltpu.VMEM((inner, width), F32),
            pltpu.VMEM((blocks, PIECES, 8, CHUNK), F32),
            pltpu.VMEM((count, blocks, PIECES, 8, CHUNK), F32),
            pltpu.SemaphoreType.DMA((count - 1, blocks)),
            pltpu.SemaphoreType.DMA((count - 1, blocks)),
            pltpu.VMEM(pair_shape, BF16),
            *line_scratch(n_fwd, width),
        ],
        compiler_params=params(0),
        cost_estimate=cost(9 * 10**10, 10**8),
        name="forward_scan",
    )(x, g, segments, *weights)

    weights = (w_z, w_x, w_bc, wdt, norm_gain, out_gain, conv_x, conv_bc, *per_head)
    n_in = 13 + len(weights)
    bits = lax.axis_size("dp").bit_length() - 1
    unit = 8 << bits
    pack_rows = -(-(dt_rows(width) + slot_rows(inner)) // unit) * unit
    shared_rows = -(-((width + bcw) // LANES * 8) // unit) * unit
    kind = F32 if (width // 2 >> bits) % 16 else BF16
    xp, gz, gx, gbc, pack, shared, carry, gout, res_y, res_x = pl.pallas_call(
        functools.partial(backward_kernel, heads, count, pairs, n_fwd, n_bwd),
        grid=(blocks,),
        in_specs=[
            rows_spec(BLOCK, inner, last),
            rows_spec(BLOCK, inner, last),
            rows_spec(BLOCK, inner, last),
            rows_spec(BLOCK, inner, last),
            rows_spec(BLOCK, bcw, last),
            rows_spec(BLOCK, bcw, last),
            rows_spec(BLOCK, LANES, last),
            rows_spec(BLOCK, inner, last),
            pl.BlockSpec((PIECES, state_n, inner), lambda i: (last - i, 0, 0)),
            pl.BlockSpec((1, BLOCK), lambda i: (0, jnp.maximum(last - i - 1, 0))),
            pl.BlockSpec((1, BLOCK), lambda i: (0, last - i)),
            pl.BlockSpec((PIECES, 8, CHUNK), lambda i: (last - i, 0, 0)),
            rows_spec(BLOCK, width, last),
            *[anywhere] * 3,
            *[whole_spec(w) for w in weights[3:]],
            *[anywhere] * 7,
        ],
        out_specs=[
            pl.BlockSpec((PIECES * PER, 2, ROWS, width), lambda i: (last - i, 0, 0, 0)),
            *[anywhere] * 9,
        ],
        out_shape=[
            shape(pair_shape, BF16),
            shape((width, inner), BF16),
            shape((width, inner), BF16),
            shape((width, bcw), F32),
            shape((pack_rows, LANES), F32),
            shape((shared_rows, LANES), F32),
            carry_shape,
            shape((2 * inner, width // 2), BF16),
            res_shape,
            res_shape,
        ],
        scratch_shapes=[
            *[pltpu.VMEM(w.shape, BF16) for w in weights[:3]],
            pltpu.SemaphoreType.DMA((3,)),
            pltpu.VMEM((8, LANES), F32),
            pltpu.VMEM((LANES, width), BF16),
            pltpu.VMEM((2 * LANES, inner), BF16),
            pltpu.VMEM((BLOCK + 8, inner), F32),
            pltpu.VMEM((BLOCK + 8, bcw), F32),
            pltpu.VMEM((BLOCK + 8, 1), F32),
            pltpu.VMEM((state_n, inner), F32),
            pltpu.VMEM((BLOCK, inner), BF16),
            pltpu.VMEM((BLOCK, inner), BF16),
            pltpu.VMEM((BLOCK, LANES), BF16),
            pltpu.VMEM((BLOCK, bcw), BF16),
            pltpu.VMEM((width, inner), F32),
            pltpu.VMEM((width, inner), F32),
            pltpu.VMEM((bcw // LANES, width, LANES), F32),
            pltpu.VMEM((width, LANES), F32),
            pltpu.VMEM((8, width), F32),
            pltpu.VMEM((8, inner), F32),
            pltpu.VMEM((8, bcw), F32),
            pltpu.VMEM((8, LANES), F32),
            pltpu.VMEM((pack_rows, LANES), F32),
            pltpu.VMEM((shared_rows, LANES), F32),
            pltpu.VMEM((2, 256, inner), BF16),
            pltpu.SemaphoreType.DMA((4 + bcw // LANES,)),
            pltpu.VMEM(pair_shape, BF16),
            pltpu.SemaphoreType.DMA,
            *finals_scratch(width),
            *cube_scratch(2 * inner, width // 2, bits, BF16),
            *line_scratch(n_bwd, width),
        ],
        input_output_aliases={n_in + 5: 8, n_in + 6: 9},
        compiler_params=params(1),
        cost_estimate=cost(12 * 10**10, 10**8),
        name="backward_scan",
    )(z, p, xc, ys, pbc, bc, dtr, dn, st, segments, segments, scal, x, *weights, yp, x4, g4, carry, gout, res_y, res_x)

    left = pairs - (n_fwd + n_bwd - LAG * (count - 1))
    res_y, res_x, gz, gx, gbc, pack, shared = pl.pallas_call(
        functools.partial(line_kernel, count, pairs, n_fwd + n_bwd, rest),
        grid=(rest,),
        in_specs=[anywhere] * 3 + [whole_spec(norm_gain)] + [anywhere] * 8,
        out_specs=[anywhere] * 7,
        out_shape=[
            res_shape,
            res_shape,
            shape((width, inner), BF16),
            shape((width, inner), BF16),
            shape((width, bcw), kind),
            shape((pack_rows, LANES), F32),
            shape((shared_rows, LANES), F32),
        ],
        scratch_shapes=[
            pltpu.VMEM((left, 2, ROWS, width), BF16),
            pltpu.SemaphoreType.DMA,
            *finals_scratch(width),
            *cube_scratch(width, inner, bits, BF16),
            *cube_scratch(width, inner, bits, BF16),
            *cube_scratch(pack_rows, LANES, bits, F32),
            *cube_scratch(shared_rows, LANES, bits, F32),
            *cross_scratch(count, shared_rows >> bits, LANES, F32),
            *cube_scratch(width // 2, bcw, bits, F32),
            *cross_scratch(count, width // 2 >> bits, bcw, kind),
            *cube_scratch(width // 2, bcw, bits, F32),
            *cross_scratch(count, width // 2 >> bits, bcw, kind),
            *line_scratch(rest, width),
        ],
        input_output_aliases={10: 0, 11: 1},
        compiler_params=params(2),
        cost_estimate=cost(10**11, 3 * 10**8),
        name="line_sums",
    )(xp, x4, g4, norm_gain, carry, gz, gx, gbc, pack, shared, res_y, res_x)

    wide = width // blocks
    tall = inner // blocks
    outs = pl.pallas_call(
        functools.partial(finish_kernel, heads),
        grid=(blocks,),
        in_specs=[
            rows_spec(BLOCK, width),
            rows_spec(BLOCK, width),
            rows_spec(BLOCK, width),
            pl.BlockSpec((PIECES, 8, CHUNK), lambda i: (i, 0, 0)),
            rows_spec(wide, inner),
            rows_spec(wide, inner),
            rows_spec(tall, width // 2),
            pl.BlockSpec((tall, width // 2), lambda i: (i + blocks, 0)),
            rows_spec(wide, bcw),
            whole_spec(pack),
            whole_spec(shared),
        ],
        out_specs=[
            rows_spec(BLOCK, width),
            rows_spec(BLOCK, width),
            rows_spec(wide, inner),
            rows_spec(wide, inner),
            rows_spec(tall, width),
            rows_spec(wide, bcw),
            fixed_spec(heads, width),
            fixed_spec(width),
            fixed_spec(4, inner),
            fixed_spec(inner),
            fixed_spec(inner),
            fixed_spec(1, heads),
            fixed_spec(4, bcw),
            fixed_spec(bcw),
            fixed_spec(1, heads),
            fixed_spec(1, heads),
        ],
        out_shape=[
            shape((length, width), BF16),
            shape((length, width), BF16),
            shape((width, inner), F32),
            shape((width, inner), F32),
            shape((inner, width), F32),
            shape((width, bcw), F32),
            shape((heads, width), F32),
            shape((width,), F32),
            shape((4, inner), F32),
            shape((inner,), F32),
            shape((inner,), F32),
            shape((1, heads), F32),
            shape((4, bcw), F32),
            shape((bcw,), F32),
            shape((1, heads), F32),
            shape((1, heads), F32),
        ],
        compiler_params=pltpu.CompilerParams(vmem_limit_bytes=60 * 2**20, dimension_semantics=("arbitrary",)),
        name="finish",
    )(x, res_y.reshape(length, width), res_x.reshape(length, width), scal, gz, gx, gout, gout, gbc, pack, shared)
    result, grad_x, gz, gx, gout, grad_wbc, grad_wdt, ng, cx, bx, og, ds, cbc, bbc, dtb, al = outs
    return (
        result[None], grad_x[None], ng, gz, gx, grad_wbc, grad_wdt.T, cx, cbc, bx, bbc, dtb[0], al[0], ds[0],
        og, gout,
    )


def solution(mesh):
    tensor_last = P(None, "tensor")
    in_specs = (
        P("dp", None, None), P("dp", None), P("dp", None, None), P(), tensor_last, tensor_last, P(), tensor_last,
        tensor_last, P(), P("tensor"), P(), P("tensor"), P("tensor"), P("tensor"), P("tensor"), P("tensor", None),
    )
    out_specs = (
        P("dp", None, None), P("dp", None, None), P(), tensor_last, tensor_last, P(), tensor_last, tensor_last, P(),
        P("tensor"), P(), P("tensor"), P("tensor"), P("tensor"), P("tensor"), P("tensor", None),
    )
    return jax.shard_map(on_device, mesh=mesh, in_specs=in_specs, out_specs=out_specs, check_vma=False)
```

```python
import functools

import jax
import jax.numpy as jnp
from jax import lax
from jax.experimental import pallas as pl
from jax.experimental.pallas import tpu as pltpu
from jax.sharding import PartitionSpec as P

EPS = 1e-05
CHUNK = 128
BLOCK = 256
PIECES = BLOCK // CHUNK
LANES = 128
ROWS = CHUNK // 4
PER = CHUNK // (2 * ROWS)
LAG = 2
RING = 4
F32 = jnp.float32
BF16 = jnp.bfloat16
HIGHEST = lax.Precision.HIGHEST
MESH = pl.DeviceIdType.MESH


def dot(a, b, precision=None):
    return lax.dot_general(a, b, (((1,), (0,)), ((), ())), precision=precision, preferred_element_type=F32)


def dot_t(a, b):
    return lax.dot_general(a, b, (((1,), (1,)), ((), ())), preferred_element_type=F32)


def tdot(a, b):
    return lax.dot_general(a, b, (((0,), (0,)), ((), ())), preferred_element_type=F32)


def sigmoid(v):
    return 1.0 / (1.0 + jnp.exp(-v))


def softplus(v):
    e = jnp.exp(-jnp.abs(v))
    series = e * (1.0 - e * (0.5 - e * (1.0 / 3.0 - e * 0.25)))
    return jnp.maximum(v, 0.0) + jnp.where(e < 0.03, series, jnp.log(1.0 + e))


def iotas(rows, cols):
    return (
        lax.broadcasted_iota(jnp.int32, (rows, cols), 0),
        lax.broadcasted_iota(jnp.int32, (rows, cols), 1),
    )


def fill_expand(expand, heads):
    r, c = iotas(*expand.shape)
    expand[...] = (lax.rem(r, LANES) == c // (expand.shape[1] // heads)).astype(BF16)


def spread(columns, expand):
    high = columns.astype(BF16)
    low = (columns - high.astype(F32)).astype(BF16)
    return dot(jnp.concatenate([high, low], axis=1), expand[...])


def decays(la, seg_col, seg_row):
    r, c = iotas(CHUNK, CHUNK)
    cum = dot((r >= c).astype(F32), la, HIGHEST)
    visible = (r >= c) & (seg_col == seg_row)
    return cum, cum.T, visible


def decay_matrix(cum, cum_t, visible, head):
    gap = cum[:, head : head + 1] - cum_t[head : head + 1, :]
    return jnp.exp(jnp.where(visible, gap, -1e30))


def split_pair(values):
    low = lax.broadcasted_iota(jnp.int32, values.shape, 1) < LANES // 2
    zero = jnp.zeros_like(values)
    return jnp.where(low, values, zero), jnp.where(low, zero, values)


def conv_taps(hist, weight, same, rows):
    out = hist[8 : 8 + rows, :] * weight[3:4, :]
    for k in range(1, 4):
        out = out + hist[8 - k : 8 - k + rows, :] * same[k - 1] * weight[3 - k : 4 - k, :]
    return out


def columns_of(segr_ref):
    rows = segr_ref.shape[1]
    pieces = []
    for at in range(0, rows, LANES):
        row = segr_ref[:, at : at + LANES].astype(F32)
        pieces.append(jnp.broadcast_to(row, (LANES, LANES)).T[:, 0:1])
    return jnp.concatenate(pieces, axis=0)


def fill_heads(hv, wdt_s, dtb_ref, al_ref, dsk_ref, wdt_ref):
    heads = wdt_ref.shape[0]
    hv[...] = jnp.zeros_like(hv)
    for j, ref in enumerate((dtb_ref, al_ref, dsk_ref)):
        hv[j : j + 1, 0:heads] = ref[...]
    wdt_s[...] = jnp.zeros_like(wdt_s)
    wdt_s[0:heads, :] = wdt_ref[...]


def row_of(ref):
    return ref[...].reshape(1, ref.shape[0])


def inverse_rms(tokens):
    return lax.rsqrt(jnp.sum(tokens * tokens, axis=1, keepdims=True) * (1.0 / tokens.shape[1]) + EPS)


def bring(src, dst, sem):
    copy = pltpu.make_async_copy(src, dst, sem)
    copy.start()
    copy.wait()


def hello(peers, dp_peers=()):
    barrier = pltpu.get_barrier_semaphore()
    for peer in dp_peers:
        pl.semaphore_signal(barrier, inc=1, device_id={"dp": peer}, device_id_type=MESH)
    for peer, there in peers:

        @pl.when(there)
        def _():
            pl.semaphore_signal(barrier, inc=1, device_id={"tensor": peer}, device_id_type=MESH)


def heard(peers, dp_peers=()):
    total = jnp.int32(len(dp_peers))
    for _, there in peers:
        total = total + there.astype(jnp.int32)
    pl.semaphore_wait(pltpu.get_barrier_semaphore(), total)


def neighbours(count):
    me = lax.axis_index("tensor")
    return [(me - 1, me > 0), (me + 1, me < count - 1)]


class Line:
    def __init__(self, count, pairs, first, steps, refs, source, finals=None):
        self.count, self.pairs, self.first, self.steps = count, pairs, first, steps
        self.source, self.finals = source, finals
        (self.res_y, self.res_x, self.land, self.send) = refs[:4]
        (self.red_out, self.red_in, self.bc_out, self.bc_in, self.local) = refs[4:]

    def to_result(self, k, q, act):
        half = self.pairs // 2

        @pl.when(k < half)
        def _():
            act(self.res_y.at[k, q])

        @pl.when(k >= half)
        def _():
            act(self.res_x.at[2 * half - 1 - k, q])

    def flow(self, q):
        me = lax.axis_index("tensor")
        if q == 0:
            return me, me - 1, me + 1
        return self.count - 1 - me, me + 1, me - 1

    def is_pair(self, i):
        return (i >= 0) & (i < self.pairs)

    def red(self, q, ls, toward, src):
        return pltpu.make_async_remote_copy(
            src_ref=src, dst_ref=self.land.at[ls + LAG, q], send_sem=self.red_out.at[q, ls],
            recv_sem=self.red_in.at[q, ls], device_id={"tensor": toward}, device_id_type=MESH,
        )

    def cast(self, q, ls, away, src, there):
        return pltpu.make_async_remote_copy(
            src_ref=src, dst_ref=there, send_sem=self.bc_out.at[q, ls],
            recv_sem=self.bc_in.at[q, ls], device_id={"tensor": away}, device_id_type=MESH,
        )

    def hold(self, q, ls):
        return self.send.at[lax.rem(ls, LAG), q]

    def keep(self, q, ls, there):
        return pltpu.make_async_copy(self.hold(q, ls), there, self.local.at[lax.rem(ls, LAG), q])

    def term(self, s, z):
        return s - LAG * (self.count - 1 - z)

    def back(self, s, z):
        return s - LAG * (self.count - 1 + z)

    def finish_red(self, q, s, ls):
        z, toward, away = self.flow(q)
        n = self.count
        i = self.term(s, z)

        @pl.when(self.is_pair(i) & (z > 0))
        def _():
            self.red(q, ls, toward, self.hold(q, ls)).wait_send()

        @pl.when(self.is_pair(i) & (z == 0))
        def _():
            self.cast(q, ls, away, self.hold(q, ls), self.res_y.at[0, q]).wait_send()
            self.keep(q, ls, self.res_y.at[0, q]).wait()

        @pl.when(self.is_pair(i + LAG) & (z < n - 1))
        def _():
            self.red(q, ls, toward, self.hold(q, ls)).wait_recv()

    def finish_cast(self, q, s, ls):
        z, _, away = self.flow(q)
        n = self.count
        k = self.back(s, z)

        @pl.when(self.is_pair(k) & (z > 0) & (z < n - 1))
        def _():
            self.cast(q, ls, away, self.res_y.at[0, q], self.res_y.at[0, q]).wait_send()

        @pl.when(self.is_pair(k + LAG) & (z > 0))
        def _():
            self.cast(q, ls, away, self.res_y.at[0, q], self.res_y.at[0, q]).wait_recv()

    def step(self, ls):
        n = self.count
        ls = jnp.int32(ls)
        s = self.first + ls
        for q in range(2):

            @pl.when(ls >= LAG)
            def _():
                self.finish_cast(q, s - LAG, ls - LAG)

            z, toward, away = self.flow(q)
            k = self.back(s, z)

            @pl.when(self.is_pair(k) & (z > 0) & (z < n - 1))
            def _():
                self.to_result(k, q, lambda there: self.cast(q, ls, away, there, there).start())

        for q in range(2):
            z, toward, away = self.flow(q)
            i = self.term(s, z)

            @pl.when(ls >= LAG)
            def _():
                self.finish_red(q, s - LAG, ls - LAG)

            @pl.when(self.is_pair(i))
            def _():
                mine = self.source(q, i)
                place = lax.rem(ls, LAG)

                @pl.when(z == n - 1)
                def _():
                    self.red(q, ls, toward, mine).start()

                @pl.when((z > 0) & (z < n - 1))
                def _():
                    self.send[place, q] = (mine[...].astype(F32) + self.land[ls, q].astype(F32)).astype(BF16)
                    self.red(q, ls, toward, self.hold(q, ls)).start()

                @pl.when(z == 0)
                def _():
                    total = mine[...].astype(F32) + self.land[ls, q].astype(F32)
                    if self.finals is None:
                        self.send[place, q] = total.astype(BF16)
                    else:
                        self.finals.last(q, i, total, self.hold(q, ls))

                    def give(there):
                        self.cast(q, ls, away, self.hold(q, ls), there).start()
                        self.keep(q, ls, there).start()

                    self.to_result(i, q, give)
                    if self.finals is not None:

                        @pl.when(ls + 1 < self.steps)
                        def _():
                            self.finals.fetch(q, i + 1)

    def held(self, q, s):
        z, _, _ = self.flow(q)
        return self.is_pair(self.term(s, z)) & (z < self.count - 1)

    def each_held(self, s, src, act):
        for q in range(2):
            for d in range(LAG):

                @pl.when(self.held(q, s + d))
                def _():
                    act(pltpu.make_async_copy(*src(d, q), self.local.at[d, q]))

    def open(self, carry):
        self.each_held(self.first, lambda d, q: (carry.at[d, q], self.land.at[d, q]), lambda copy: copy.start())
        for q in range(2):
            z, _, _ = self.flow(q)

            @pl.when(z == 0)
            def _():
                self.finals.fetch(q, jnp.int32(self.first - LAG * (self.count - 1)))

    def opened(self, carry):
        self.each_held(self.first, lambda d, q: (carry.at[d, q], self.land.at[d, q]), lambda copy: copy.wait())

    def close(self, carry):
        for d in range(LAG):
            ls = self.steps - LAG + d
            for q in range(2):
                self.finish_cast(q, self.first + ls, jnp.int32(ls))
                self.finish_red(q, self.first + ls, jnp.int32(ls))
        if carry is None:
            return
        left = (self.first + self.steps, lambda d, q: (self.land.at[self.steps + d, q], carry.at[d, q]))
        self.each_held(*left, lambda copy: copy.start())
        self.each_held(*left, lambda copy: copy.wait())


def line_scratch(steps, width):
    return [
        pltpu.VMEM((steps + LAG, 2, ROWS, width), BF16),
        pltpu.VMEM((LAG, 2, ROWS, width), BF16),
        pltpu.SemaphoreType.DMA((2, steps)),
        pltpu.SemaphoreType.DMA((2, steps)),
        pltpu.SemaphoreType.DMA((2, steps)),
        pltpu.SemaphoreType.DMA((2, steps)),
        pltpu.SemaphoreType.DMA((LAG, 2)),
    ]


class Finals:
    def __init__(self, pairs, x_any, g_any, gain, rows, sems):
        self.pairs, self.half, self.x_any, self.g_any, self.gain, self.rows, self.sems = (
            pairs, pairs // 2, x_any, g_any, gain, rows, sems,
        )

    def copies(self, q, i):
        b = 2 * self.half - 1 - i
        return [
            pltpu.make_async_copy(src.at[b, q], self.rows.at[q, j], self.sems.at[q, j])
            for j, src in enumerate((self.x_any, self.g_any))
        ]

    def fetch(self, q, i):
        @pl.when((i >= self.half) & (i < self.pairs))
        def _():
            for copy in self.copies(q, i):
                copy.start()

    def last(self, q, i, total, out):
        @pl.when(i < self.half)
        def _():
            out[...] = total.astype(BF16)

        @pl.when(i >= self.half)
        def _():
            for copy in self.copies(q, i):
                copy.wait()
            x = self.rows[q, 0].astype(F32)
            r1 = inverse_rms(x)
            scaled = total * self.gain
            across = jnp.sum(scaled * x, axis=1, keepdims=True) * (1.0 / x.shape[1])
            out[...] = (self.rows[q, 1].astype(F32) + r1 * scaled - x * (r1 * r1 * r1 * across)).astype(BF16)


def finals_scratch(width):
    return [pltpu.VMEM((2, 2, ROWS, width), BF16), pltpu.SemaphoreType.DMA((2, 2))]


def dp_bits():
    me = lax.axis_index("dp")
    bits = []
    for b in range(lax.axis_size("dp").bit_length() - 1):
        bit = lax.rem(me // 2**b, 2)
        bits.append((bit, me + (1 - 2 * bit) * 2**b))
    return bits


class Cube:
    def __init__(self, order, refs, across=None):
        self.order, self.across = order, across
        (self.src, self.out, self.total, self.send, self.land, self.out_sem, self.in_sem, self.local) = refs
        self.rows = self.src.shape[0]
        self.bits = dp_bits()
        self.turns = 0 if across is None else len(across[4])
        self.events = 2 * len(order) + 1 + self.turns

    def start_of(self, depth):
        at = 0
        for j in range(depth):
            at = at + self.bits[self.order[j]][0] * (self.rows >> (j + 1))
        return at

    def span(self, at, size):
        return pl.ds(pl.multiple_of(at, 8 if self.src.dtype == F32 else 16), size)

    def inside(self, depth):
        return self.start_of(depth) - self.start_of(1)

    def own_half(self):
        mine = self.src.at[self.span(self.start_of(1), self.rows // 2), :]
        return pltpu.make_async_copy(mine, self.send.at[pl.ds(0, self.rows // 2), :], self.local)

    def halving(self, j):
        size = self.rows >> (j + 1)
        bit, partner = self.bits[self.order[j]]
        theirs = self.start_of(j) + (1 - bit) * size
        src = self.src.at[self.span(theirs, size), :] if j == 0 else self.send.at[pl.ds(0, size), :]
        return pltpu.make_async_remote_copy(
            src_ref=src, dst_ref=self.land.at[pl.ds(self.rows - 2 * size, size), :], send_sem=self.out_sem.at[j],
            recv_sem=self.in_sem.at[j], device_id={"dp": partner}, device_id_type=MESH,
        )

    def doubling(self, j):
        count = len(self.order)
        size = self.rows >> (count - j)
        _, partner = self.bits[self.order[count - 1 - j]]
        mine = self.out.at[self.span(self.start_of(count - j), size), :]
        return pltpu.make_async_remote_copy(
            src_ref=mine, dst_ref=mine, send_sem=self.out_sem.at[count + j], recv_sem=self.in_sem.at[count + j],
            device_id={"dp": partner}, device_id_type=MESH,
        )

    def crossing(self, t):
        mine, land, out_sem, in_sem, partners = self.across
        return pltpu.make_async_remote_copy(
            src_ref=mine, dst_ref=land.at[t], send_sem=out_sem.at[t], recv_sem=in_sem.at[t],
            device_id={"tensor": partners[t]}, device_id_type=MESH,
        )

    def turn(self, part):
        count = len(self.order)
        size = self.rows >> count
        bring(part, self.out.at[self.span(self.start_of(count), size), :], self.local)
        self.doubling(0).start()

    def event(self, e):
        count = len(self.order)
        if e == 0:
            self.halving(0).start()
            self.own_half().start()
            return
        if e <= count:
            if e == 1:
                self.own_half().wait()
            self.halving(e - 1).wait()
            size = self.rows >> e
            at = self.inside(e)
            for r in range(0, size, 192):
                tile = min(192, size - r)
                landed = self.land[self.rows - 2 * size + r : self.rows - 2 * size + r + tile, :].astype(F32)
                here = self.span(at + r, tile)
                if e == 1:
                    self.total[here, :] = self.send[r : r + tile, :].astype(F32) + landed
                else:
                    self.total[here, :] = self.total[here, :] + landed
            if e < count:
                bit, _ = self.bits[self.order[e]]
                at = at + (1 - bit) * (size // 2)
                size = size // 2
            part = self.total[self.span(at, size), :]
            if e == count and self.across is not None:
                self.across[0][...] = part.astype(self.across[0].dtype)
                self.crossing(0).start()
                return
            self.send[0:size, :] = part.astype(self.send.dtype)
            if e < count:
                self.halving(e).start()
            else:
                self.turn(self.send.at[pl.ds(0, size), :])
            return
        if self.across is not None:
            t = e - count - 1
            if t < self.turns:
                mine, land = self.across[0], self.across[1]
                self.crossing(t).wait()
                mine[...] = (mine[...].astype(F32) + land[t].astype(F32)).astype(mine.dtype)
                if t + 1 < self.turns:
                    self.crossing(t + 1).start()
                else:
                    self.turn(mine)
                return
            e = e - self.turns
        self.doubling(e - count - 1).wait()
        if e < 2 * count:
            self.doubling(e - count).start()


def cube_scratch(rows, cols, bits, dtype):
    return [
        pltpu.VMEM((rows // 2, cols), F32),
        pltpu.VMEM((rows // 2, cols), dtype),
        pltpu.VMEM((rows - (rows >> bits), cols), dtype),
        pltpu.SemaphoreType.DMA((2 * bits,)),
        pltpu.SemaphoreType.DMA((2 * bits,)),
        pltpu.SemaphoreType.DMA,
    ]


def cross_scratch(count, rows, cols, dtype):
    turns = count.bit_length() - 1
    return [
        pltpu.VMEM((rows, cols), dtype),
        pltpu.VMEM((turns, rows, cols), dtype),
        pltpu.SemaphoreType.DMA((turns,)),
        pltpu.SemaphoreType.DMA((turns,)),
    ]


def tensor_partners(count):
    me = lax.axis_index("tensor")
    return [me + (1 - 2 * lax.rem(me // 2**b, 2)) * 2**b for b in range(count.bit_length() - 1)]


def tensor_peers(count):
    me = lax.axis_index("tensor")
    return [lax.rem(me + d, count) for d in range(1, count)]


def line_kernel(
    count, pairs, first, steps, xp_ref, x_any, g_any, ng_ref, carry_ref, gz_ref, gx_ref, gb_ref, pk_ref, sh_ref, res_y_in, res_x_in,
    res_y, res_x, oz_ref, ox_ref, ob_ref, op_ref, os_ref, part, part_sem, rows, sems, *scratch,
):
    del res_y_in, res_x_in
    half = pairs // 2
    order = list(range(len(dp_bits())))
    other = order[:1] + order[:0:-1]
    peers = tensor_peers(count)
    partners = tensor_partners(count)
    cubes = [
        Cube(order, (gz_ref, oz_ref, *scratch[0:6])),
        Cube(other, (gx_ref, ox_ref, *scratch[6:12])),
        Cube(order, (pk_ref, op_ref, *scratch[12:18])),
        Cube(order, (sh_ref, os_ref, *scratch[18:24]), (*scratch[24:28], partners)),
    ]
    tall = gb_ref.shape[0] // 2
    for j, way in enumerate((order, other)):
        rows_j = pl.ds(j * tall, tall)
        refs = scratch[28 + 10 * j : 38 + 10 * j]
        cubes.append(Cube(way, (gb_ref.at[rows_j, :], ob_ref.at[rows_j, :], *refs[0:6]), (*refs[6:10], partners)))

    finals = Finals(pairs, x_any, g_any, row_of(ng_ref), rows, sems)
    line = Line(
        count, pairs, first, steps, (res_y, res_x, *scratch[48:]), lambda q, i: part.at[2 * half - 1 - i, q], finals
    )
    at = pl.program_id(0)

    @pl.when(at == 0)
    def _():
        terms = pltpu.make_async_copy(xp_ref.at[pl.ds(0, part.shape[0])], part, part_sem)
        everyone = [(peer, peer >= 0) for peer in peers], [partner for _, partner in dp_bits()]
        hello(*everyone)
        terms.start()
        line.open(carry_ref)
        line.opened(carry_ref)
        terms.wait()
        heard(*everyone)

    if len(order) == 3:
        first_times, other_times = [0, 2, 6, 8, 10, 14, 16], [0, 3, 7, 9, 11, 15, 17]
        across_times = [0, 4, 8, 9, 10, 12, 15, 16, 17]
    else:
        first_times = other_times = across_times = range(2 * len(order) + 4)
    for cube in cubes:
        when = other_times if cube is cubes[1] else first_times
        if cube.across is not None:
            when = across_times
        for e in range(cube.events):

            @pl.when(at == min(when[e], steps - 1))
            def _():
                cube.event(e)

    line.step(at)

    @pl.when(at == steps - 1)
    def _():
        line.close(None)


def finish_kernel(
    heads, x_ref, y_ref, dx_ref, scal_ref, gz_ref, gx_ref, go_ref, go2_ref, gb_ref, pack_ref, shared_ref,
    yo_ref, xo_ref, oz_ref, ox_ref, oo_ref, wbc_ref, wdt_ref, ng_ref, cx_ref, bx_ref, og_ref, ds_ref, cbc_ref, bbc_ref,
    dtb_ref, al_ref,
):
    inner = cx_ref.shape[1]
    width, bcw = x_ref.shape[1], wbc_ref.shape[1]
    for piece in range(x_ref.shape[0] // CHUNK):
        span = slice(piece * CHUNK, (piece + 1) * CHUNK)
        r2 = jnp.concatenate([scal_ref[piece], jnp.zeros((CHUNK - 8, CHUNK), F32)], axis=0).T[:, 0:1]
        yo_ref[span, :] = (x_ref[span, :].astype(F32) + r2 * y_ref[span, :].astype(F32)).astype(BF16)
    xo_ref[...] = dx_ref[...]
    oz_ref[...] = gz_ref[...].astype(F32)
    ox_ref[...] = gx_ref[...].astype(F32)
    oo_ref[:, 0 : width // 2] = go_ref[...].astype(F32)
    oo_ref[:, width // 2 :] = go2_ref[...].astype(F32)
    wbc_ref[...] = gb_ref[...].astype(F32)

    @pl.when(pl.program_id(0) == 0)
    def _():
        for j in range(width // LANES):
            wdt_ref[:, j * LANES : (j + 1) * LANES] = pack_ref[16 * j : 16 * j + 16, :][0:heads, :]

        def put(ref, row):
            ref[...] = row.reshape(ref.shape)

        def side_by_side(ref, at, pieces, rows=8):
            return jnp.concatenate([ref[at + 8 * j : at + 8 * j + rows, :] for j in range(pieces)], axis=1)

        put(ng_ref, side_by_side(shared_ref, 0, width // LANES, 1))
        rows = side_by_side(shared_ref, width // LANES * 8, bcw // LANES)
        cbc_ref[...] = rows[0:4, :]
        put(bbc_ref, rows[4:5, :])
        rows = side_by_side(pack_ref, dt_rows(width), inner // LANES)
        cx_ref[...] = rows[0:4, :]
        put(bx_ref, rows[4:5, :])
        put(og_ref, rows[6:7, :])
        lane = lax.broadcasted_iota(jnp.int32, (1, heads), 1)
        skip = jnp.zeros((1, heads), F32)
        for h in range(heads):
            head = jnp.sum(rows[5:6, h * 64 : h * 64 + 64], axis=1, keepdims=True)
            skip = jnp.where(lane == h, head, skip)
        ds_ref[...] = skip
        at = dt_rows(width) + inner // LANES * 8
        rows = pack_ref[at : at + 8, :]
        dtb_ref[...] = rows[0:1, 0:heads]
        al_ref[...] = rows[1:2, 0:heads]


def forward_kernel(
    heads, count, pairs, steps, blocks,
    x_ref, g_ref, segr_ref, wz_any, wx_ref, wbc_ref, wdt_ref, wo_any, ng_ref, bx_ref, og_ref, bbc_ref, cx_ref, cbc_ref,
    dtb_ref, al_ref, dsk_ref,
    z_ref, p_ref, xc_ref, ys_ref, pbc_ref, bc_ref, dtr_ref, dn_ref, st_ref, yp_ref, scal_ref, wout_ref,
    carry_out, res_y, res_x,
    wz_ref, wo_ref, w_sem, hv_ref, wdt_s, expand, hist, hist_bc, segs, state, scaled_s, g_s, acc_out, stat_mine, stat_land, stat_out, stat_in, part, *scratch,
):
    rows, width = x_ref.shape
    inner = z_ref.shape[1]
    block = pl.program_id(0)
    me = lax.axis_index("tensor")
    ng, bx, og, bbc = row_of(ng_ref), row_of(bx_ref), row_of(og_ref), row_of(bbc_ref)

    line = Line(count, pairs, 0, steps, (res_y, res_x, *scratch), lambda q, i: part.at[i, q])

    load_z = pltpu.make_async_copy(wz_any, wz_ref, w_sem.at[0])
    load = pltpu.make_async_copy(wo_any, wo_ref, w_sem.at[1])
    everyone = [(peer, peer >= 0) for peer in tensor_peers(count)]

    @pl.when(block == 0)
    def _():
        hello(everyone)
        load_z.start()
        load.start()
        fill_heads(hv_ref, wdt_s, dtb_ref, al_ref, dsk_ref, wdt_ref)
        fill_expand(expand, heads)
        hist[0:8, :] = jnp.zeros((8, hist.shape[1]), F32)
        hist_bc[0:8, :] = jnp.zeros((8, hist_bc.shape[1]), F32)
        segs[0:8, :] = jnp.full((8, 1), -1.0, F32)
        state[...] = jnp.zeros_like(state)
        acc_out[...] = jnp.zeros_like(acc_out)

    x = x_ref[...].astype(F32)
    xn = (x * inverse_rms(x) * ng).astype(BF16)
    xc = dot(xn, wx_ref[...])
    bc = dot(xn, wbc_ref[...])
    dtr = dot_t(xn, wdt_s[...])
    xc_ref[...] = xc.astype(BF16)
    bc_ref[...] = bc
    dtr_ref[...] = dtr
    seg_all = columns_of(segr_ref)
    segs[8 : 8 + rows, :] = seg_all
    hist[8 : 8 + rows, :] = xc
    hist_bc[8 : 8 + rows, :] = bc
    same = [(segs[8 - k : 8 - k + rows, :] == seg_all).astype(F32) for k in range(1, 4)]
    p_ref[...] = conv_taps(hist, cx_ref, same, rows) + bx
    pbc_ref[...] = conv_taps(hist_bc, cbc_ref, same, rows) + bbc
    @pl.when(block == 0)
    def _():
        load_z.wait()

    z_ref[...] = dot(xn, wz_ref[...])
    g = g_ref[...]
    g_s[lax.rem(block, RING)] = g
    dt_all = softplus(dtr + hv_ref[0:1, :])
    la_all = -jnp.exp(hv_ref[1:2, :]) * dt_all
    dsk = spread(hv_ref[...], expand)[2:3, :]
    row_i, lane_i = iotas(CHUNK, LANES)
    squares = []
    for piece in range(PIECES):
        at = pl.ds(piece * CHUNK, CHUNK)
        span = slice(piece * CHUNK, (piece + 1) * CHUNK)
        seg_col = seg_all[span, :]
        keep = (seg_col == segs[7 + piece * CHUNK : 8 + piece * CHUNK, :]).astype(F32)
        tail = (seg_col == seg_col[CHUNK - 1 : CHUNK, :]).astype(F32)
        dt = dt_all[span, :]
        cum, cum_t, visible = decays(la_all[span, :], seg_col, segr_ref[:, span].astype(F32))
        p = p_ref[at, :]
        u = p * sigmoid(p)
        pbc = pbc_ref[at, :]
        bcu = (pbc * sigmoid(pbc)).astype(BF16)
        n = bcu.shape[1] // 2
        b, c = bcu[:, :n], bcu[:, n:]
        scores = dot_t(c, b)
        last = cum[CHUNK - 1 : CHUNK, :]
        flows = [dt, jnp.exp(cum) * keep, jnp.exp(last - cum) * tail]
        flows.append(jnp.broadcast_to(jnp.exp(last) * keep[CHUNK - 1 : CHUNK, :], (8, LANES)))
        wide = spread(jnp.concatenate(flows, axis=0), expand)
        dt_x, enter_x, end_x = (wide[k * CHUNK : (k + 1) * CHUNK, :] for k in range(3))
        carry = wide[3 * CHUNK : 3 * CHUNK + 1, :]
        v = dt_x * u
        v_low = v.astype(BF16)
        pieces = []
        for pair in range(heads // 2):
            mats = [
                (scores * decay_matrix(cum, cum_t, visible, 2 * pair + k)).astype(BF16)
                for k in range(2)
            ]
            halves = split_pair(v_low[:, pair * LANES : (pair + 1) * LANES])
            pieces.append(dot(jnp.concatenate(mats, axis=1), jnp.concatenate(halves, axis=0)))
        if piece:

            @pl.when(block < 2)
            def _():
                line.step(4 * block + 1)

        inside = jnp.concatenate(pieces, axis=1)
        old = state[...]
        old_low = old.astype(BF16)
        st_ref[piece] = old_low
        entering = dot(c, old_low) * enter_x
        state[...] = old * carry + tdot(b, (end_x * v).astype(BF16))
        ys = inside + entering + dsk * u
        ys_ref[at, :] = ys
        z = z_ref[at, :]
        gated = ys * (z * sigmoid(z))
        scaled = gated * og
        scaled_s[lax.rem(block, RING), at, :] = scaled
        if piece == 0:

            @pl.when(block == 0)
            def _():
                heard(everyone)
                load.wait()

        y_part = dot(scaled.astype(BF16), wo_ref[...]).astype(BF16)
        for r in range(PER):
            for q in range(2):
                low = y_part[(2 * r + q) * ROWS : (2 * r + q + 1) * ROWS, :]
                yp_ref[piece * PER + r, q] = low
                part[(block * PIECES + piece) * PER + r, q] = low

        later = jnp.where(block < 4, 3 * block + 2 + piece, 2 * block + 6 + piece)
        line.step(jnp.where(block < 2, 4 * block + 2 * piece, later))

        squares.append(jnp.sum(gated * gated, axis=1, keepdims=True))

    dn = dot_t(g, wo_ref[...])
    dn_ref[...] = dn
    for piece in range(PIECES):
        span = slice(piece * CHUNK, (piece + 1) * CHUNK)
        across = jnp.sum(dn[span, :] * scaled_s[lax.rem(block, RING), span, :], axis=1, keepdims=True)
        both = jnp.where(lane_i == 0, squares[piece], jnp.where(lane_i == 1, across, 0.0))
        stat_mine[block, piece] = both.T[0:8, :]
    hist[0:8, :] = hist[rows : rows + 8, :]
    hist_bc[0:8, :] = hist_bc[rows : rows + 8, :]
    segs[0:8, :] = segs[rows : rows + 8, :]

    def stat_copy(d, b):
        return pltpu.make_async_remote_copy(
            src_ref=stat_mine.at[b], dst_ref=stat_land.at[d, b], send_sem=stat_out.at[d - 1, b],
            recv_sem=stat_in.at[d - 1, b], device_id={"tensor": lax.rem(me + d, count)}, device_id_type=MESH,
        )

    def settle(pair):
        low, up = [], []
        for b in (pair, pair + 1):
            for d in range(1, count):
                stat_copy(d, b).wait()
            stat_land[0, b] = stat_mine[b]
            total = stat_land[me, b]
            for rank in range(1, count):
                total = total + stat_land[lax.rem(me - rank + count, count), b]
            place = lax.rem(b, RING)
            for piece in range(PIECES):
                r2 = lax.rsqrt(total[piece, 0:1, :] * (1.0 / (inner * count)) + EPS)
                k2 = r2 * r2 * r2 * (total[piece, 1:2, :] * (1.0 / (inner * count)))
                both = jnp.where(row_i == 0, r2, jnp.where(row_i == 1, k2, 0.0))
                scal_ref[b * PIECES + piece] = both[0:8, :]
                low.append((scaled_s[place, piece * CHUNK : (piece + 1) * CHUNK, :] * both.T[:, 0:1]).astype(BF16))
            up.append(g_s[place])
        normed = jnp.concatenate(low, axis=0)
        up = jnp.concatenate(up, axis=0)
        for c in range(0, inner, 256):
            acc_out[c : c + 256, :] += tdot(normed[:, c : c + 256], up)

    for d in range(1, count):
        stat_copy(d, block).start()

    @pl.when(block < 4)
    def _():
        line.step(jnp.where(block < 2, 4 * block + 3, 3 * block + 4))

    @pl.when((block >= RING - 1) & (lax.rem(block, 2) == 1))
    def _():
        settle(block - (RING - 1))

    @pl.when(block == blocks - 1)
    def _():
        settle(blocks - 2)
        for c in range(0, inner, 256):
            low = acc_out[c : c + 256, :].astype(BF16)
            wout_ref[c : c + 256, :] = low[:, 0 : width // 2]
            wout_ref[inner + c : inner + c + 256, :] = low[:, width // 2 :]
        line.close(carry_out)


def backward_kernel(
    heads, count, pairs, first, steps,
    z_ref, p_ref, xc_ref, ys_ref, pbc_ref, bc_ref, dtr_ref, dn_ref, st_ref, segp_ref, segr_ref, scal_ref, x_ref,
    wz_any, wx_any, wbc_any, wdt_ref, ng_ref, og_ref, cx_ref, cbc_ref, dtb_ref, al_ref, dsk_ref, y_ref, x_any, g_any, carry_ref, go_ref, res_y_in, res_x_in,
    xp_ref, gz_ref, gx_ref, gb_ref, pack_ref, shared_ref, carry_out, go_sum, res_y, res_x,
    wz_ref, wx_ref, wbc_ref, w_sem, hv_ref, wdt_s, expand, ahead, ahead_bc, segs, d_state, dz_s, dx_s, ddt_s, dbc_s, acc_z, acc_x, acc_bc, acc_dt,
    a1536, a768, a256, a128, rest, shared, stage, stage_sem, part, part_sem, rows_s, rows_sem, *scratch,
):
    del res_y_in, res_x_in
    rows, inner = z_ref.shape
    width = x_ref.shape[1]
    block = pl.program_id(0)
    blocks = steps // (PIECES * PER)
    half = pairs // 2
    me = lax.axis_index("tensor")
    ng, og = row_of(ng_ref), row_of(og_ref)

    finals = Finals(pairs, x_any, g_any, ng, rows_s, rows_sem)
    line = Line(
        count, pairs, first, steps, (res_y, res_x, *scratch[6:]), lambda q, i: part.at[lax.rem(i, half), q], finals
    )
    loads = [
        pltpu.make_async_copy(src, dst, w_sem.at[j])
        for j, (src, dst) in enumerate(((wz_any, wz_ref), (wx_any, wx_ref), (wbc_any, wbc_ref)))
    ]
    cube = Cube(list(range(len(dp_bits()))), (go_ref, go_sum, *scratch[0:6]))
    old = first - LAG * (count - 1)

    @pl.when(block == 0)
    def _():
        terms = pltpu.make_async_copy(y_ref.at[pl.ds(old, half - old)], part.at[pl.ds(old, half - old)], part_sem)
        everyone = neighbours(count), [partner for _, partner in dp_bits()]
        hello(*everyone)
        terms.start()
        line.open(carry_ref)
        for load in loads:
            load.start()
        line.opened(carry_ref)
        terms.wait()
        heard(*everyone)
        line.step(0)
        fill_heads(hv_ref, wdt_s, dtb_ref, al_ref, dsk_ref, wdt_ref)
        fill_expand(expand, heads)
        ahead[rows : rows + 8, :] = jnp.zeros((8, ahead.shape[1]), F32)
        ahead_bc[rows : rows + 8, :] = jnp.zeros((8, ahead_bc.shape[1]), F32)
        segs[rows : rows + 8, :] = jnp.full((8, 1), -1.0, F32)
        for ref in (d_state, acc_z, acc_x, acc_bc, acc_dt, a1536, a768, a256, a128, rest, shared):
            ref[...] = jnp.zeros_like(ref)

    @pl.when(block > 0)
    def _():
        line.step(4 * block)

    seg_all = columns_of(segr_ref)
    segs[0:rows, :] = seg_all
    before = jnp.where(block == blocks - 1, -1.0, segp_ref[:, rows - 1 : rows].astype(F32))
    r, c_ = iotas(CHUNK, CHUNK)
    both_ways = jnp.concatenate([(r <= c_).astype(F32), (r > c_).astype(F32)], axis=1)
    all_r, all_l = iotas(heads * CHUNK, LANES)
    pick = (all_r // CHUNK == all_l).astype(BF16)
    decay_rate = -jnp.exp(hv_ref[1:2, :])
    dsk = spread(hv_ref[...], expand)[2:3, :]
    for piece in reversed(range(PIECES)):
        at = pl.ds(piece * CHUNK, CHUNK)
        span = slice(piece * CHUNK, (piece + 1) * CHUNK)
        seg_col = seg_all[span, :]
        prev = seg_all[piece * CHUNK - 1 : piece * CHUNK, :] if piece else before
        keep = (seg_col == prev).astype(F32)
        tail = (seg_col == seg_col[CHUNK - 1 : CHUNK, :]).astype(F32)
        scal = jnp.concatenate([scal_ref[piece], jnp.zeros((CHUNK - 8, CHUNK), F32)], axis=0).T
        r2 = scal[:, 0:1]
        k2 = scal[:, 1:2]
        pre = dtr_ref[at, :] + hv_ref[0:1, :]
        dt = softplus(pre)
        la = decay_rate * dt
        cum, cum_t, visible = decays(la, seg_col, segr_ref[:, span].astype(F32))
        z = z_ref[at, :]
        ys = ys_ref[at, :]
        sz = sigmoid(z)
        silu = z * sz
        gated = ys * silu
        dn = dn_ref[at, :]
        d_gated = r2 * og * dn - gated * k2
        a768[6:7, :] += jnp.sum(dn * gated * r2, axis=0, keepdims=True)
        dz_s[at, :] = (d_gated * ys * (sz * (1.0 + z * (1.0 - sz)))).astype(BF16)
        dy = d_gated * silu
        dy_low = dy.astype(BF16)
        p = p_ref[at, :]
        sp = sigmoid(p)
        u = p * sp
        a768[5:6, :] += jnp.sum(dy * u, axis=0, keepdims=True)
        pbc = pbc_ref[at, :]
        spbc = sigmoid(pbc)
        bcu = (pbc * spbc).astype(BF16)
        n = bcu.shape[1] // 2
        b, c = bcu[:, :n], bcu[:, n:]
        scores = dot_t(c, b)
        last = cum[CHUNK - 1 : CHUNK, :]
        flows = [dt, jnp.exp(cum) * keep, jnp.exp(last - cum) * tail]
        flows.append(jnp.broadcast_to(jnp.exp(last) * keep[CHUNK - 1 : CHUNK, :], (8, LANES)))
        wide = spread(jnp.concatenate(flows, axis=0), expand)
        dt_x, enter_x, end_x = (wide[k * CHUNK : (k + 1) * CHUNK, :] for k in range(3))
        carry = wide[3 * CHUNK : 3 * CHUNK + 1, :]
        v = dt_x * u
        v_low = v.astype(BF16)
        d_scores = jnp.zeros((CHUNK, CHUNK), F32)
        pieces, weighed = [], []
        for pair in range(heads // 2):
            lanes = slice(pair * LANES, (pair + 1) * LANES)
            dy_halves = jnp.concatenate(split_pair(dy_low[:, lanes]), axis=0)
            grads = dot_t(dy_halves, v_low[:, lanes])
            mats = []
            for k in range(2):
                decay = decay_matrix(cum, cum_t, visible, 2 * pair + k)
                grad = grads[k * CHUNK : (k + 1) * CHUNK, :]
                mat = scores * decay
                d_scores = d_scores + grad * decay
                weighed.append((grad * mat).astype(BF16))
                mats.append(mat.astype(BF16))
            pieces.append(tdot(jnp.concatenate(mats, axis=0), dy_halves))
        old_low = st_ref[piece]
        line.step(4 * block + 2 - piece)
        d_cum = dot(jnp.concatenate(weighed, axis=1), pick) - tdot(jnp.concatenate(weighed, axis=0), pick)
        ds = d_state[...]
        ds_low = ds.astype(BF16)
        dv_state = end_x * dot(b, ds_low)
        dv = jnp.concatenate(pieces, axis=1) + dv_state
        dy_enter = enter_x * dy
        dy_enter_low = dy_enter.astype(BF16)
        d_b = dot_t((end_x * v).astype(BF16), ds_low)
        d_c = dot_t(dy_enter_low, old_low)
        flow = jnp.broadcast_to(jnp.sum(ds * old_low.astype(F32) * carry, axis=0, keepdims=True), (8, inner))
        flow_low = flow.astype(BF16)
        products = [dy_enter * dot(c, old_low), dv_state * v, dv * u, flow, flow - flow_low.astype(F32)]
        sums = dot_t(jnp.concatenate(products, axis=0).astype(BF16), expand[0:LANES, :])
        e, f, d_dt = (sums[k * CHUNK : (k + 1) * CHUNK, :] for k in range(3))
        flow = sums[3 * CHUNK : 3 * CHUNK + 1, :] + sums[3 * CHUNK + 8 : 3 * CHUNK + 9, :]
        d_state[...] = carry * ds + tdot(c, dy_enter_low)
        d_scores_low = d_scores.astype(BF16)
        d_c = d_c + dot(d_scores_low, b)
        d_b = d_b + tdot(d_scores_low, c)
        d_la = dot(both_ways, jnp.concatenate([d_cum + e, f], axis=0), HIGHEST) + flow
        d_dt = d_la * decay_rate + d_dt
        d_pre = d_dt * sigmoid(pre)
        ddt_s[at, :] = d_pre.astype(BF16)
        a128[0:1, :] += jnp.sum(d_pre, axis=0, keepdims=True)
        a128[1:2, :] += jnp.sum(d_la * la, axis=0, keepdims=True)
        du = dt_x * dv + dsk * dy
        ahead[at, :] = du * (sp * (1.0 + p * (1.0 - sp)))
        d_bcu = jnp.concatenate([d_b, d_c], axis=1)
        ahead_bc[at, :] = d_bcu * (spbc * (1.0 + pbc * (1.0 - spbc)))

    for e in range(cube.events):

        @pl.when(block == min(e, blocks - 1))
        def _():
            cube.event(e)

    same = [(segs[k : k + rows, :] == seg_all).astype(F32) for k in range(1, 4)]
    for hist, weight, raw, out, acc in (
        (ahead, cx_ref, xc_ref, dx_s, a768),
        (ahead_bc, cbc_ref, bc_ref, dbc_s, a256),
    ):
        value = raw[...].astype(F32)
        dp = hist[0:rows, :]
        acc[4:5, :] += jnp.sum(dp, axis=0, keepdims=True)
        acc[3:4, :] += jnp.sum(dp * value, axis=0, keepdims=True)
        total = dp * weight[3:4, :]
        for k in range(1, 4):
            later = hist[k : k + rows, :] * same[k - 1]
            total = total + later * weight[3 - k : 4 - k, :]
            acc[3 - k : 4 - k, :] += jnp.sum(later * value, axis=0, keepdims=True)
        out[...] = total.astype(BF16)
        hist[rows : rows + 8, :] = hist[0:8, :]
    segs[rows : rows + 8, :] = segs[0:8, :]

    @pl.when(block == 0)
    def _():
        for load in loads:
            load.wait()

    partial = dot_t(dz_s[...], wz_ref[...]) + dot_t(dx_s[...], wx_ref[...])
    partial = partial + dot(ddt_s[...], wdt_s[...]) + dot_t(dbc_s[...], wbc_ref[...])
    for piece in range(PIECES):
        low = partial[piece * CHUNK : (piece + 1) * CHUNK, :].astype(BF16)
        for r in range(PER):
            for q in range(2):
                part_low = low[(2 * r + q) * ROWS : (2 * r + q + 1) * ROWS, :]
                xp_ref[piece * PER + r, q] = part_low
                part[(block + 1) * PIECES * PER - 1 - piece * PER - r, q] = part_low

    line.step(4 * block + 3)
    x = x_ref[...].astype(F32)
    xr = x * inverse_rms(x)
    a1536[0:1, :] += jnp.sum(partial * xr, axis=0, keepdims=True)
    xn = (xr * ng).astype(BF16)
    for w in range(0, width, 512):
        left = xn[:, w : w + 512]
        acc_z[w : w + 512, :] += tdot(left, dz_s[...])
        acc_x[w : w + 512, :] += tdot(left, dx_s[...])
        for j in range(acc_bc.shape[0]):
            acc_bc[j, w : w + 512, :] += tdot(left, dbc_s[:, j * LANES : (j + 1) * LANES])
        acc_dt[w : w + 512, :] += tdot(left, ddt_s[...])
    @pl.when(block == blocks - 1)
    def _():
        bits = [(acc_z, gz_ref, w) for w in range(0, width, 256)] + [(acc_x, gx_ref, w) for w in range(0, width, 256)]
        line.step(steps - 2)
        copies = []
        for j, (acc, out, w) in enumerate(bits):
            if j >= 2:
                copies[j - 2].wait()
            stage[j % 2] = acc[w : w + 256, :].astype(BF16)
            copies.append(pltpu.make_async_copy(stage.at[j % 2], out.at[pl.ds(w, 256), :], stage_sem.at[j % 2]))
            copies[j].start()
        line.step(steps - 1)
        copies[-2].wait()
        copies[-1].wait()
        for j in range(width // LANES):
            rest[16 * j : 16 * j + 16, :] = acc_dt[j * LANES : (j + 1) * LANES, :].T[0:16, :]
        base = dt_rows(width)
        for acc, out in ((a768, rest), (a128, rest), (a1536, shared), (a256, shared)):
            if acc is a1536:
                base = 0
            for j in range(acc.shape[1] // LANES):
                out[base : base + 8, :] = acc[:, j * LANES : (j + 1) * LANES]
                base += 8
        packed = [
            pltpu.make_async_copy(rest, pack_ref, stage_sem.at[2]),
            pltpu.make_async_copy(shared, shared_ref, stage_sem.at[3]),
        ]
        for j in range(acc_bc.shape[0]):
            there = gb_ref.at[:, pl.ds(j * LANES, LANES)]
            packed.append(pltpu.make_async_copy(acc_bc.at[j], there, stage_sem.at[4 + j]))
        for copy in packed:
            copy.start()
        for copy in packed:
            copy.wait()
        line.close(carry_out)


def dt_rows(width):
    return width // LANES * 16


def slot_rows(inner):
    return (inner // LANES + 1) * 8


def rows_spec(block, cols, last=None):
    if last is None:
        return pl.BlockSpec((block, cols), lambda i: (i, 0))
    return pl.BlockSpec((block, cols), lambda i: (last - i, 0))


def whole_spec(array):
    return pl.BlockSpec(array.shape, lambda i: (0,) * array.ndim, pipeline_mode=pl.Buffered(1))


def fixed_spec(*dims):
    return pl.BlockSpec(dims, lambda i: (0,) * len(dims))


def on_device(
    x_in, segments, out_grad, norm_gain, w_z, w_x, w_bc, w_dt, conv_x, conv_bc, bias_x, bias_bc,
    dt_bias, a_log, d_skip, out_gain, w_out,
):
    count = lax.axis_size("tensor")
    x, g = x_in[0], out_grad[0]
    length, width = x.shape
    inner = w_x.shape[1]
    heads = w_dt.shape[1]
    bcw = w_bc.shape[1]
    state_n = bcw // 2
    blocks = length // BLOCK
    chunks = length // CHUNK
    last = blocks - 1
    pairs = length // ROWS
    all_steps = pairs + LAG * (2 * count - 3)
    n_fwd = 2 * blocks + 6
    n_bwd = pairs // 2 + 2
    rest = all_steps - n_fwd - n_bwd
    wdt = w_dt.T
    per_head = (dt_bias[None, :], a_log[None, :], d_skip[None, :])
    x4 = x.reshape(pairs // 2, 2, ROWS, width)
    g4 = g.reshape(pairs // 2, 2, ROWS, width)
    shape = jax.ShapeDtypeStruct
    anywhere = pl.BlockSpec(memory_space=pl.ANY)
    pair_shape = (pairs // 2, 2, ROWS, width)
    carry_shape = shape((LAG, 2, ROWS, width), BF16)
    res_shape = shape(pair_shape, BF16)

    def params(ident):
        return pltpu.CompilerParams(
            vmem_limit_bytes=62 * 2**20, dimension_semantics=("arbitrary",), collective_id=ident, has_side_effects=True
        )

    def cost(flops, moved):
        return pl.CostEstimate(flops=flops, bytes_accessed=moved, transcendentals=0)

    weights = (w_z, w_x, w_bc, wdt, w_out, norm_gain, bias_x, out_gain, bias_bc, conv_x, conv_bc, *per_head)
    z, p, xc, ys, pbc, bc, dtr, dn, st, yp, scal, gout, carry, res_y, res_x = pl.pallas_call(
        functools.partial(forward_kernel, heads, count, pairs, n_fwd, blocks),
        grid=(blocks,),
        in_specs=[
            rows_spec(BLOCK, width),
            rows_spec(BLOCK, width),
            pl.BlockSpec((1, BLOCK), lambda i: (0, i)),
            *[anywhere if w is w_out or w is w_z else whole_spec(w) for w in weights],
        ],
        out_specs=[
            rows_spec(BLOCK, inner),
            rows_spec(BLOCK, inner),
            rows_spec(BLOCK, inner),
            rows_spec(BLOCK, inner),
            rows_spec(BLOCK, bcw),
            rows_spec(BLOCK, bcw),
            rows_spec(BLOCK, LANES),
            rows_spec(BLOCK, inner),
            pl.BlockSpec((PIECES, state_n, inner), lambda i: (i, 0, 0)),
            pl.BlockSpec((PIECES * PER, 2, ROWS, width), lambda i: (i, 0, 0, 0)),
            fixed_spec(chunks, 8, CHUNK),
            fixed_spec(2 * inner, width // 2),
            anywhere,
            anywhere,
            anywhere,
        ],
        out_shape=[
            shape((length, inner), F32),
            shape((length, inner), F32),
            shape((length, inner), BF16),
            shape((length, inner), F32),
            shape((length, bcw), F32),
            shape((length, bcw), F32),
            shape((length, LANES), F32),
            shape((length, inner), F32),
            shape((chunks, state_n, inner), BF16),
            shape(pair_shape, BF16),
            shape((chunks, 8, CHUNK), F32),
            shape((2 * inner, width // 2), BF16),
            carry_shape,
            res_shape,
            res_shape,
        ],
        scratch_shapes=[
            pltpu.VMEM(w_z.shape, BF16),
            pltpu.VMEM(w_out.shape, BF16),
            pltpu.SemaphoreType.DMA((2,)),
            pltpu.VMEM((8, LANES), F32),
            pltpu.VMEM((LANES, width), BF16),
            pltpu.VMEM((2 * LANES, inner), BF16),
            pltpu.VMEM((BLOCK + 8, inner), F32),
            pltpu.VMEM((BLOCK + 8, bcw), F32),
            pltpu.VMEM((BLOCK + 8, 1), F32),
            pltpu.VMEM((state_n, inner), F32),
            pltpu.VMEM((RING, BLOCK, inner), F32),
            pltpu.VMEM((RING, BLOCK, width), BF16),
            pltpu.VMEM((inner, width), F32),
            pltpu.VMEM((blocks, PIECES, 8, CHUNK), F32),
            pltpu.VMEM((count, blocks, PIECES, 8, CHUNK), F32),
            pltpu.SemaphoreType.DMA((count - 1, blocks)),
            pltpu.SemaphoreType.DMA((count - 1, blocks)),
            pltpu.VMEM(pair_shape, BF16),
            *line_scratch(n_fwd, width),
        ],
        compiler_params=params(0),
        cost_estimate=cost(9 * 10**10, 10**8),
        name="forward_scan",
    )(x, g, segments, *weights)

    weights = (w_z, w_x, w_bc, wdt, norm_gain, out_gain, conv_x, conv_bc, *per_head)
    n_in = 13 + len(weights)
    bits = lax.axis_size("dp").bit_length() - 1
    unit = 8 << bits
    pack_rows = -(-(dt_rows(width) + slot_rows(inner)) // unit) * unit
    shared_rows = -(-((width + bcw) // LANES * 8) // unit) * unit
    kind = F32 if (width // 2 >> bits) % 16 else BF16
    xp, gz, gx, gbc, pack, shared, carry, gout, res_y, res_x = pl.pallas_call(
        functools.partial(backward_kernel, heads, count, pairs, n_fwd, n_bwd),
        grid=(blocks,),
        in_specs=[
            rows_spec(BLOCK, inner, last),
            rows_spec(BLOCK, inner, last),
            rows_spec(BLOCK, inner, last),
            rows_spec(BLOCK, inner, last),
            rows_spec(BLOCK, bcw, last),
            rows_spec(BLOCK, bcw, last),
            rows_spec(BLOCK, LANES, last),
            rows_spec(BLOCK, inner, last),
            pl.BlockSpec((PIECES, state_n, inner), lambda i: (last - i, 0, 0)),
            pl.BlockSpec((1, BLOCK), lambda i: (0, jnp.maximum(last - i - 1, 0))),
            pl.BlockSpec((1, BLOCK), lambda i: (0, last - i)),
            pl.BlockSpec((PIECES, 8, CHUNK), lambda i: (last - i, 0, 0)),
            rows_spec(BLOCK, width, last),
            *[anywhere] * 3,
            *[whole_spec(w) for w in weights[3:]],
            *[anywhere] * 7,
        ],
        out_specs=[
            pl.BlockSpec((PIECES * PER, 2, ROWS, width), lambda i: (last - i, 0, 0, 0)),
            *[anywhere] * 9,
        ],
        out_shape=[
            shape(pair_shape, BF16),
            shape((width, inner), BF16),
            shape((width, inner), BF16),
            shape((width, bcw), F32),
            shape((pack_rows, LANES), F32),
            shape((shared_rows, LANES), F32),
            carry_shape,
            shape((2 * inner, width // 2), BF16),
            res_shape,
            res_shape,
        ],
        scratch_shapes=[
            *[pltpu.VMEM(w.shape, BF16) for w in weights[:3]],
            pltpu.SemaphoreType.DMA((3,)),
            pltpu.VMEM((8, LANES), F32),
            pltpu.VMEM((LANES, width), BF16),
            pltpu.VMEM((2 * LANES, inner), BF16),
            pltpu.VMEM((BLOCK + 8, inner), F32),
            pltpu.VMEM((BLOCK + 8, bcw), F32),
            pltpu.VMEM((BLOCK + 8, 1), F32),
            pltpu.VMEM((state_n, inner), F32),
            pltpu.VMEM((BLOCK, inner), BF16),
            pltpu.VMEM((BLOCK, inner), BF16),
            pltpu.VMEM((BLOCK, LANES), BF16),
            pltpu.VMEM((BLOCK, bcw), BF16),
            pltpu.VMEM((width, inner), F32),
            pltpu.VMEM((width, inner), F32),
            pltpu.VMEM((bcw // LANES, width, LANES), F32),
            pltpu.VMEM((width, LANES), F32),
            pltpu.VMEM((8, width), F32),
            pltpu.VMEM((8, inner), F32),
            pltpu.VMEM((8, bcw), F32),
            pltpu.VMEM((8, LANES), F32),
            pltpu.VMEM((pack_rows, LANES), F32),
            pltpu.VMEM((shared_rows, LANES), F32),
            pltpu.VMEM((2, 256, inner), BF16),
            pltpu.SemaphoreType.DMA((4 + bcw // LANES,)),
            pltpu.VMEM(pair_shape, BF16),
            pltpu.SemaphoreType.DMA,
            *finals_scratch(width),
            *cube_scratch(2 * inner, width // 2, bits, BF16),
            *line_scratch(n_bwd, width),
        ],
        input_output_aliases={n_in + 5: 8, n_in + 6: 9},
        compiler_params=params(1),
        cost_estimate=cost(12 * 10**10, 10**8),
        name="backward_scan",
    )(z, p, xc, ys, pbc, bc, dtr, dn, st, segments, segments, scal, x, *weights, yp, x4, g4, carry, gout, res_y, res_x)

    left = pairs - (n_fwd + n_bwd - LAG * (count - 1))
    res_y, res_x, gz, gx, gbc, pack, shared = pl.pallas_call(
        functools.partial(line_kernel, count, pairs, n_fwd + n_bwd, rest),
        grid=(rest,),
        in_specs=[anywhere] * 3 + [whole_spec(norm_gain)] + [anywhere] * 8,
        out_specs=[anywhere] * 7,
        out_shape=[
            res_shape,
            res_shape,
            shape((width, inner), BF16),
            shape((width, inner), BF16),
            shape((width, bcw), kind),
            shape((pack_rows, LANES), F32),
            shape((shared_rows, LANES), F32),
        ],
        scratch_shapes=[
            pltpu.VMEM((left, 2, ROWS, width), BF16),
            pltpu.SemaphoreType.DMA,
            *finals_scratch(width),
            *cube_scratch(width, inner, bits, BF16),
            *cube_scratch(width, inner, bits, BF16),
            *cube_scratch(pack_rows, LANES, bits, F32),
            *cube_scratch(shared_rows, LANES, bits, F32),
            *cross_scratch(count, shared_rows >> bits, LANES, F32),
            *cube_scratch(width // 2, bcw, bits, F32),
            *cross_scratch(count, width // 2 >> bits, bcw, kind),
            *cube_scratch(width // 2, bcw, bits, F32),
            *cross_scratch(count, width // 2 >> bits, bcw, kind),
            *line_scratch(rest, width),
        ],
        input_output_aliases={10: 0, 11: 1},
        compiler_params=params(2),
        cost_estimate=cost(10**11, 3 * 10**8),
        name="line_sums",
    )(xp, x4, g4, norm_gain, carry, gz, gx, gbc, pack, shared, res_y, res_x)

    wide = width // blocks
    tall = inner // blocks
    outs = pl.pallas_call(
        functools.partial(finish_kernel, heads),
        grid=(blocks,),
        in_specs=[
            rows_spec(BLOCK, width),
            rows_spec(BLOCK, width),
            rows_spec(BLOCK, width),
            pl.BlockSpec((PIECES, 8, CHUNK), lambda i: (i, 0, 0)),
            rows_spec(wide, inner),
            rows_spec(wide, inner),
            rows_spec(tall, width // 2),
            pl.BlockSpec((tall, width // 2), lambda i: (i + blocks, 0)),
            rows_spec(wide, bcw),
            whole_spec(pack),
            whole_spec(shared),
        ],
        out_specs=[
            rows_spec(BLOCK, width),
            rows_spec(BLOCK, width),
            rows_spec(wide, inner),
            rows_spec(wide, inner),
            rows_spec(tall, width),
            rows_spec(wide, bcw),
            fixed_spec(heads, width),
            fixed_spec(width),
            fixed_spec(4, inner),
            fixed_spec(inner),
            fixed_spec(inner),
            fixed_spec(1, heads),
            fixed_spec(4, bcw),
            fixed_spec(bcw),
            fixed_spec(1, heads),
            fixed_spec(1, heads),
        ],
        out_shape=[
            shape((length, width), BF16),
            shape((length, width), BF16),
            shape((width, inner), F32),
            shape((width, inner), F32),
            shape((inner, width), F32),
            shape((width, bcw), F32),
            shape((heads, width), F32),
            shape((width,), F32),
            shape((4, inner), F32),
            shape((inner,), F32),
            shape((inner,), F32),
            shape((1, heads), F32),
            shape((4, bcw), F32),
            shape((bcw,), F32),
            shape((1, heads), F32),
            shape((1, heads), F32),
        ],
        compiler_params=pltpu.CompilerParams(vmem_limit_bytes=60 * 2**20, dimension_semantics=("arbitrary",)),
        name="finish",
    )(x, res_y.reshape(length, width), res_x.reshape(length, width), scal, gz, gx, gout, gout, gbc, pack, shared)
    result, grad_x, gz, gx, gout, grad_wbc, grad_wdt, ng, cx, bx, og, ds, cbc, bbc, dtb, al = outs
    return (
        result[None], grad_x[None], ng, gz, gx, grad_wbc, grad_wdt.T, cx, cbc, bx, bbc, dtb[0], al[0], ds[0],
        og, gout,
    )


def solution(mesh):
    tensor_last = P(None, "tensor")
    in_specs = (
        P("dp", None, None), P("dp", None), P("dp", None, None), P(), tensor_last, tensor_last, P(), tensor_last,
        tensor_last, P(), P("tensor"), P(), P("tensor"), P("tensor"), P("tensor"), P("tensor"), P("tensor", None),
    )
    out_specs = (
        P("dp", None, None), P("dp", None, None), P(), tensor_last, tensor_last, P(), tensor_last, tensor_last, P(),
        P("tensor"), P(), P("tensor"), P("tensor"), P("tensor"), P("tensor"), P("tensor", None),
    )
    return jax.shard_map(on_device, mesh=mesh, in_specs=in_specs, out_specs=out_specs, check_vma=False)
```
